32 devices in a mesh: seq: 8 (over z, x), fsdp: 4 (over y, core).
Axes of the slice: x: 2, y: 2, z: 4, core: 2. Of those that a mesh axis runs over, the one named last changes fastest.
Arguments:
- tokens: bfloat16 [8192, 1024], P(('seq', 'fsdp')), may hold values from -6 to 6
- attn_gain: bfloat16 [1024], P(('seq', 'fsdp')), may hold values from 0.25 to 1.75
- w_query: bfloat16 [1024, 1024], P(('seq', 'fsdp')), may hold values from -0.1875 to 0.1875
- w_key: bfloat16 [1024, 1024], P(('seq', 'fsdp')), may hold values from -0.1875 to 0.1875
- w_value: bfloat16 [1024, 1024], P(('seq', 'fsdp')), may hold values from -0.1875 to 0.1875
- conv_weight: bfloat16 [4, 3072], P(None, ('seq', 'fsdp')), may hold values from -3 to 3
- w_beta: bfloat16 [1024, 8], P(('seq', 'fsdp')), may hold values from -0.1875 to 0.1875
- w_gate_out: bfloat16 [1024, 1024], P(('seq', 'fsdp')), may hold values from -0.1875 to 0.1875
- onorm_gain: bfloat16 [128], P(('seq', 'fsdp')), may hold values from 0.25 to 1.75
- w_out: bfloat16 [1024, 1024], P(('seq', 'fsdp')), may hold values from -0.375 to 0.375
- mlp_gain: bfloat16 [1024], P(('seq', 'fsdp')), may hold values from 0.25 to 1.75
- w_mlp_gate: bfloat16 [1024, 2816], P(('seq', 'fsdp')), may hold values from -0.1875 to 0.1875
- w_mlp_up: bfloat16 [1024, 2816], P(('seq', 'fsdp')), may hold values from -0.1875 to 0.1875
- w_down: bfloat16 [2816, 1024], P(('seq', 'fsdp')), may hold values from -0.21875 to 0.21875
- seq_lengths: int32 [4], replicated, may hold values from 1024 to 4096, as said below
- cotangent: bfloat16 [8192, 1024], P(('seq', 'fsdp')), may hold values from -6 to 6
Outputs:
- output: bfloat16 [8192, 1024], P(('seq', 'fsdp'))
- grad_tokens: float32 [8192, 1024], P(('seq', 'fsdp'))
- grad_attn_gain: float32 [1024], P(('seq', 'fsdp'))
- grad_query: float32 [1024, 1024], P(('seq', 'fsdp'))
- grad_key: float32 [1024, 1024], P(('seq', 'fsdp'))
- grad_value: float32 [1024, 1024], P(('seq', 'fsdp'))
- grad_conv: float32 [4, 3072], P(None, ('seq', 'fsdp'))
- grad_beta: float32 [1024, 8], P(('seq', 'fsdp'))
- grad_gate_out: float32 [1024, 1024], P(('seq', 'fsdp'))
- grad_onorm: float32 [128], P(('seq', 'fsdp'))
- grad_out: float32 [1024, 1024], P(('seq', 'fsdp'))
- grad_mlp_gain: float32 [1024], P(('seq', 'fsdp'))
- grad_mlp_gate: float32 [1024, 2816], P(('seq', 'fsdp'))
- grad_mlp_up: float32 [1024, 2816], P(('seq', 'fsdp'))
- grad_down: float32 [2816, 1024], P(('seq', 'fsdp'))
The draws below stay inside these ranges and needn't reach their ends.
Inputs may be any that keep to these rules, and one draw needn't show every extreme that they name: `seq_lengths`: every length is a multiple of 64; the lengths sum to 8192; one sequence has exactly 4096 tokens and two have exactly 1024 tokens each.
All inputs are finite; a program needn't handle non-finite values.
Results may differ from the reference program's by a relative error of at most 0.013.
The reference program's roundings to bfloat16 on the way (of `normed`, `projected`, `branch`, `normed_two` and `inner_act`) count: a program that leaves them out, or rounds other values in their place, can miss the bound.
Values may be sent and summed in bfloat16 or wider, within the bound.
No kernel may reach another device: no remote copies, remote signals or barrier semaphores. Data moves between devices by JAX's collectives and lax.ppermute only.
A program may use at most 448 MiB of HBM per device.

```python
import jax
import jax.numpy as jnp
from jax import lax

D = 1024
H = 8
DK = 128
FF = 2816
CONV = 4
BLOCK = 64
SEQUENCES = 4
TOKENS = 8192
MEANLEN = 2048


def draw_seq_lengths(key, part):
    unit_count = MEANLEN // BLOCK
    half_units = unit_count // 2
    seq_count = SEQUENCES
    shifts = jax.random.randint(jax.random.fold_in(key, 11), (seq_count,), 0, half_units + 1)
    shuffled = jax.random.permutation(jax.random.fold_in(key, 12), seq_count)
    position = jnp.arange(seq_count, dtype=jnp.int32)
    offset = position - 3
    pair_index = jnp.maximum(offset, 0) // 2
    partner = (offset >= 0) & (2 * pair_index + 5 <= seq_count)
    direction = jnp.where(offset % 2 == 0, 1, -1)
    transfer = jnp.where(partner, direction * shifts[pair_index], 0)
    leading = jnp.where(position == 0, unit_count, jnp.where(position < 3, -half_units, 0))
    length_units = unit_count + leading + transfer
    return (length_units[shuffled] * BLOCK).astype(jnp.int32)


def levels(key, dims, pieces, smallest, high):
    level, own = 1.0, jax.random.fold_in(key, 6)
    for dim, parts in pieces:
        draws = jnp.exp(jax.random.uniform(jax.random.fold_in(own, dim), (parts,), jnp.float32, smallest / len(pieces), high / len(pieces)))
        level = level * jnp.repeat(draws, dims[dim] // parts).reshape([-1 if axis == dim else 1 for axis in range(len(dims))])
    return level


def noise(rng, extent, width, bound, shards=(), held_as=jnp.bfloat16):
    values = jax.random.normal(rng, extent, jnp.float32) * width
    if len(shards) > 0:
        values = levels(rng, extent, shards, -0.22, 0.18) * values
    return jnp.clip(values, min=-bound, max=bound).astype(held_as)


def setup_inputs(seed: int = 0) -> dict:
    key_list = jax.random.split(jax.random.key(seed), 17)
    tokens = noise(key_list[0], (TOKENS, D), 1.0, 6.0, ((0, 32),))
    attn_gain = jnp.clip(1.0 + 0.15 * jax.random.normal(key_list[1], (D,), jnp.float32), 0.25, 1.75).astype(jnp.bfloat16)
    w_query = noise(key_list[2], (D, D), D ** -0.5, 0.1875, ((0, 32),))
    w_key = noise(key_list[3], (D, D), D ** -0.5, 0.1875, ((0, 32),))
    w_value = noise(key_list[4], (D, D), D ** -0.5, 0.1875, ((0, 32),))
    conv_weight = noise(key_list[5], (CONV, 3 * D), 0.5, 3.0, ((1, 32),))
    w_beta = noise(key_list[6], (D, H), D ** -0.5, 0.1875, ((0, 32),))
    w_gate_out = noise(key_list[7], (D, D), D ** -0.5, 0.1875, ((0, 32),))
    onorm_gain = jnp.clip(1.0 + 0.15 * jax.random.normal(key_list[8], (DK,), jnp.float32), 0.25, 1.75).astype(jnp.bfloat16)
    w_out = noise(key_list[9], (D, D), (D // 4) ** -0.5, 0.375, ((0, 32),))
    mlp_gain = jnp.clip(1.0 + 0.15 * jax.random.normal(key_list[10], (D,), jnp.float32), 0.25, 1.75).astype(jnp.bfloat16)
    w_mlp_gate = noise(key_list[11], (D, FF), D ** -0.5, 0.1875, ((0, 32),))
    w_mlp_up = noise(key_list[12], (D, FF), D ** -0.5, 0.1875, ((0, 32),))
    w_down = noise(key_list[13], (FF, D), (FF // 4) ** -0.5, 0.21875, ((0, 32),))
    seq_lengths = draw_seq_lengths(jax.random.fold_in(key_list[16], 71), 0)
    cotangent = noise(key_list[15], (TOKENS, D), 1.0, 6.0, ((0, 32),))
    return {"tokens": tokens, "attn_gain": attn_gain, "w_query": w_query, "w_key": w_key, "w_value": w_value, "conv_weight": conv_weight, "w_beta": w_beta, "w_gate_out": w_gate_out, "onorm_gain": onorm_gain, "w_out": w_out, "mlp_gain": mlp_gain, "w_mlp_gate": w_mlp_gate, "w_mlp_up": w_mlp_up, "w_down": w_down, "seq_lengths": seq_lengths, "cotangent": cotangent}


@jax.custom_vjp
def low(v):
    return lax.optimization_barrier(v.astype(jnp.bfloat16)).astype(jnp.float32)

@jax.custom_vjp
def low_back(v):
    return v

def low_keep(v):
    return (low(v), None)

def low_pass(kept, grad):
    return (grad,)

def back_keep(v):
    return (v, None)

def back_low(kept, grad):
    return (low(grad),)
low.defvjp(low_keep, low_pass)
low_back.defvjp(back_keep, back_low)
highest = lax.Precision.HIGHEST

def matmul(left, right):
    return jnp.dot(left, right, precision=highest)

def rms_scale(values, gain):
    return values * lax.rsqrt(lax.optimization_barrier(jnp.mean(values * values, axis=-1, keepdims=True)) + 1e-05) * gain

def unit_rows(values):
    return values * lax.rsqrt(lax.optimization_barrier(jnp.sum(values * values, axis=-1, keepdims=True)) + 1e-06)

def seq_offsets(seq_lengths, positions):
    starts = (jnp.cumsum(seq_lengths) - seq_lengths).astype(jnp.int32)
    begins = lax.optimization_barrier(jnp.max(jnp.where(starts[None, :] <= positions[:, None], starts[None, :], 0), axis=1))
    return (positions - begins).astype(jnp.int32)

def delta_rule(queries, key_rows, values, beta_rows, restarts):

    def token_step(carried, inputs):
        query_row, key_row, value_row, beta_row, restart = inputs
        initial = carried * (1.0 - restart)
        guessed = jnp.einsum('hvk,hk->hv', initial, key_row, precision=highest)
        updated = initial - (beta_row[:, None] * (guessed - value_row))[:, :, None] * key_row[:, None, :]
        return (updated, jnp.einsum('hvk,hk->hv', updated, query_row, precision=highest))

    def block_step(carried, inputs):
        return lax.scan(token_step, carried, inputs)
    blocks = tuple((column.reshape((-1, BLOCK) + column.shape[1:]) for column in (queries, key_rows, values, beta_rows, restarts)))
    initial = jnp.zeros((H, DK, DK), jnp.float32)
    final_state, outputs = lax.scan(jax.checkpoint(block_step), initial, blocks)
    return outputs.reshape(queries.shape)

def reference(tokens, attn_gain, w_query, w_key, w_value, conv_weight, w_beta, w_gate_out, onorm_gain, w_out, mlp_gain, w_mlp_gate, w_mlp_up, w_down, seq_lengths, cotangent):
    total_rows = tokens.shape[0]
    positions = jnp.arange(total_rows, dtype=jnp.int32)
    distance = seq_offsets(seq_lengths, positions)
    restarts = (distance == 0).astype(jnp.float32)

    def forward(token_rows, gain_attn, query_weight, key_weight, value_weight, conv_rows, beta_weight, gate_out_weight, onorm_scale, out_weight, gain_mlp, mlp_gate_weight, mlp_up_weight, down_weight):
        normed = low(rms_scale(token_rows, gain_attn))
        projected = low_back(low(matmul(normed, jnp.concatenate([query_weight, key_weight, value_weight], axis=1))))
        convolved = conv_rows[CONV - 1] * projected
        for offset in range(CONV - 1):
            lagged = CONV - 1 - offset
            shifted = jnp.concatenate([jnp.zeros((lagged, projected.shape[1]), jnp.float32), projected[:total_rows - lagged]], axis=0)
            inside = (distance >= lagged).astype(jnp.float32)[:, None]
            convolved = convolved + conv_rows[offset] * shifted * inside
        active = jax.nn.silu(convolved).reshape(total_rows, 3, H, DK)
        queries = unit_rows(active[:, 0])
        key_rows = unit_rows(active[:, 1])
        values = active[:, 2]
        beta_rows = jax.nn.sigmoid(low_back(matmul(normed, beta_weight)))
        gate_logit = low_back(matmul(normed, gate_out_weight))
        mixed_heads = delta_rule(queries, key_rows, values, beta_rows, restarts)
        normalized = mixed_heads * lax.rsqrt(lax.optimization_barrier(jnp.mean(mixed_heads * mixed_heads, axis=-1, keepdims=True)) + 1e-05) * onorm_scale
        branch = low((normalized * jax.nn.silu(gate_logit.reshape(mixed_heads.shape))).reshape(total_rows, D))
        hidden = token_rows + low_back(matmul(branch, out_weight))
        normed_two = low(rms_scale(hidden, gain_mlp))
        gate_rows = low_back(matmul(normed_two, mlp_gate_weight))
        up_rows = low_back(matmul(normed_two, mlp_up_weight))
        inner_act = low(jax.nn.silu(gate_rows) * up_rows)
        return hidden + matmul(inner_act, down_weight)
    floats = tuple((array.astype(jnp.float32) for array in (tokens, attn_gain, w_query, w_key, w_value, conv_weight, w_beta, w_gate_out, onorm_gain, w_out, mlp_gain, w_mlp_gate, w_mlp_up, w_down)))
    result, pullback = jax.vjp(forward, *floats)
    gradients = pullback(cotangent.astype(jnp.float32))
    return (result.astype(jnp.bfloat16), gradients[0], gradients[1], gradients[2], gradients[3], gradients[4], gradients[5], gradients[6], gradients[7], gradients[8], gradients[9], gradients[10], gradients[11], gradients[12], gradients[13])
```

```python
from functools import partial

import jax
import jax.numpy as jnp
from jax import lax
from jax.experimental import pallas as pl
from jax.experimental.pallas import tpu as pltpu
from jax.sharding import PartitionSpec as P

CONV = 4
RIM = 8
LANES = 128
BASE = 16
SEQ, FSDP = "seq", "fsdp"
BOTH = (SEQ, FSDP)
f32 = jnp.float32
bf16 = jnp.bfloat16
highest = lax.Precision.HIGHEST
NN = (((1,), (0,)), ((), ()))
NT = (((1,), (1,)), ((), ()))
TN = (((0,), (0,)), ((), ()))


def mm(a, b, dims=NN, passes=6):
    if passes == 6:
        return lax.dot_general(a, b, dims, precision=highest, preferred_element_type=f32)
    a_high = a.astype(bf16)
    b_high = b.astype(bf16)
    out = lax.dot_general(a_high, b_high, dims, preferred_element_type=f32)
    if passes == 3:
        a_low = (a - a_high.astype(f32)).astype(bf16)
        b_low = (b - b_high.astype(f32)).astype(bf16)
        out = out + lax.dot_general(a_low, b_high, dims, preferred_element_type=f32)
        out = out + lax.dot_general(a_high, b_low, dims, preferred_element_type=f32)
    return out


def sigmoid(v):
    return 1.0 / (1.0 + jnp.exp(-v))


def iotas(rows):
    return (
        lax.broadcasted_iota(jnp.int32, (rows, rows), 0),
        lax.broadcasted_iota(jnp.int32, (rows, rows), 1),
    )


def unit_lower_inverse(lower, rows, cols, passes):
    size = lower.shape[0]
    same = (rows // BASE) == (cols // BASE)
    power = jnp.where(same, -lower, 0.0)
    inverse = jnp.where(rows == cols, 1.0, power)
    covered = 2
    while covered < BASE:
        power = mm(power, power, passes=passes)
        inverse = inverse + mm(inverse, power, passes=passes)
        covered *= 2
    block = BASE
    while block < size:
        joined = ((rows // (2 * block)) == (cols // (2 * block))) & (
            (rows // block) != (cols // block)
        )
        off = jnp.where(joined, lower, 0.0)
        inverse = inverse - mm(mm(inverse, off, passes=passes), inverse, passes=passes)
        block *= 2
    return inverse


def head_column(table, head):
    lanes = lax.broadcasted_iota(jnp.int32, table.shape, 1)
    return jnp.sum(jnp.where(lanes == head, table, 0.0), axis=1, keepdims=True)


def load_extended(ref, scratch, rows):
    scratch[0:RIM, :] = ref[rows : rows + RIM, :].astype(f32)
    scratch[RIM : RIM + rows, :] = ref[0:rows, :].astype(f32)


def convolve(scratch, taps, rows):
    total = taps[CONV - 1 : CONV, :] * scratch[RIM : RIM + rows, :]
    for j in range(CONV - 1):
        first = RIM - (CONV - 1) + j
        total = total + taps[j : j + 1, :] * scratch[first : first + rows, :]
    return total


FRONT_PASSES = 6
PASS_PASSES = 6
BACK_PASSES = 6


def front_kernel(
    pq, pk, pv, tq, tk, tv, beta_logit, q_out, k_out, v_out, t_out, l_out, b_out, scratch
):
    head = pl.program_id(0)
    rows = q_out.shape[0]
    active = []
    for ref, taps in ((pq, tq), (pk, tk), (pv, tv)):
        load_extended(ref, scratch, rows)
        c = convolve(scratch, taps, rows)
        active.append(c * sigmoid(c))
    a, b, v = active
    q_out[...] = a * lax.rsqrt(jnp.sum(a * a, axis=1, keepdims=True) + 1e-06)
    k = b * lax.rsqrt(jnp.sum(b * b, axis=1, keepdims=True) + 1e-06)
    k_out[...] = k
    v_out[...] = v
    beta = sigmoid(head_column(beta_logit[...], head))
    ri, ci = iotas(rows)
    lower = jnp.where(ri > ci, beta * mm(k, k, NT, FRONT_PASSES), 0.0)
    t = unit_lower_inverse(lower, ri, ci, FRONT_PASSES)
    t_out[0] = t
    u = mm(t, beta * v, NN, FRONT_PASSES)
    w = mm(t, beta * k, NN, FRONT_PASSES)
    size = k.shape[1]
    rs, cs = iotas(size)
    l_out[0] = jnp.where(rs == cs, 1.0, 0.0) - mm(w, k, TN, FRONT_PASSES)
    b_out[0] = mm(u, k, TN, FRONT_PASSES)


def pass_kernel(
    q_ref, k_ref, v_ref, t_ref, beta_logit, s_ref, gate_ref, gain_ref, branch_out, o_out, d_out, p_out
):
    head = pl.program_id(0)
    rows = q_ref.shape[0]
    q, k, s = q_ref[...], k_ref[...], s_ref[0]
    beta = sigmoid(head_column(beta_logit[...], head))
    ri, ci = iotas(rows)
    p = jnp.where(ri >= ci, mm(q, k, NT, PASS_PASSES), 0.0)
    p_out[0] = p
    missing = v_ref[...] - mm(k, s, NT, PASS_PASSES)
    d = mm(t_ref[0], beta * missing, NN, PASS_PASSES)
    d_out[...] = d
    o = mm(q, s, NT, PASS_PASSES) + mm(p, d, NN, PASS_PASSES)
    o_out[...] = o
    n = o * lax.rsqrt(jnp.mean(o * o, axis=1, keepdims=True) + 1e-05)
    g = gate_ref[...]
    branch_out[...] = (n * gain_ref[...] * (g * sigmoid(g))).astype(bf16)


def back_one_kernel(
    db_ref, o_ref, gate_ref, gain_ref, p_ref, t_ref, q_ref, k_ref, beta_logit,
    dgate_out, donorm_out, do_out, dr_out, g_out,
):
    head = pl.program_id(0)
    o = o_ref[...]
    g = gate_ref[...]
    gain = gain_ref[...]
    db = db_ref[...]
    beta = sigmoid(head_column(beta_logit[...], head))
    scale = lax.rsqrt(jnp.mean(o * o, axis=1, keepdims=True) + 1e-05)
    n = o * scale
    sig = sigmoid(g)
    z = g * sig
    dgate_out[...] = (db * n * gain * (sig * (1.0 + g * (1.0 - sig)))).astype(bf16)
    dy = db * z
    donorm_out[0] = jnp.sum(dy * n, axis=0, keepdims=True)
    dyg = dy * gain
    do = scale * dyg - o * (scale * scale * scale) * jnp.mean(dyg * o, axis=1, keepdims=True)
    do_out[...] = do
    dd = mm(p_ref[0], do, TN, BACK_PASSES)
    dr = mm(t_ref[0], dd, TN, BACK_PASSES)
    dr_out[...] = dr
    g_out[0] = mm(do, q_ref[...], TN, BACK_PASSES) - mm(beta * dr, k_ref[...], TN, BACK_PASSES)


def back_two_kernel(
    ds_ref, s_ref, t_ref, p_ref, q_ref, k_ref, v_ref, beta_logit, do_ref, dr_ref, d_ref,
    pq, pk, pv, tq, tk, tv,
    dq_out, dk_out, dv_out, rq_out, rk_out, rv_out, cq_out, ck_out, cv_out, dbeta_out,
    scratch, spread,
):
    head = pl.program_id(0)
    rows = q_ref.shape[0]
    ds, s = ds_ref[0], s_ref[0]
    q, k, v = q_ref[...], k_ref[...], v_ref[...]
    do, d = do_ref[...], d_ref[...]
    beta = sigmoid(head_column(beta_logit[...], head))
    ri, ci = iotas(rows)
    dr = dr_ref[...] + mm(t_ref[0], mm(k, ds, NT, BACK_PASSES), TN, BACK_PASSES)
    missing = v - mm(k, s, NT, BACK_PASSES)
    dp = jnp.where(ri >= ci, mm(do, d, NT, BACK_PASSES), 0.0)
    bdr = beta * dr
    dq = mm(do, s, NN, BACK_PASSES) + mm(dp, k, NN, BACK_PASSES)
    dk = mm(dp, q, TN, BACK_PASSES) + mm(d, ds, NN, BACK_PASSES) - mm(bdr, s, NN, BACK_PASSES)
    da = jnp.where(ri > ci, -mm(dr, d, NT, BACK_PASSES), 0.0)
    dbeta = jnp.sum(dr * missing, axis=1, keepdims=True) + jnp.sum(
        da * mm(k, k, NT, BACK_PASSES), axis=1, keepdims=True
    )
    dm = beta * da
    dk = dk + mm(dm, k, NN, BACK_PASSES) + mm(dm, k, TN, BACK_PASSES)
    dlogit = dbeta * beta * (1.0 - beta)

    @pl.when(head == 0)
    def _():
        dbeta_out[...] = jnp.zeros_like(dbeta_out)

    lanes = lax.broadcasted_iota(jnp.int32, dbeta_out.shape, 1)
    dbeta_out[...] = jnp.where(lanes == head, dlogit, dbeta_out[...])
    width = q.shape[1]
    spread[0:RIM, :] = jnp.zeros((RIM, width), f32)
    spread[RIM + rows : RIM + rows + RIM, :] = jnp.zeros((RIM, width), f32)
    sets = (
        (pq, tq, dq, q, dq_out, rq_out, cq_out),
        (pk, tk, dk, k, dk_out, rk_out, ck_out),
        (pv, tv, bdr, None, dv_out, rv_out, cv_out),
    )
    for proj, taps, du, unit, out, rim_out, tap_out in sets:
        load_extended(proj, scratch, rows)
        c = convolve(scratch, taps, rows)
        sig = sigmoid(c)
        if unit is not None:
            act = c * sig
            inv = lax.rsqrt(jnp.sum(act * act, axis=1, keepdims=True) + 1e-06)
            du = (du - unit * jnp.sum(unit * du, axis=1, keepdims=True)) * inv
        dc = du * (sig * (1.0 + c * (1.0 - sig)))
        spread[RIM : RIM + rows, :] = dc
        total = jnp.zeros((rows, width), f32)
        rim = jnp.zeros((RIM, width), f32)
        for j in range(CONV):
            lag = CONV - 1 - j
            tap = taps[j : j + 1, :]
            total = total + tap * spread[RIM + lag : RIM + lag + rows, :]
            rim = rim + tap * spread[lag : lag + RIM, :]
            first = RIM - lag
            tap_out[j : j + 1, :] = jnp.sum(
                dc * scratch[first : first + rows, :], axis=0, keepdims=True
            )
        out[...] = total
        rim_out[...] = rim


def params():
    return pltpu.CompilerParams(
        dimension_semantics=("arbitrary",), vmem_limit_bytes=48 * 1024 * 1024
    )


def column_block(rows, heads, part):
    return pl.BlockSpec((rows, LANES), lambda h, part=part: (0, part * heads + h))


def whole(shape):
    return pl.BlockSpec(shape, lambda h: (0,) * len(shape))


def per_head(shape):
    return pl.BlockSpec((1,) + shape, lambda h: (h, 0, 0))


def run_front(proj, taps, beta_logit, rows, heads):
    width = LANES
    p_spec = [column_block(rows + RIM, heads, i) for i in range(3)]
    t_spec = [column_block(CONV, heads, i) for i in range(3)]
    row_spec = column_block(rows, heads, 0)
    return pl.pallas_call(
        front_kernel,
        grid=(heads,),
        in_specs=p_spec + t_spec + [whole((rows, LANES))],
        out_specs=[row_spec] * 3
        + [per_head((rows, rows)), per_head((width, width)), per_head((width, width))],
        out_shape=[jax.ShapeDtypeStruct((rows, heads * width), f32)] * 3
        + [
            jax.ShapeDtypeStruct((heads, rows, rows), f32),
            jax.ShapeDtypeStruct((heads, width, width), f32),
            jax.ShapeDtypeStruct((heads, width, width), f32),
        ],
        scratch_shapes=[pltpu.VMEM((rows + RIM, width), f32)],
        compiler_params=params(),
        name="front",
    )(proj, proj, proj, taps, taps, taps, beta_logit)


def run_pass(q, k, v, t, beta_logit, states, gate, gain, rows, heads):
    width = LANES
    row_spec = column_block(rows, heads, 0)
    square = per_head((rows, rows))
    return pl.pallas_call(
        pass_kernel,
        grid=(heads,),
        in_specs=[
            row_spec, row_spec, row_spec, square, whole((rows, LANES)),
            per_head((width, width)), row_spec, whole((1, width)),
        ],
        out_specs=[row_spec, row_spec, row_spec, square],
        out_shape=[
            jax.ShapeDtypeStruct((rows, heads * width), bf16),
            jax.ShapeDtypeStruct((rows, heads * width), f32),
            jax.ShapeDtypeStruct((rows, heads * width), f32),
            jax.ShapeDtypeStruct((heads, rows, rows), f32),
        ],
        compiler_params=params(),
        name="chunk_pass",
    )(q, k, v, t, beta_logit, states, gate, gain)


def run_back_one(d_branch, o, gate, gain, p, t, q, k, beta_logit, rows, heads):
    width = LANES
    row_spec = column_block(rows, heads, 0)
    square = per_head((rows, rows))
    return pl.pallas_call(
        back_one_kernel,
        grid=(heads,),
        in_specs=[
            row_spec, row_spec, row_spec, whole((1, width)), square, square, row_spec, row_spec,
            whole((rows, LANES)),
        ],
        out_specs=[row_spec, per_head((1, width)), row_spec, row_spec, per_head((width, width))],
        out_shape=[
            jax.ShapeDtypeStruct((rows, heads * width), bf16),
            jax.ShapeDtypeStruct((heads, 1, width), f32),
            jax.ShapeDtypeStruct((rows, heads * width), f32),
            jax.ShapeDtypeStruct((rows, heads * width), f32),
            jax.ShapeDtypeStruct((heads, width, width), f32),
        ],
        compiler_params=params(),
        name="back_one",
    )(d_branch, o, gate, gain, p, t, q, k, beta_logit)


def run_back_two(ds, s, t, p, q, k, v, beta_logit, do, dr, d, proj, taps, rows, heads):
    width = LANES
    row_spec = column_block(rows, heads, 0)
    square = per_head((rows, rows))
    state = per_head((width, width))
    p_spec = [column_block(rows + RIM, heads, i) for i in range(3)]
    t_spec = [column_block(CONV, heads, i) for i in range(3)]
    return pl.pallas_call(
        back_two_kernel,
        grid=(heads,),
        in_specs=[
            state, state, square, square, row_spec, row_spec, row_spec, whole((rows, LANES)),
            row_spec, row_spec, row_spec,
        ]
        + p_spec
        + t_spec,
        out_specs=[row_spec] * 3
        + [column_block(RIM, heads, 0)] * 3
        + [column_block(CONV, heads, 0)] * 3
        + [whole((rows, LANES))],
        out_shape=[jax.ShapeDtypeStruct((rows, heads * width), f32)] * 3
        + [jax.ShapeDtypeStruct((RIM, heads * width), f32)] * 3
        + [jax.ShapeDtypeStruct((CONV, heads * width), f32)] * 3
        + [jax.ShapeDtypeStruct((rows, LANES), f32)],
        scratch_shapes=[
            pltpu.VMEM((rows + RIM, width), f32),
            pltpu.VMEM((rows + 2 * RIM, width), f32),
        ],
        compiler_params=params(),
        name="back_two",
    )(ds, s, t, p, q, k, v, beta_logit, do, dr, d, proj, proj, proj, taps, taps, taps)


def swap_parts(parts, axis):
    count = lax.axis_size(axis)
    place = lax.axis_index(axis)
    own = lax.dynamic_slice_in_dim(parts, place, 1, 0)
    result = jnp.zeros_like(parts)
    result = lax.dynamic_update_slice_in_dim(result, own, place, 0)
    for hop in range(1, count):
        target = lax.rem(place + hop, count)
        sent = lax.dynamic_slice_in_dim(parts, target, 1, 0)
        pairs = [(i, (i + hop) % count) for i in range(count)]
        got = lax.ppermute(sent, axis, pairs)
        source = lax.rem(place + count - hop, count)
        result = lax.dynamic_update_slice_in_dim(result, got, source, 0)
    return result


def bmm(a, b):
    return jnp.einsum("...ij,...jk->...ik", a, b, precision=highest)


def bmm_t(a, b):
    return jnp.einsum("...ij,...kj->...ik", a, b, precision=highest)


def shift_groups(array, by):
    size = lax.axis_size(SEQ)
    return lax.ppermute(
        array, SEQ, [(i, i + by) for i in range(size) if 0 <= i + by < size]
    )


def states_entering(linear, constant, before, reach):
    count = lax.axis_size(FSDP)
    heads, width = linear.shape[0], linear.shape[1]
    mine = heads // count
    pair = jnp.concatenate([linear, constant], axis=1).reshape(count, mine, 2 * width, width)
    pair = swap_parts(pair, FSDP)
    linears = [pair[i, :, :width] for i in range(count)]
    prefix = [pair[0]]
    for i in range(1, count):
        joined = bmm(prefix[-1], linears[i])
        prefix.append(
            jnp.concatenate(
                [joined[:, :width], joined[:, width:] + pair[i, :, width:]], axis=1
            )
        )
    group = prefix[-1]
    earlier = [shift_groups(group, hop) for hop in range(1, reach + 1)]
    state = jnp.zeros((mine, width, width), f32)
    for hop in range(reach, 0, -1):
        total = earlier[hop - 1]
        state = bmm(state, total[:, :width]) + total[:, width:]
        state = jnp.where(hop <= before, state, 0.0)
    entries = [state]
    for i in range(1, count):
        entries.append(bmm(state, prefix[i - 1][:, :width]) + prefix[i - 1][:, width:])
    entering = swap_parts(jnp.stack(entries), FSDP).reshape(heads, width, width)
    later = [shift_groups(group[:, :width], -hop) for hop in range(1, reach + 1)]
    return entering, linears, later


def state_grads_leaving(grads, linears, later, after, reach):
    count = lax.axis_size(FSDP)
    heads, width = grads.shape[0], grads.shape[1]
    mine = heads // count
    parts = swap_parts(grads.reshape(count, mine, width, width), FSDP)
    inner = [None] * count
    inner[count - 1] = jnp.zeros((mine, width, width), f32)
    tails = [None] * count
    for i in range(count - 2, -1, -1):
        inner[i] = bmm_t(inner[i + 1], linears[i + 1]) + parts[i + 1]
        tails[i] = (
            linears[i + 1] if tails[i + 1] is None else bmm(linears[i + 1], tails[i + 1])
        )
    group = bmm_t(inner[0], linears[0]) + parts[0]
    beyond = [shift_groups(group, -hop) for hop in range(1, reach + 1)]
    state = jnp.zeros((mine, width, width), f32)
    for hop in range(reach, 0, -1):
        state = bmm_t(state, later[hop - 1]) + beyond[hop - 1]
        state = jnp.where(hop <= after, state, 0.0)
    entries = [inner[i] + bmm_t(state, tails[i]) for i in range(count - 1)] + [state]
    return swap_parts(jnp.stack(entries), FSDP).reshape(heads, width, width)


def rms(values):
    return lax.rsqrt(jnp.mean(values * values, axis=-1, keepdims=True) + 1e-05)


def rms_back(values, scale, gain, dy):
    dyg = dy * gain
    grad = scale * dyg - values * (scale * scale * scale) * jnp.mean(
        dyg * values, axis=-1, keepdims=True
    )
    return grad, jnp.sum(dy * values * scale, axis=0)


def dot(a, b):
    return jnp.dot(a, b, preferred_element_type=f32)


def dot_t(a, b):
    return lax.dot_general(a, b, NT, preferred_element_type=f32)


def t_dot(a, b):
    return lax.dot_general(a, b, TN, preferred_element_type=f32)


def local(
    tokens, attn_gain, w_query, w_key, w_value, conv_weight, w_beta, w_gate_out, onorm_gain,
    w_out, mlp_gain, w_mlp_gate, w_mlp_up, w_down, seq_lengths, cotangent,
):
    rows, model = tokens.shape
    heads = w_beta.shape[1]
    hidden_size = w_mlp_gate.shape[1]
    devices = lax.axis_size(BOTH)
    share = model // devices
    groups = lax.axis_size(SEQ)
    reach = groups // 2 - 1
    width = model // heads
    chan = 3 * model
    taps_per_row = CONV * 3

    group_rows = rows * lax.axis_size(FSDP)
    first = lax.axis_index(BOTH) * rows
    group_first = lax.axis_index(SEQ) * group_rows
    ends = jnp.cumsum(seq_lengths)
    starts = ends - seq_lengths
    begin = jnp.max(jnp.where(starts <= first, starts, 0))
    end = jnp.min(jnp.where(ends > first, ends, rows * devices))
    opens = first == begin
    before = (group_first - begin) // group_rows
    after = (end - group_first) // group_rows - 1

    misc = jnp.zeros((share, LANES), bf16)
    misc = misc.at[:, :heads].set(w_beta)
    misc = misc.at[:, heads].set(attn_gain)
    misc = misc.at[:, heads + 1].set(mlp_gain)
    misc = misc.at[:, heads + 2 : heads + 2 + taps_per_row].set(
        conv_weight.reshape(share, taps_per_row)
    )
    misc = misc.at[: onorm_gain.shape[0], heads + 2 + taps_per_row].set(onorm_gain)
    pack_one = jnp.concatenate([w_query, w_key, w_value, misc], axis=1)
    full_one = lax.all_gather(pack_one, BOTH, axis=0, tiled=True)
    pack_two = jnp.concatenate([w_gate_out, w_out, w_mlp_gate, w_mlp_up], axis=1)
    pack_two, full_one = lax.optimization_barrier((pack_two, full_one))
    full_two = lax.all_gather(pack_two, BOTH, axis=0, tiled=True)
    w_down, full_two = lax.optimization_barrier((w_down, full_two))
    full_down = lax.all_gather(w_down, BOTH, axis=0, tiled=True)

    w_qkv = full_one[:, :chan]
    full_misc = full_one[:, chan:]
    gain_one = full_misc[:, heads].astype(f32)
    gain_two = full_misc[:, heads + 1].astype(f32)
    taps = (
        full_misc[:, heads + 2 : heads + 2 + taps_per_row]
        .reshape(devices, CONV, chan // devices)
        .swapaxes(0, 1)
        .reshape(CONV, chan)
        .astype(f32)
    )
    onorm = (
        full_misc[:, heads + 2 + taps_per_row]
        .reshape(devices, share)[:, : onorm_gain.shape[0]]
        .reshape(1, width)
        .astype(f32)
    )
    w_gate_full = full_two[:, :model]
    w_out_full = full_two[:, model : 2 * model]
    w_mg = full_two[:, 2 * model : 2 * model + hidden_size]
    w_mu = full_two[:, 2 * model + hidden_size :]

    rim_tokens = lax.ppermute(
        tokens[rows - RIM :], BOTH, [(i, i + 1) for i in range(devices - 1)]
    )
    rim_tokens = jnp.where(opens, jnp.zeros_like(rim_tokens), rim_tokens)
    x_all = jnp.concatenate([tokens, rim_tokens], axis=0).astype(f32)
    scale_all = rms(x_all)
    normed_all = (x_all * scale_all * gain_one).astype(bf16)
    projected = dot(normed_all, w_qkv).astype(bf16)
    normed = normed_all[:rows]
    x = tokens.astype(f32)
    scale_one = scale_all[:rows]
    beta_logit = dot(normed, full_misc)
    q, k, v, t, linear, constant = run_front(projected, taps, beta_logit, rows, heads)
    entering, linears, later = states_entering(linear, constant, before, reach)
    gate_logit = dot(normed, w_gate_full)
    branch, o, d, p = run_pass(
        q, k, v, t, beta_logit, entering, gate_logit, onorm, rows, heads
    )
    hidden = x + dot(branch, w_out_full)
    scale_two = rms(hidden)
    normed_two = (hidden * scale_two * gain_two).astype(bf16)
    gate_rows = dot(normed_two, w_mg)
    up_rows = dot(normed_two, w_mu)
    sig = sigmoid(gate_rows)
    act = gate_rows * sig
    inner = (act * up_rows).astype(bf16)
    output = (hidden + dot(inner, full_down)).astype(bf16)

    d_inner = dot_t(cotangent, full_down)
    d_gate = (d_inner * up_rows * (sig * (1.0 + gate_rows * (1.0 - sig)))).astype(bf16)
    d_up = (d_inner * act).astype(bf16)
    grad_down = t_dot(inner, cotangent).astype(bf16)
    grad_mg = t_dot(normed_two, d_gate).astype(bf16)
    grad_mu = t_dot(normed_two, d_up).astype(bf16)
    d_normed_two = dot_t(d_gate, w_mg) + dot_t(d_up, w_mu)
    d_norm, grad_gain_two = rms_back(hidden, scale_two, gain_two, d_normed_two)
    d_hidden = cotangent.astype(f32) + d_norm
    d_attn = d_hidden.astype(bf16)
    d_branch = dot_t(d_attn, w_out_full)
    grad_wout = t_dot(branch, d_attn).astype(bf16)

    d_gate_logit, d_onorm, d_o, d_r, state_grad = run_back_one(
        d_branch, o, gate_logit, onorm, p, t, q, k, beta_logit, rows, heads
    )
    leaving = state_grads_leaving(state_grad, linears, later, after, reach)
    grad_wgate = t_dot(normed, d_gate_logit).astype(bf16)
    outs = run_back_two(
        leaving, entering, t, p, q, k, v, beta_logit, d_o, d_r, d, projected, taps, rows, heads
    )
    d_local = outs[0:3]
    rims = jnp.concatenate(outs[3:6], axis=1)
    d_taps = jnp.concatenate(outs[6:9], axis=1)
    d_beta = outs[9].astype(bf16)
    rims = jnp.where(opens, jnp.zeros_like(rims), rims)
    rims = lax.ppermute(rims, BOTH, [(i + 1, i) for i in range(devices - 1)])
    d_cols = []
    for i in range(3):
        part = d_local[i]
        tail = part[rows - RIM :] + rims[:, i * model : (i + 1) * model]
        d_cols.append(jnp.concatenate([part[: rows - RIM], tail], axis=0).astype(bf16))
    d_proj = jnp.concatenate(d_cols, axis=1)
    grad_qkv = t_dot(normed, d_proj).astype(bf16)
    grad_beta = t_dot(normed, d_beta)[:, :heads]
    beta_cols = jnp.where(
        lax.broadcasted_iota(jnp.int32, full_misc.shape, 1) < heads, full_misc, 0
    )
    d_normed = dot_t(d_proj, w_qkv) + dot_t(d_beta, beta_cols) + dot_t(d_gate_logit, w_gate_full)
    d_token_norm, grad_gain_one = rms_back(x, scale_one, gain_one, d_normed)
    grad_tokens = d_hidden + d_token_norm

    grad_misc = jnp.zeros((model, LANES), f32)
    grad_misc = grad_misc.at[:, :heads].set(grad_beta)
    grad_misc = grad_misc.at[:, heads].set(grad_gain_one)
    grad_misc = grad_misc.at[:, heads + 1].set(grad_gain_two)
    grad_misc = grad_misc.at[:, heads + 2 : heads + 2 + taps_per_row].set(
        d_taps.reshape(CONV, devices, chan // devices).swapaxes(0, 1).reshape(model, taps_per_row)
    )
    own_gain = onorm_gain.shape[0]
    onorm_cols = jnp.zeros((devices, share), f32)
    onorm_cols = onorm_cols.at[:, :own_gain].set(
        jnp.sum(d_onorm, axis=(0, 1)).reshape(devices, own_gain)
    )
    grad_misc = grad_misc.at[:, heads + 2 + taps_per_row].set(onorm_cols.reshape(model))

    def scattered(term):
        return lax.psum_scatter(term, BOTH, scatter_dimension=0, tiled=True).astype(f32)

    g_mlp = scattered(jnp.concatenate([grad_mg, grad_mu], axis=1))
    g_down = scattered(grad_down)
    g_attn = scattered(
        jnp.concatenate([grad_qkv, grad_wgate, grad_wout, grad_misc.astype(bf16)], axis=1)
    )
    g_misc = g_attn[:, 5 * model :]
    return (
        output,
        grad_tokens,
        g_misc[:, heads],
        g_attn[:, :model],
        g_attn[:, model : 2 * model],
        g_attn[:, 2 * model : 3 * model],
        g_misc[:, heads + 2 : heads + 2 + taps_per_row].reshape(CONV, chan // devices),
        g_misc[:, :heads],
        g_attn[:, 3 * model : 4 * model],
        g_misc[:own_gain, heads + 2 + taps_per_row],
        g_attn[:, 4 * model : 5 * model],
        g_misc[:, heads + 1],
        g_mlp[:, :hidden_size],
        g_mlp[:, hidden_size:],
        g_down,
    )


def solution(mesh):
    rows = P(BOTH, None)
    flat = P(BOTH)
    cols = P(None, BOTH)
    return jax.shard_map(
        local,
        mesh=mesh,
        in_specs=(
            rows, flat, rows, rows, rows, cols, rows, rows, flat, rows, flat, rows, rows, rows,
            P(), rows,
        ),
        out_specs=(
            rows, rows, flat, rows, rows, rows, cols, rows, rows, flat, rows, flat, rows, rows,
            rows,
        ),
        check_vma=False,
    )
```

```python
import jax
import jax.numpy as jnp
from jax import lax
from jax.experimental import pallas as pl
from jax.experimental.pallas import tpu as pltpu
from jax.sharding import PartitionSpec as P

CONV = 4
RIM = 8
TAIL = 16
LANES = 128
BASE = 16
SEQ, FSDP = "seq", "fsdp"
BOTH = (SEQ, FSDP)
f32 = jnp.float32
bf16 = jnp.bfloat16
highest = lax.Precision.HIGHEST
NN = (((1,), (0,)), ((), ()))
NT = (((1,), (1,)), ((), ()))
TN = (((0,), (0,)), ((), ()))


class Parts:
    def __init__(self, value, passes=3):
        self.high = value.astype(bf16)
        self.low = (value - self.high.astype(f32)).astype(bf16) if passes == 3 else None


def mm(a, b, dims=NN, passes=3):
    a = a if isinstance(a, Parts) else Parts(a, passes)
    b = b if isinstance(b, Parts) else Parts(b, passes)
    if passes == 1:
        return lax.dot_general(a.high, b.high, dims, preferred_element_type=f32)
    left = jnp.concatenate([a.high, a.low, a.high], axis=dims[0][0][0])
    right = jnp.concatenate([b.high, b.high, b.low], axis=dims[0][1][0])
    return lax.dot_general(left, right, dims, preferred_element_type=f32)


def sigmoid(v):
    return 1.0 / (1.0 + jnp.exp(-v))


def iotas(rows):
    return (
        lax.broadcasted_iota(jnp.int32, (rows, rows), 0),
        lax.broadcasted_iota(jnp.int32, (rows, rows), 1),
    )


def unit_lower_inverses(lowers, rows, cols, passes):
    size = lowers[0].shape[0]
    same = (rows // BASE) == (cols // BASE)
    powers = [jnp.where(same, -lower, 0.0) for lower in lowers]
    inverses = [jnp.where(rows == cols, 1.0, power) for power in powers]
    covered = 2
    while covered < BASE:
        parts = [Parts(power, passes) for power in powers]
        powers = [mm(part, part, NN, passes) for part in parts]
        inverses = [a + mm(a, b, NN, passes) for a, b in zip(inverses, powers)]
        covered *= 2
    block = BASE
    while block < size:
        joined = ((rows // (2 * block)) == (cols // (2 * block))) & (
            (rows // block) != (cols // block)
        )
        parts = [Parts(inverse, passes) for inverse in inverses]
        inner = [
            mm(part, jnp.where(joined, lower, 0.0), NN, passes)
            for part, lower in zip(parts, lowers)
        ]
        inverses = [
            inverse - mm(off, part, NN, passes)
            for inverse, off, part in zip(inverses, inner, parts)
        ]
        block *= 2
    return inverses


def head_column(table, head):
    lanes = lax.broadcasted_iota(jnp.int32, table.shape, 1)
    first = LANES - pl.num_programs(0) * PER_STEP
    return jnp.sum(jnp.where(lanes == first + head, table, 0.0), axis=1, keepdims=True)


def load_extended(ref, scratch, rows):
    scratch[0:RIM, :] = ref[rows : rows + RIM, :].astype(f32)
    scratch[RIM : RIM + rows, :] = ref[0:rows, :].astype(f32)


def convolve(scratch, taps, rows):
    total = taps[CONV - 1 : CONV, :] * scratch[RIM : RIM + rows, :]
    for j in range(CONV - 1):
        first = RIM - (CONV - 1) + j
        total = total + taps[j : j + 1, :] * scratch[first : first + rows, :]
    return total


FRONT_PASSES = 3
PASS_PASSES = 3
BACK_PASSES = 3
PER_STEP = 2


def lanes_of(i):
    return slice(i * LANES, (i + 1) * LANES)


def front_kernel(
    pq, pk, pv, tq, tk, tv, beta_logit, q_out, k_out, v_out, t_out, pair_out, scratch
):
    rows = q_out.shape[0]
    active = []
    for ref, taps in ((pq, tq), (pk, tk), (pv, tv)):
        load_extended(ref, scratch, rows)
        c = convolve(scratch, taps, rows)
        active.append(c * sigmoid(c))
    logits = beta_logit[...]
    ri, ci = iotas(rows)
    lowers, keys, values, betas = [], [], [], []
    for i in range(PER_STEP):
        head = pl.program_id(0) * PER_STEP + i
        a, b, v = (part[:, lanes_of(i)] for part in active)
        q_out[:, lanes_of(i)] = a * lax.rsqrt(jnp.sum(a * a, axis=1, keepdims=True) + 1e-06)
        k = b * lax.rsqrt(jnp.sum(b * b, axis=1, keepdims=True) + 1e-06)
        k_out[:, lanes_of(i)] = k
        v_out[:, lanes_of(i)] = v
        beta = sigmoid(head_column(logits, head))
        part = Parts(k, FRONT_PASSES)
        lowers.append(jnp.where(ri > ci, beta * mm(part, part, NT, FRONT_PASSES), 0.0))
        keys.append(part)
        values.append(beta * v)
        betas.append(beta * k)
    inverses = unit_lower_inverses(lowers, ri, ci, FRONT_PASSES)
    for i in range(PER_STEP):
        t_out[i] = inverses[i]
        both = mm(
            inverses[i], jnp.concatenate([betas[i], values[i]], axis=1), NN, FRONT_PASSES
        )
        rs, cs = iotas(LANES)
        made = mm(both, keys[i], TN, FRONT_PASSES)
        pair_out[i, :LANES] = jnp.where(rs == cs, 1.0, 0.0) - made[:LANES]
        pair_out[i, LANES:] = made[LANES:]


def by_hop(place_ref, refs):
    count = len(refs)
    hop = lax.rem(place_ref[0] - pl.program_id(0) + count, count)
    value = refs[0][...]
    for h in range(1, count):
        value = jnp.where(hop == h, refs[h][...], value)
    return value[0]


def pass_kernel(
    place_ref, q_ref, k_ref, v_ref, t_ref, beta_logit, gate_ref, gain_ref, *rest
):
    state_refs, (branch_out, o_out, d_out, p_out) = rest[:-4], rest[-4:]
    states = by_hop(place_ref, state_refs)
    rows = q_ref.shape[0]
    logits = beta_logit[...]
    ri, ci = iotas(rows)
    for i in range(PER_STEP):
        head = pl.program_id(0) * PER_STEP + i
        cols = lanes_of(i)
        q, k, s = (Parts(m, PASS_PASSES) for m in (q_ref[:, cols], k_ref[:, cols], states[i]))
        beta = sigmoid(head_column(logits, head))
        p = jnp.where(ri >= ci, mm(q, k, NT, PASS_PASSES), 0.0)
        p_out[i] = p
        missing = v_ref[:, cols] - mm(k, s, NT, PASS_PASSES)
        d = mm(t_ref[i], beta * missing, NN, PASS_PASSES)
        d_out[:, cols] = d
        o = mm(q, s, NT, PASS_PASSES) + mm(p, d, NN, PASS_PASSES)
        o_out[:, cols] = o
        n = o * lax.rsqrt(jnp.mean(o * o, axis=1, keepdims=True) + 1e-05)
        g = gate_ref[:, cols]
        branch_out[:, cols] = (n * gain_ref[...] * (g * sigmoid(g))).astype(bf16)


def back_one_kernel(
    db_ref, o_ref, gate_ref, gain_ref, p_ref, t_ref, q_ref, k_ref, beta_logit,
    dgate_out, donorm_out, do_out, dr_out, g_out,
):
    gain = gain_ref[...]
    logits = beta_logit[...]
    for i in range(PER_STEP):
        head = pl.program_id(0) * PER_STEP + i
        cols = lanes_of(i)
        o = o_ref[:, cols]
        g = gate_ref[:, cols]
        db = db_ref[:, cols]
        beta = sigmoid(head_column(logits, head))
        scale = lax.rsqrt(jnp.mean(o * o, axis=1, keepdims=True) + 1e-05)
        n = o * scale
        sig = sigmoid(g)
        z = g * sig
        dgate_out[:, cols] = (db * n * gain * (sig * (1.0 + g * (1.0 - sig)))).astype(bf16)
        dy = db * z
        donorm_out[i] = jnp.sum(dy * n, axis=0, keepdims=True)
        dyg = dy * gain
        do = scale * dyg - o * (scale * scale * scale) * jnp.mean(dyg * o, axis=1, keepdims=True)
        do_out[:, cols] = do
        do = Parts(do, BACK_PASSES)
        dd = mm(p_ref[i], do, TN, BACK_PASSES)
        dr = mm(t_ref[i], dd, TN, BACK_PASSES)
        dr_out[:, cols] = dr
        g_out[i] = mm(do, q_ref[:, cols], TN, BACK_PASSES) - mm(
            beta * dr, k_ref[:, cols], TN, BACK_PASSES
        )


def back_two_kernel(
    place_ref, t_ref, p_ref, q_ref, k_ref, v_ref, beta_logit, do_ref, dr_ref, d_ref,
    pq, pk, pv, tq, tk, tv, *rest,
):
    count = (len(rest) - 15) // 2
    grads_in = by_hop(place_ref, rest[:count])
    states_in = by_hop(place_ref, rest[count : 2 * count])
    dq_out, dk_out, dv_out, eq_out, ek_out, ev_out, rq_out, rk_out, rv_out = rest[-15:-6]
    cq_out, ck_out, cv_out, dbeta_out, scratch, spread = rest[-6:]
    step = pl.program_id(0)
    rows = q_ref.shape[0]
    logits = beta_logit[...]
    ri, ci = iotas(rows)
    passes = BACK_PASSES

    @pl.when(step == 0)
    def _():
        dbeta_out[...] = jnp.zeros_like(dbeta_out)

    d_units = ([], [], [])
    for i in range(PER_STEP):
        head = step * PER_STEP + i
        cols = lanes_of(i)
        ds, s, q, k, do, d = (
            Parts(m, passes)
            for m in (
                grads_in[i], states_in[i], q_ref[:, cols], k_ref[:, cols], do_ref[:, cols],
                d_ref[:, cols],
            )
        )
        beta = sigmoid(head_column(logits, head))
        dr = dr_ref[:, cols] + mm(t_ref[i], mm(k, ds, NT, passes), TN, passes)
        missing = v_ref[:, cols] - mm(k, s, NT, passes)
        dp = Parts(jnp.where(ri >= ci, mm(do, d, NT, passes), 0.0), passes)
        bdr = beta * dr
        dq = mm(do, s, NN, passes) + mm(dp, k, NN, passes)
        dk = mm(dp, q, TN, passes) + mm(d, ds, NN, passes) - mm(bdr, s, NN, passes)
        da = jnp.where(ri > ci, -mm(dr, d, NT, passes), 0.0)
        dbeta = jnp.sum(dr * missing, axis=1, keepdims=True) + jnp.sum(
            da * mm(k, k, NT, passes), axis=1, keepdims=True
        )
        dm = Parts(beta * da, passes)
        dk = dk + mm(dm, k, NN, passes) + mm(dm, k, TN, passes)
        dlogit = dbeta * beta * (1.0 - beta)
        lanes = lax.broadcasted_iota(jnp.int32, dbeta_out.shape, 1)
        column = LANES - pl.num_programs(0) * PER_STEP + head
        dbeta_out[...] = jnp.where(lanes == column, dlogit, dbeta_out[...])
        for grads, grad in zip(d_units, (dq, dk, bdr)):
            grads.append(grad)

    width = q_ref.shape[1]
    spread[0:RIM, :] = jnp.zeros((RIM, width), f32)
    spread[RIM + rows : RIM + rows + RIM, :] = jnp.zeros((RIM, width), f32)
    sets = (
        (pq, tq, d_units[0], q_ref, dq_out, eq_out, rq_out, cq_out),
        (pk, tk, d_units[1], k_ref, dk_out, ek_out, rk_out, ck_out),
        (pv, tv, d_units[2], None, dv_out, ev_out, rv_out, cv_out),
    )
    for proj, taps, grads, units, out, tail_out, rim_out, tap_out in sets:
        load_extended(proj, scratch, rows)
        c = convolve(scratch, taps, rows)
        sig = sigmoid(c)
        if units is not None:
            act = c * sig
            for i in range(PER_STEP):
                cols = lanes_of(i)
                part, unit = act[:, cols], units[:, cols]
                inv = lax.rsqrt(jnp.sum(part * part, axis=1, keepdims=True) + 1e-06)
                grads[i] = (
                    grads[i] - unit * jnp.sum(unit * grads[i], axis=1, keepdims=True)
                ) * inv
        dc = jnp.concatenate(grads, axis=1) * (sig * (1.0 + c * (1.0 - sig)))
        spread[RIM : RIM + rows, :] = dc
        total = jnp.zeros((rows, width), f32)
        rim = jnp.zeros((RIM, width), f32)
        for j in range(CONV):
            lag = CONV - 1 - j
            tap = taps[j : j + 1, :]
            total = total + tap * spread[RIM + lag : RIM + lag + rows, :]
            rim = rim + tap * spread[lag : lag + RIM, :]
            first = RIM - lag
            tap_out[j : j + 1, :] = jnp.sum(
                dc * scratch[first : first + rows, :], axis=0, keepdims=True
            )
        out[...] = total.astype(bf16)
        tail_out[...] = total[rows - TAIL :]
        rim_out[...] = rim


LIGHT = pl.CostEstimate(flops=1, bytes_accessed=1, transcendentals=0)


def params():
    return pltpu.CompilerParams(
        dimension_semantics=("arbitrary",), vmem_limit_bytes=56 * 1024 * 1024
    )


def column_block(rows, heads, part):
    steps = heads // PER_STEP
    return pl.BlockSpec((rows, PER_STEP * LANES), lambda h, part=part: (0, part * steps + h))


def whole(shape):
    return pl.BlockSpec(shape, lambda h: (0,) * len(shape))


def scalar():
    return pl.BlockSpec(memory_space=pltpu.SMEM)


def per_head(shape):
    return pl.BlockSpec((PER_STEP,) + shape, lambda h: (h, 0, 0))


def pack_kernel(
    wq, wk, wv, wg, beta_ref, conv_ref, gain_ref, onorm_ref, mlp_ref, out, scratch
):
    model = wq.shape[1]
    for i, ref in enumerate((wq, wk, wv, wg)):
        out[:, i * model : (i + 1) * model] = ref[...]
    scratch[...] = jnp.zeros_like(scratch)
    taps, wide = conv_ref.shape
    scratch[0:taps, 0:wide] = conv_ref[...].astype(f32)
    for i, ref in enumerate((gain_ref, mlp_ref, onorm_ref)):
        scratch[taps + i : taps + i + 1, 0 : ref.shape[1]] = ref[...].astype(f32)
    heads = beta_ref.shape[1]
    scratch[:, LANES - heads :] = beta_ref[...].astype(f32)
    out[:, 4 * model :] = scratch[...].astype(bf16)


def run_pack(wq, wk, wv, wg, w_beta, conv, gain, onorm, mlp_gain):
    share, model = wq.shape
    return pl.pallas_call(
        pack_kernel,
        out_shape=jax.ShapeDtypeStruct((share, 4 * model + LANES), bf16),
        scratch_shapes=[pltpu.VMEM((share, LANES), f32)],
        name="pack",
    )(
        wq, wk, wv, wg, w_beta, conv, gain.reshape(1, -1), onorm.reshape(1, -1),
        mlp_gain.reshape(1, -1),
    )


def run_front(proj, taps, beta_logit, rows, heads):
    width = LANES
    p_spec = [column_block(rows + RIM, heads, i) for i in range(3)]
    t_spec = [column_block(CONV, heads, i) for i in range(3)]
    row_spec = column_block(rows, heads, 0)
    return pl.pallas_call(
        front_kernel,
        grid=(heads // PER_STEP,),
        in_specs=p_spec + t_spec + [whole((rows, LANES))],
        out_specs=[row_spec] * 3
        + [per_head((rows, rows)), per_head((2 * width, width))],
        out_shape=[jax.ShapeDtypeStruct((rows, heads * width), f32)] * 3
        + [
            jax.ShapeDtypeStruct((heads, rows, rows), f32),
            jax.ShapeDtypeStruct((heads, 2 * width, width), f32),
        ],
        scratch_shapes=[pltpu.VMEM((rows + RIM, PER_STEP * width), f32)],
        compiler_params=params(),
        cost_estimate=LIGHT,
        name="front",
    )(proj, proj, proj, taps, taps, taps, beta_logit)


def run_pass(place, q, k, v, t, beta_logit, states, gate, gain, rows, heads):
    width = LANES
    row_spec = column_block(rows, heads, 0)
    square = per_head((rows, rows))
    return pl.pallas_call(
        pass_kernel,
        grid=(heads // PER_STEP,),
        in_specs=[
            scalar(), row_spec, row_spec, row_spec, square, whole((rows, LANES)), row_spec,
            whole((1, width)),
        ]
        + [whole(state.shape) for state in states],
        out_specs=[row_spec, row_spec, row_spec, square],
        out_shape=[
            jax.ShapeDtypeStruct((rows, heads * width), bf16),
            jax.ShapeDtypeStruct((rows, heads * width), f32),
            jax.ShapeDtypeStruct((rows, heads * width), f32),
            jax.ShapeDtypeStruct((heads, rows, rows), f32),
        ],
        compiler_params=params(),
        cost_estimate=LIGHT,
        name="chunk_pass",
    )(place, q, k, v, t, beta_logit, gate, gain, *states)


def run_back_one(d_branch, o, gate, gain, p, t, q, k, beta_logit, rows, heads):
    width = LANES
    row_spec = column_block(rows, heads, 0)
    square = per_head((rows, rows))
    return pl.pallas_call(
        back_one_kernel,
        grid=(heads // PER_STEP,),
        in_specs=[
            row_spec, row_spec, row_spec, whole((1, width)), square, square, row_spec, row_spec,
            whole((rows, LANES)),
        ],
        out_specs=[row_spec, per_head((1, width)), row_spec, row_spec, per_head((width, width))],
        out_shape=[
            jax.ShapeDtypeStruct((rows, heads * width), bf16),
            jax.ShapeDtypeStruct((heads, 1, width), f32),
            jax.ShapeDtypeStruct((rows, heads * width), f32),
            jax.ShapeDtypeStruct((rows, heads * width), f32),
            jax.ShapeDtypeStruct((heads, width, width), f32),
        ],
        compiler_params=params(),
        cost_estimate=LIGHT,
        name="back_one",
    )(d_branch, o, gate, gain, p, t, q, k, beta_logit)


def run_back_two(
    place, grads, states, t, p, q, k, v, beta_logit, do, dr, d, proj, taps, rows, heads
):
    width = LANES
    row_spec = column_block(rows, heads, 0)
    square = per_head((rows, rows))
    p_spec = [column_block(rows + RIM, heads, i) for i in range(3)]
    t_spec = [column_block(CONV, heads, i) for i in range(3)]
    return pl.pallas_call(
        back_two_kernel,
        grid=(heads // PER_STEP,),
        in_specs=[
            scalar(), square, square, row_spec, row_spec, row_spec, whole((rows, LANES)),
            row_spec, row_spec, row_spec,
        ]
        + p_spec
        + t_spec
        + [whole(part.shape) for part in grads]
        + [whole(part.shape) for part in states],
        out_specs=[row_spec] * 3
        + [column_block(TAIL, heads, 0)] * 3
        + [column_block(RIM, heads, 0)] * 3
        + [column_block(CONV, heads, 0)] * 3
        + [whole((rows, LANES))],
        out_shape=[jax.ShapeDtypeStruct((rows, heads * width), bf16)] * 3
        + [jax.ShapeDtypeStruct((TAIL, heads * width), f32)] * 3
        + [jax.ShapeDtypeStruct((RIM, heads * width), f32)] * 3
        + [jax.ShapeDtypeStruct((CONV, heads * width), f32)] * 3
        + [jax.ShapeDtypeStruct((rows, LANES), f32)],
        scratch_shapes=[
            pltpu.VMEM((rows + RIM, PER_STEP * width), f32),
            pltpu.VMEM((rows + 2 * RIM, PER_STEP * width), f32),
        ],
        compiler_params=params(),
        cost_estimate=LIGHT,
        name="back_two",
    )(
        place, t, p, q, k, v, beta_logit, do, dr, d, proj, proj, proj, taps, taps, taps,
        *grads, *states,
    )


def prefix_kernel(place_ref, *rest):
    prefix_out, linear_out, ordered_ref = rest[-3:]
    parts = rest[:-3]
    count = len(parts)
    for hop in range(count):
        ordered_ref[lax.rem(place_ref[0] - hop + count, count)] = parts[hop][0]
    for m in range(ordered_ref.shape[1]):
        joined = ordered_ref[0, m]
        prefix_out[0, m] = joined
        linear_out[0, m] = joined[:LANES]
        for i in range(1, count):
            linear = ordered_ref[i, m, :LANES]
            linear_out[i, m] = linear
            joined = mm(joined, linear)
            joined = jnp.concatenate(
                [joined[:LANES], joined[LANES:] + ordered_ref[i, m, LANES:]], axis=0
            )
            prefix_out[i, m] = joined


def entry_kernel(before_ref, prefix, *rest):
    totals, out = rest[:-1], rest[-1]
    for m in range(prefix.shape[1]):
        state = jnp.zeros((LANES, LANES), f32)
        for hop in range(len(totals), 0, -1):
            total = totals[hop - 1]
            state = mm(state, total[m, :LANES]) + total[m, LANES:]
            state = jnp.where(hop <= before_ref[0], state, 0.0)
        out[0, m] = state
        for i in range(1, prefix.shape[0]):
            out[i, m] = mm(state, prefix[i - 1, m, :LANES]) + prefix[i - 1, m, LANES:]


def suffix_kernel(place_ref, linears, *rest):
    inner_out, group_out, ordered_ref = rest[-3:]
    parts = rest[:-3]
    count = len(parts)
    for hop in range(count):
        ordered_ref[lax.rem(place_ref[0] - hop + count, count)] = parts[hop][0]
    for m in range(ordered_ref.shape[1]):
        grad = jnp.zeros((LANES, LANES), f32)
        for i in range(count - 1, -1, -1):
            inner_out[i, m] = grad
            grad = mm(grad, linears[i, m], NT) + ordered_ref[i, m]
        group_out[m] = grad


def leave_kernel(after_ref, inner, linears, *rest):
    out = rest[-1]
    reach = (len(rest) - 1) // 2
    count = inner.shape[0]
    for m in range(inner.shape[1]):
        grad = jnp.zeros((LANES, LANES), f32)
        for hop in range(reach, 0, -1):
            grad = mm(grad, rest[reach + hop - 1][m], NT) + rest[hop - 1][m]
            grad = jnp.where(hop <= after_ref[0], grad, 0.0)
        for i in range(count - 1, -1, -1):
            out[i, m] = inner[i, m] + grad
            if i:
                grad = mm(grad, linears[i, m], NT)


def run_small(kernel, number, arrays, shapes, scratch, name):
    return pl.pallas_call(
        kernel,
        in_specs=[scalar()] + [pl.BlockSpec(memory_space=pltpu.VMEM)] * len(arrays),
        out_specs=[pl.BlockSpec(memory_space=pltpu.VMEM)] * len(shapes),
        out_shape=[jax.ShapeDtypeStruct(shape, f32) for shape in shapes],
        scratch_shapes=scratch,
        compiler_params=pltpu.CompilerParams(vmem_limit_bytes=56 * 1024 * 1024),
        cost_estimate=LIGHT,
        name=name,
    )(number, *arrays)


def swapped(parts, axis):
    count = lax.axis_size(axis)
    place = lax.axis_index(axis)
    result = [lax.dynamic_slice_in_dim(parts, place, 1, 0)]
    for hop in range(1, count):
        sent = lax.dynamic_slice_in_dim(parts, lax.rem(place + hop, count), 1, 0)
        result.append(lax.ppermute(sent, axis, [(i, (i + hop) % count) for i in range(count)]))
    return result


def shift_groups(array, by):
    size = lax.axis_size(SEQ)
    return lax.ppermute(
        array, SEQ, [(i, i + by) for i in range(size) if 0 <= i + by < size]
    )


def joined_chunks(pair, place):
    count = lax.axis_size(FSDP)
    heads, tall, width = pair.shape
    mine = heads // count
    parts = swapped(pair.reshape(count, mine, tall, width), FSDP)
    prefix, linears = run_small(
        prefix_kernel, place, parts,
        [(count, mine, tall, width), (count, mine, width, width)],
        [pltpu.VMEM((count, mine, tall, width), f32)], "prefix",
    )
    return prefix, linears


def states_entering(prefix, before, reach, others):
    count, mine, tall, width = prefix.shape
    group = prefix[count - 1]
    earlier = [shift_groups(group, hop) for hop in range(1, reach + 1)]
    earlier, others = tied(earlier, others)
    (entries,) = run_small(
        entry_kernel, before, [prefix] + earlier, [(count, mine, width, width)], [], "entry"
    )
    later = [shift_groups(group[:, :width], -hop) for hop in range(1, reach + 1)]
    return swapped(entries, FSDP), later, others


def state_grads_leaving(grads, linears, later, place, after, reach):
    count = lax.axis_size(FSDP)
    heads, width = grads.shape[0], grads.shape[1]
    mine = heads // count
    parts = swapped(grads.reshape(count, mine, width, width), FSDP)
    inner, group = run_small(
        suffix_kernel, place, [linears] + parts,
        [(count, mine, width, width), (mine, width, width)],
        [pltpu.VMEM((count, mine, width, width), f32)], "suffix",
    )
    beyond = [shift_groups(group, -hop) for hop in range(1, reach + 1)]
    (entries,) = run_small(
        leave_kernel, after, [inner, linears] + beyond + later,
        [(count, mine, width, width)], [], "leave",
    )
    return swapped(entries, FSDP)


def rms(values):
    return lax.rsqrt(jnp.mean(values * values, axis=-1, keepdims=True) + 1e-05)


def rms_back(values, scale, gain, dy):
    dyg = dy * gain
    grad = scale * dyg - values * (scale * scale * scale) * jnp.mean(
        dyg * values, axis=-1, keepdims=True
    )
    return grad, jnp.sum(dy * values * scale, axis=0)


def dot(a, b):
    return jnp.dot(a, b, preferred_element_type=f32)


def dot_t(a, b):
    return lax.dot_general(a, b, NT, preferred_element_type=f32)


def t_dot(a, b):
    return lax.dot_general(a, b, TN, preferred_element_type=f32)


def flips(bit, count):
    return [(i, i ^ bit) for i in range(count)]


def exchanged(array, bit):
    return lax.ppermute(array, BOTH, flips(bit, lax.axis_size(BOTH)))


def place_bits():
    index = lax.axis_index(BOTH)
    return {bit: lax.rem(index // bit, 2) for bit in (1, 2, 4)}


def tied(*values):
    return lax.optimization_barrier(values)


def owner_order(array, axis):
    count = lax.axis_size(BOTH)
    shape = array.shape
    blocks = array.reshape(shape[:axis] + (count // 8, 2, 2, 2, -1) + shape[axis + 1 :])
    order = tuple(range(axis)) + tuple(axis + i for i in (3, 2, 1, 0, 4))
    return blocks.transpose(order + tuple(range(axis + 5, blocks.ndim))).reshape(shape)


def owner_matrix(size):
    source = owner_order(jnp.arange(size, dtype=jnp.int32), 0)
    return (jnp.arange(size, dtype=jnp.int32)[:, None] == source[None, :]).astype(bf16)


def half(array, which, axis=0):
    size = array.shape[axis] // 2
    return lax.dynamic_slice_in_dim(array, which * size, size, axis)


FIRST = (2, 4)


def pick(array, axis, which):
    return lax.dynamic_index_in_dim(array, which, axis, False)


def columns(array, i):
    wide = array.shape[-1] // 2
    return array[..., i * wide : (i + 1) * wide]


def begin_terms(left, right):
    sent = t_dot(half(left, 1 - place_bits()[1], 1), right).astype(bf16)
    return exchanged(sent, 1)


def middle_terms(left, right, got):
    bits = place_bits()
    rows = left.shape[0]
    left = half(left, bits[1], 1).reshape(rows, 2, 2, -1)
    got = got.reshape((2, 2, -1) + got.shape[1:])
    kepts, sents = [], []
    for i, first in enumerate(FIRST):
        for side, outs in ((1 - bits[first], sents), (bits[first], kepts)):
            term = t_dot(pick(left, i + 1, side).reshape(rows, -1), columns(right, i))
            came = pick(columns(got, i), i, side)
            outs.append((term + came.reshape(term.shape).astype(f32)).astype(bf16))
    return kepts, sents


def cross(sents, bits):
    return [exchanged(sent, bit) for sent, bit in zip(sents, bits)]


def end_terms(kepts, gots):
    bits = place_bits()
    kepts = [(k.astype(f32) + g.astype(f32)).astype(bf16) for k, g in zip(kepts, gots)]
    mine = [half(k, bits[6 - first]) for k, first in zip(kepts, FIRST)]
    sents = [half(k, 1 - bits[6 - first]) for k, first in zip(kepts, FIRST)]
    return mine, sents


def owner_blocks(mine, gots):
    length = lax.axis_size(BOTH) // 8
    parts = [(m.astype(f32) + g.astype(f32)).astype(bf16) for m, g in zip(mine, gots)]
    return jnp.concatenate([p.reshape(length, -1, p.shape[-1]) for p in parts], axis=-1)


def stacked(blocks):
    length = len(blocks)
    place = lax.axis_index(BOTH) // 8
    back = jnp.stack(blocks[::-1] + blocks[::-1])
    return lax.dynamic_slice_in_dim(back, length - 1 - place, length, 0)


def merged(blocks, got, bit):
    mine = place_bits()[bit] == 0
    return jnp.stack([jnp.where(mine, blocks, got), jnp.where(mine, got, blocks)])


def along_last(by):
    count = lax.axis_size(BOTH)
    return [(i, (i + 8 * by) % count) for i in range(count)]


def send_blocks(blocks):
    length = blocks.shape[0]
    place = lax.axis_index(BOTH) // 8

    def block(i):
        return lax.dynamic_index_in_dim(blocks, lax.rem(i, length), 0, False)

    return [block(place)] + [
        lax.ppermute(block(place + hop), BOTH, along_last(hop)) for hop in range(1, length)
    ]


def added(parts):
    total = parts[0].astype(f32)
    for part in parts[1:]:
        total = total + part.astype(f32)
    return total


def local(
    tokens, attn_gain, w_query, w_key, w_value, conv_weight, w_beta, w_gate_out, onorm_gain,
    w_out, mlp_gain, w_mlp_gate, w_mlp_up, w_down, seq_lengths, cotangent,
):
    rows, model = tokens.shape
    heads = w_beta.shape[1]
    hidden_size = w_mlp_gate.shape[1]
    devices = lax.axis_size(BOTH)
    share = model // devices
    groups = lax.axis_size(SEQ)
    reach = groups // 2 - 1
    width = model // heads
    chan = 3 * model
    wide = chan // devices
    own_gain = onorm_gain.shape[0]
    pack_one = run_pack(
        w_query, w_key, w_value, w_gate_out, w_beta, conv_weight, attn_gain, onorm_gain, mlp_gain
    )
    full_one = lax.all_gather(pack_one, BOTH, axis=0, tiled=True)
    seq_lengths, w_mlp_gate, w_mlp_up, w_out, w_down, tokens, pack_one = (
        lax.optimization_barrier(
            (seq_lengths, w_mlp_gate, w_mlp_up, w_out, w_down, tokens, pack_one)
        )
    )
    down = [w_down] + [
        lax.ppermute(w_down, BOTH, along_last(hop)) for hop in range(1, devices // 8)
    ]
    down = stacked(down)
    halves = [columns(down, i) for i in range(2)]
    gots = cross(halves, FIRST[::-1])
    halves = [merged(h, g, bit) for h, g, bit in zip(halves, gots, FIRST[::-1])]
    full_one, halves = tied(full_one, halves)
    full_two = lax.all_gather(
        jnp.concatenate([w_out, owner_order(w_mlp_gate, 1), owner_order(w_mlp_up, 1)], axis=1),
        BOTH,
        axis=0,
        tiled=True,
    )
    to_order = owner_matrix(model)

    group_rows = rows * lax.axis_size(FSDP)
    first = lax.axis_index(BOTH) * rows
    group_first = lax.axis_index(SEQ) * group_rows
    ends = jnp.cumsum(seq_lengths)
    starts = ends - seq_lengths
    begin = jnp.max(jnp.where(starts <= first, starts, 0))
    end = jnp.min(jnp.where(ends > first, ends, rows * devices))
    opens = first == begin
    before = ((group_first - begin) // group_rows).reshape(1)
    beyond = ((end - group_first) // group_rows - 1).reshape(1)
    place = lax.axis_index(FSDP).reshape(1)

    heads_wide = chan + model
    w_heads = full_one[:, :heads_wide]
    full_misc = full_one[:, heads_wide:]
    w_out_full = full_two[:, :model]
    w_both = full_two[:, model:]
    misc = full_misc.reshape(devices, share, LANES)
    gain_one = misc[:, CONV, :share].reshape(model).astype(f32)
    gain_two = misc[:, CONV + 1, :share].reshape(model).astype(f32)
    onorm = misc[:, CONV + 2, :own_gain].reshape(1, width).astype(f32)
    taps = misc[:, :CONV, :wide].swapaxes(0, 1).reshape(CONV, chan).astype(f32)
    beta_cols = jnp.where(
        lax.broadcasted_iota(jnp.int32, full_misc.shape, 1) >= LANES - heads, full_misc, 0
    )

    rim_tokens = lax.ppermute(
        tokens[rows - RIM :], BOTH, [(i, i + 1) for i in range(devices - 1)]
    )
    rim_tokens = jnp.where(opens, jnp.zeros_like(rim_tokens), rim_tokens)
    x_all = jnp.concatenate([tokens, rim_tokens], axis=0).astype(f32)
    scale_all = rms(x_all)
    normed_all = (x_all * scale_all * gain_one).astype(bf16)
    projected = dot(normed_all, w_heads[:, :chan]).astype(bf16)
    normed = normed_all[:rows]
    x = tokens.astype(f32)
    scale_one = scale_all[:rows]
    beta_logit = dot(normed, full_misc)
    normed_order = dot(normed, to_order).astype(bf16)
    gots = cross(halves, FIRST)
    q, k, v, t, pair = run_front(projected, taps, beta_logit, rows, heads)
    pair, gots = tied(pair, gots)
    prefix, linears = joined_chunks(pair, place)
    halves = [merged(h, g, bit) for h, g, bit in zip(halves, gots, FIRST)]
    gots = cross(halves, (1, 1))
    prefix, gots = tied(prefix, gots)
    halves = [merged(h, g, 1) for h, g in zip(halves, gots)]
    halves[1] = halves[1].swapaxes(1, 2)
    full_down = jnp.concatenate([h.reshape(hidden_size, -1) for h in halves], axis=1)
    gate_logit = dot(normed, w_heads[:, chan:])
    states, later, (full_down, gate_logit) = states_entering(
        prefix, before, reach, (full_down, gate_logit)
    )
    branch, o, d, p = run_pass(
        place, q, k, v, t, beta_logit, states, gate_logit, onorm, rows, heads
    )
    hidden = x + dot(branch, w_out_full)
    scale_two = rms(hidden)
    normed_two = (hidden * scale_two * gain_two).astype(bf16)
    both_rows = dot(normed_two, w_both)
    gate_rows, up_rows = both_rows[:, :hidden_size], both_rows[:, hidden_size:]
    sig = sigmoid(gate_rows)
    act = gate_rows * sig
    inner = (act * up_rows).astype(bf16)
    down_got = begin_terms(inner, cotangent)
    output = (hidden + dot(inner, full_down)).astype(bf16)
    d_inner = dot_t(cotangent, full_down)
    d_both = jnp.concatenate(
        [d_inner * up_rows * (sig * (1.0 + gate_rows * (1.0 - sig))), d_inner * act], axis=1
    ).astype(bf16)
    grad_both = t_dot(normed_two, d_both).astype(bf16)
    down_kepts, down_sents = middle_terms(inner, cotangent, down_got)
    grad_both, d_both, down_kepts, down_sents = tied(grad_both, d_both, down_kepts, down_sents)
    g_mlp = lax.psum_scatter(grad_both, BOTH, scatter_dimension=0, tiled=True).astype(f32)
    down_gots = cross(down_sents, FIRST)
    d_normed_two = dot_t(d_both, w_both)
    d_norm, grad_gain_two = rms_back(hidden, scale_two, gain_two, d_normed_two)
    d_hidden = cotangent.astype(f32) + d_norm
    d_attn = d_hidden.astype(bf16)
    d_branch = dot_t(d_attn, w_out_full)
    branch_order = dot(branch, to_order).astype(bf16)
    out_got = begin_terms(branch_order, d_attn)
    d_branch, down_gots = tied(d_branch, down_gots)
    down_mine, down_sents = end_terms(down_kepts, down_gots)
    d_branch, down_mine, down_sents = tied(d_branch, down_mine, down_sents)
    down_gots = cross(down_sents, FIRST[::-1])
    d_gate_logit, d_onorm, d_o, d_r, state_grad = run_back_one(
        d_branch, o, gate_logit, onorm, p, t, q, k, beta_logit, rows, heads
    )
    leaving = state_grads_leaving(state_grad, linears, later, place, beyond, reach)
    out_kepts, out_sents = middle_terms(branch_order, d_attn, out_got)
    down_blocks = owner_blocks(down_mine, down_gots)
    leaving, out_kepts, out_sents, down_blocks = tied(leaving, out_kepts, out_sents, down_blocks)
    out_gots = cross(out_sents, FIRST)
    down_parts = send_blocks(down_blocks)
    outs = run_back_two(
        place, leaving, states, t, p, q, k, v, beta_logit, d_o, d_r, d, projected, taps,
        rows, heads,
    )
    outs, out_gots = tied(outs, out_gots)
    tails = jnp.concatenate(outs[3:6], axis=1)
    rims = jnp.concatenate(outs[6:9], axis=1)
    d_beta = outs[12].astype(bf16)
    rims = jnp.where(opens, jnp.zeros_like(rims), rims)
    rims = lax.ppermute(rims, BOTH, [(i + 1, i) for i in range(devices - 1)])
    tails = tails + jnp.pad(rims, ((TAIL - RIM, 0), (0, 0)))
    d_proj = lax.dynamic_update_slice_in_dim(
        jnp.concatenate(outs[0:3], axis=1), tails.astype(bf16), rows - TAIL, 0
    )
    d_heads = jnp.concatenate([d_proj, d_gate_logit], axis=1)
    d_heads, d_beta, out_gots = tied(d_heads, d_beta, out_gots)
    last_got = begin_terms(normed_order, d_heads)
    d_normed = dot_t(d_heads, w_heads) + dot_t(d_beta, beta_cols)
    d_token_norm, grad_gain_one = rms_back(x, scale_one, gain_one, d_normed)
    grad_tokens = d_hidden + d_token_norm
    out_mine, out_sents = end_terms(out_kepts, out_gots)
    last_got, grad_tokens, grad_gain_one, out_mine, out_sents = tied(
        last_got, grad_tokens, grad_gain_one, out_mine, out_sents
    )
    last_kepts, last_sents = middle_terms(normed_order, d_heads, last_got)
    last_kepts, last_sents, out_mine, out_sents, down_parts, grad_gain_one, d_beta = tied(
        last_kepts, last_sents, out_mine, out_sents, down_parts, grad_gain_one, d_beta
    )
    last_gots = cross(last_sents, FIRST)
    out_gots = cross(out_sents, FIRST[::-1])
    grad_beta = t_dot(d_beta, normed)[LANES - heads :]
    table = jnp.concatenate(
        list(outs[9:12])
        + [
            grad_gain_one.reshape(1, model),
            grad_gain_two.reshape(1, model),
            jnp.pad(jnp.sum(d_onorm, axis=(0, 1)).reshape(1, width), ((0, 0), (0, model - width))),
            grad_beta,
        ],
        axis=0,
    )
    tables = [table] + [
        lax.ppermute(table, BOTH, along_last(hop)) for hop in range(1, devices // 8)
    ]
    last_gots, out_gots, tables = tied(last_gots, out_gots, tables)
    last_mine, last_sents = end_terms(last_kepts, last_gots)
    last_mine, last_sents, out_mine, out_gots, tables, g_mlp, down_parts = tied(
        last_mine, last_sents, out_mine, out_gots, tables, g_mlp, down_parts
    )
    last_gots = cross(last_sents, FIRST[::-1])
    table = added(tables)
    table_got = exchanged(table, 1)
    last_gots, table, table_got = tied(last_gots, table, table_got)
    last_parts = send_blocks(
        jnp.concatenate(
            [owner_blocks(last_mine, last_gots), owner_blocks(out_mine, out_gots)], axis=-1
        )
    )
    table = table + table_got
    for bit in (4, 2):
        table = table + exchanged(table, bit)
    g_down = added(down_parts)
    g_last = added(last_parts)
    index = lax.axis_index(BOTH)
    g_taps = jnp.concatenate([table[i * CONV : (i + 1) * CONV] for i in range(3)], axis=1)

    def own(rows_of, size):
        return lax.dynamic_slice_in_dim(rows_of, index * size, size, rows_of.ndim - 1)

    line = 3 * CONV

    def from_order(grad):
        blocks = grad.reshape(share, 2, 2, 2, devices // 8, -1)
        return blocks.transpose(0, 4, 3, 2, 1, 5).reshape(share, hidden_size)

    return (
        output,
        grad_tokens,
        own(table[line], share),
        g_last[:, :model],
        g_last[:, model : 2 * model],
        g_last[:, 2 * model : chan],
        own(g_taps, wide),
        own(table[line + 3 :], share).T,
        g_last[:, chan : chan + model],
        own(table[line + 2], own_gain),
        g_last[:, heads_wide:],
        own(table[line + 1], share),
        from_order(g_mlp[:, :hidden_size]),
        from_order(g_mlp[:, hidden_size:]),
        g_down,
    )


def solution(mesh):
    rows = P(BOTH, None)
    flat = P(BOTH)
    cols = P(None, BOTH)
    return jax.shard_map(
        local,
        mesh=mesh,
        in_specs=(
            rows, flat, rows, rows, rows, cols, rows, rows, flat, rows, flat, rows, rows, rows,
            P(), rows,
        ),
        out_specs=(
            rows, rows, flat, rows, rows, rows, cols, rows, rows, flat, rows, flat, rows, rows,
            rows,
        ),
        check_vma=False,
    )
```

```python
import jax
import jax.numpy as jnp
from jax import lax
from jax.experimental import pallas as pl
from jax.experimental.pallas import tpu as pltpu
from jax.sharding import Mesh, PartitionSpec as P

CONV = 4
RIM = 8
TAIL = 16
LANES = 128
BASE = 16
LAST = "z"
SEQ, FSDP = (LAST, "x"), ("y", "c")
BOTH = SEQ + FSDP
f32 = jnp.float32
bf16 = jnp.bfloat16
highest = lax.Precision.HIGHEST
NN = (((1,), (0,)), ((), ()))
NT = (((1,), (1,)), ((), ()))
TN = (((0,), (0,)), ((), ()))


class Parts:
    def __init__(self, value, passes=3):
        value = value.astype(f32)
        self.high = value.astype(bf16)
        self.low = (value - self.high.astype(f32)).astype(bf16) if passes == 3 else None


def mm(a, b, dims=NN, passes=3):
    a = a if isinstance(a, Parts) else Parts(a, passes)
    b = b if isinstance(b, Parts) else Parts(b, passes)
    if passes == 1:
        return lax.dot_general(a.high, b.high, dims, preferred_element_type=f32)
    left = jnp.concatenate([a.high, a.low, a.high], axis=dims[0][0][0])
    right = jnp.concatenate([b.high, b.high, b.low], axis=dims[0][1][0])
    return lax.dot_general(left, right, dims, preferred_element_type=f32)


def sigmoid(v):
    return 1.0 / (1.0 + jnp.exp(-v))


def iotas(rows):
    return (
        lax.broadcasted_iota(jnp.int32, (rows, rows), 0),
        lax.broadcasted_iota(jnp.int32, (rows, rows), 1),
    )


def unit_lower_inverses(lowers, rows, cols, passes):
    size = lowers[0].shape[0]
    same = (rows // BASE) == (cols // BASE)
    powers = [jnp.where(same, -lower, 0.0) for lower in lowers]
    inverses = [jnp.where(rows == cols, 1.0, power) for power in powers]
    covered = 2
    while covered < BASE:
        parts = [Parts(power, passes) for power in powers]
        powers = [mm(part, part, NN, passes) for part in parts]
        inverses = [a + mm(a, b, NN, passes) for a, b in zip(inverses, powers)]
        covered *= 2
    block = BASE
    while block < size:
        joined = ((rows // (2 * block)) == (cols // (2 * block))) & (
            (rows // block) != (cols // block)
        )
        parts = [Parts(inverse, passes) for inverse in inverses]
        inner = [
            mm(part, jnp.where(joined, lower, 0.0), NN, passes)
            for part, lower in zip(parts, lowers)
        ]
        inverses = [
            inverse - mm(off, part, NN, passes)
            for inverse, off, part in zip(inverses, inner, parts)
        ]
        block *= 2
    return inverses


def head_column(table, head):
    lanes = lax.broadcasted_iota(jnp.int32, table.shape, 1)
    first = LANES - pl.num_programs(0) * PER_STEP
    return jnp.sum(jnp.where(lanes == first + head, table, 0.0), axis=1, keepdims=True)


def load_extended(ref, scratch, rows):
    scratch[0:RIM, :] = ref[rows : rows + RIM, :].astype(f32)
    scratch[RIM : RIM + rows, :] = ref[0:rows, :].astype(f32)


def convolve(scratch, taps, rows):
    total = taps[CONV - 1 : CONV, :] * scratch[RIM : RIM + rows, :]
    for j in range(CONV - 1):
        first = RIM - (CONV - 1) + j
        total = total + taps[j : j + 1, :] * scratch[first : first + rows, :]
    return total


FRONT_PASSES = 3
PASS_PASSES = 3
BACK_PASSES = 1
PER_STEP = 2


def lanes_of(i):
    return slice(i * LANES, (i + 1) * LANES)


def front_kernel(
    pq, pk, pv, tq, tk, tv, beta_logit, q_out, k_out, v_out, t_out, pair_out, scratch
):
    rows = q_out.shape[0]
    active = []
    for ref, taps in ((pq, tq), (pk, tk), (pv, tv)):
        load_extended(ref, scratch, rows)
        c = convolve(scratch, taps, rows)
        active.append(c * sigmoid(c))
    logits = beta_logit[...]
    ri, ci = iotas(rows)
    lowers, keys, values, betas = [], [], [], []
    for i in range(PER_STEP):
        head = pl.program_id(0) * PER_STEP + i
        a, b, v = (part[:, lanes_of(i)] for part in active)
        q_out[:, lanes_of(i)] = a * lax.rsqrt(jnp.sum(a * a, axis=1, keepdims=True) + 1e-06)
        k = b * lax.rsqrt(jnp.sum(b * b, axis=1, keepdims=True) + 1e-06)
        k_out[:, lanes_of(i)] = k
        v_out[:, lanes_of(i)] = v
        beta = sigmoid(head_column(logits, head))
        part = Parts(k, FRONT_PASSES)
        lowers.append(jnp.where(ri > ci, beta * mm(part, part, NT, FRONT_PASSES), 0.0))
        keys.append(part)
        values.append(beta * v)
        betas.append(beta * k)
    inverses = unit_lower_inverses(lowers, ri, ci, FRONT_PASSES)
    for i in range(PER_STEP):
        t_out[i] = inverses[i]
        both = mm(
            inverses[i], jnp.concatenate([betas[i], values[i]], axis=1), NN, FRONT_PASSES
        )
        rs, cs = iotas(LANES)
        made = mm(both, keys[i], TN, FRONT_PASSES)
        pair_out[i, :LANES] = (jnp.where(rs == cs, 1.0, 0.0) - made[:LANES]).astype(bf16)
        pair_out[i, LANES:] = made[LANES:].astype(bf16)


def by_hop(place_ref, refs):
    count = len(refs)
    hop = lax.rem(place_ref[0] - pl.program_id(0) + count, count)
    value = refs[0][...]
    for h in range(1, count):
        value = jnp.where(hop == h, refs[h][...], value)
    return value[0]


def pass_kernel(
    place_ref, q_ref, k_ref, v_ref, t_ref, beta_logit, gate_ref, gain_ref, *rest
):
    state_refs, (branch_out, o_out, d_out, p_out) = rest[:-4], rest[-4:]
    states = by_hop(place_ref, state_refs)
    rows = q_ref.shape[0]
    logits = beta_logit[...]
    ri, ci = iotas(rows)
    for i in range(PER_STEP):
        head = pl.program_id(0) * PER_STEP + i
        cols = lanes_of(i)
        q, k, s = (Parts(m, PASS_PASSES) for m in (q_ref[:, cols], k_ref[:, cols], states[i]))
        beta = sigmoid(head_column(logits, head))
        p = jnp.where(ri >= ci, mm(q, k, NT, PASS_PASSES), 0.0)
        p_out[i] = p
        missing = v_ref[:, cols] - mm(k, s, NT, PASS_PASSES)
        d = mm(t_ref[i], beta * missing, NN, PASS_PASSES)
        d_out[:, cols] = d
        o = mm(q, s, NT, PASS_PASSES) + mm(p, d, NN, PASS_PASSES)
        o_out[:, cols] = o
        n = o * lax.rsqrt(jnp.mean(o * o, axis=1, keepdims=True) + 1e-05)
        g = gate_ref[:, cols]
        branch_out[:, cols] = (n * gain_ref[...] * (g * sigmoid(g))).astype(bf16)


def back_one_kernel(
    db_ref, o_ref, gate_ref, gain_ref, p_ref, t_ref, q_ref, k_ref, beta_logit,
    dgate_out, donorm_out, do_out, dr_out, g_out,
):
    gain = gain_ref[...]
    logits = beta_logit[...]
    for i in range(PER_STEP):
        head = pl.program_id(0) * PER_STEP + i
        cols = lanes_of(i)
        o = o_ref[:, cols]
        g = gate_ref[:, cols]
        db = db_ref[:, cols]
        beta = sigmoid(head_column(logits, head))
        scale = lax.rsqrt(jnp.mean(o * o, axis=1, keepdims=True) + 1e-05)
        n = o * scale
        sig = sigmoid(g)
        z = g * sig
        dgate_out[:, cols] = (db * n * gain * (sig * (1.0 + g * (1.0 - sig)))).astype(bf16)
        dy = db * z
        donorm_out[i] = jnp.sum(dy * n, axis=0, keepdims=True)
        dyg = dy * gain
        do = scale * dyg - o * (scale * scale * scale) * jnp.mean(dyg * o, axis=1, keepdims=True)
        do_out[:, cols] = do
        do = Parts(do, BACK_PASSES)
        dd = mm(p_ref[i], do, TN, BACK_PASSES)
        dr = mm(t_ref[i], dd, TN, BACK_PASSES)
        dr_out[:, cols] = dr
        g_out[i] = (
            mm(do, q_ref[:, cols], TN, BACK_PASSES)
            - mm(beta * dr, k_ref[:, cols], TN, BACK_PASSES)
        ).astype(bf16)


def back_two_kernel(
    place_ref, t_ref, p_ref, q_ref, k_ref, v_ref, beta_logit, do_ref, dr_ref, d_ref,
    pq, pk, pv, tq, tk, tv, *rest,
):
    count = (len(rest) - 15) // 2
    grads_in = by_hop(place_ref, rest[:count])
    states_in = by_hop(place_ref, rest[count : 2 * count])
    dq_out, dk_out, dv_out, eq_out, ek_out, ev_out, rq_out, rk_out, rv_out = rest[-15:-6]
    cq_out, ck_out, cv_out, dbeta_out, scratch, spread = rest[-6:]
    step = pl.program_id(0)
    rows = q_ref.shape[0]
    logits = beta_logit[...]
    ri, ci = iotas(rows)
    passes = BACK_PASSES

    @pl.when(step == 0)
    def _():
        dbeta_out[...] = jnp.zeros_like(dbeta_out)

    d_units = ([], [], [])
    for i in range(PER_STEP):
        head = step * PER_STEP + i
        cols = lanes_of(i)
        ds, s, q, k, do, d = (
            Parts(m, passes)
            for m in (
                grads_in[i], states_in[i], q_ref[:, cols], k_ref[:, cols], do_ref[:, cols],
                d_ref[:, cols],
            )
        )
        beta = sigmoid(head_column(logits, head))
        dr = dr_ref[:, cols] + mm(t_ref[i], mm(k, ds, NT, passes), TN, passes)
        missing = v_ref[:, cols] - mm(k, s, NT, passes)
        dp = Parts(jnp.where(ri >= ci, mm(do, d, NT, passes), 0.0), passes)
        bdr = beta * dr
        dq = mm(do, s, NN, passes) + mm(dp, k, NN, passes)
        dk = mm(dp, q, TN, passes) + mm(d, ds, NN, passes) - mm(bdr, s, NN, passes)
        da = jnp.where(ri > ci, -mm(dr, d, NT, passes), 0.0)
        dbeta = jnp.sum(dr * missing, axis=1, keepdims=True) + jnp.sum(
            da * mm(k, k, NT, passes), axis=1, keepdims=True
        )
        dm = Parts(beta * da, passes)
        dk = dk + mm(dm, k, NN, passes) + mm(dm, k, TN, passes)
        dlogit = dbeta * beta * (1.0 - beta)
        lanes = lax.broadcasted_iota(jnp.int32, dbeta_out.shape, 1)
        column = LANES - pl.num_programs(0) * PER_STEP + head
        dbeta_out[...] = jnp.where(lanes == column, dlogit, dbeta_out[...])
        for grads, grad in zip(d_units, (dq, dk, bdr)):
            grads.append(grad)

    width = q_ref.shape[1]
    spread[0:RIM, :] = jnp.zeros((RIM, width), f32)
    spread[RIM + rows : RIM + rows + RIM, :] = jnp.zeros((RIM, width), f32)
    sets = (
        (pq, tq, d_units[0], q_ref, dq_out, eq_out, rq_out, cq_out),
        (pk, tk, d_units[1], k_ref, dk_out, ek_out, rk_out, ck_out),
        (pv, tv, d_units[2], None, dv_out, ev_out, rv_out, cv_out),
    )
    for proj, taps, grads, units, out, tail_out, rim_out, tap_out in sets:
        load_extended(proj, scratch, rows)
        c = convolve(scratch, taps, rows)
        sig = sigmoid(c)
        if units is not None:
            act = c * sig
            for i in range(PER_STEP):
                cols = lanes_of(i)
                part, unit = act[:, cols], units[:, cols]
                inv = lax.rsqrt(jnp.sum(part * part, axis=1, keepdims=True) + 1e-06)
                grads[i] = (
                    grads[i] - unit * jnp.sum(unit * grads[i], axis=1, keepdims=True)
                ) * inv
        dc = jnp.concatenate(grads, axis=1) * (sig * (1.0 + c * (1.0 - sig)))
        spread[RIM : RIM + rows, :] = dc
        total = jnp.zeros((rows, width), f32)
        rim = jnp.zeros((RIM, width), f32)
        for j in range(CONV):
            lag = CONV - 1 - j
            tap = taps[j : j + 1, :]
            total = total + tap * spread[RIM + lag : RIM + lag + rows, :]
            rim = rim + tap * spread[lag : lag + RIM, :]
            first = RIM - lag
            tap_out[j : j + 1, :] = jnp.sum(
                dc * scratch[first : first + rows, :], axis=0, keepdims=True
            )
        out[...] = total.astype(bf16)
        tail_out[...] = total[rows - TAIL :]
        rim_out[...] = rim


LIGHT = pl.CostEstimate(flops=1, bytes_accessed=1, transcendentals=0)


def params():
    return pltpu.CompilerParams(
        dimension_semantics=("arbitrary",), vmem_limit_bytes=56 * 1024 * 1024
    )


def column_block(rows, heads, part):
    steps = heads // PER_STEP
    return pl.BlockSpec((rows, PER_STEP * LANES), lambda h, part=part: (0, part * steps + h))


def whole(shape):
    return pl.BlockSpec(shape, lambda h: (0,) * len(shape))


def scalar():
    return pl.BlockSpec(memory_space=pltpu.SMEM)


def per_head(shape):
    return pl.BlockSpec((PER_STEP,) + shape, lambda h: (h, 0, 0))


def pack_kernel(
    wq, wk, wv, wg, beta_ref, conv_ref, gain_ref, onorm_ref, mlp_ref, out, scratch
):
    model = wq.shape[1]
    for i, ref in enumerate((wq, wk, wv, wg)):
        out[:, i * model : (i + 1) * model] = ref[...]
    scratch[...] = jnp.zeros_like(scratch)
    taps, wide = conv_ref.shape
    scratch[0:taps, 0:wide] = conv_ref[...].astype(f32)
    for i, ref in enumerate((gain_ref, mlp_ref, onorm_ref)):
        scratch[taps + i : taps + i + 1, 0 : ref.shape[1]] = ref[...].astype(f32)
    heads = beta_ref.shape[1]
    scratch[:, LANES - heads :] = beta_ref[...].astype(f32)
    out[:, 4 * model :] = scratch[...].astype(bf16)


def run_pack(wq, wk, wv, wg, w_beta, conv, gain, onorm, mlp_gain):
    share, model = wq.shape
    return pl.pallas_call(
        pack_kernel,
        out_shape=jax.ShapeDtypeStruct((share, 4 * model + LANES), bf16),
        scratch_shapes=[pltpu.VMEM((share, LANES), f32)],
        name="pack",
    )(
        wq, wk, wv, wg, w_beta, conv, gain.reshape(1, -1), onorm.reshape(1, -1),
        mlp_gain.reshape(1, -1),
    )


def run_front(proj, taps, beta_logit, rows, heads):
    width = LANES
    p_spec = [column_block(rows + RIM, heads, i) for i in range(3)]
    t_spec = [column_block(CONV, heads, i) for i in range(3)]
    row_spec = column_block(rows, heads, 0)
    return pl.pallas_call(
        front_kernel,
        grid=(heads // PER_STEP,),
        in_specs=p_spec + t_spec + [whole((rows, LANES))],
        out_specs=[row_spec] * 3
        + [per_head((rows, rows)), per_head((2 * width, width))],
        out_shape=[jax.ShapeDtypeStruct((rows, heads * width), f32)] * 3
        + [
            jax.ShapeDtypeStruct((heads, rows, rows), f32),
            jax.ShapeDtypeStruct((heads, 2 * width, width), bf16),
        ],
        scratch_shapes=[pltpu.VMEM((rows + RIM, PER_STEP * width), f32)],
        compiler_params=params(),
        cost_estimate=LIGHT,
        name="front",
    )(proj, proj, proj, taps, taps, taps, beta_logit)


def run_pass(place, q, k, v, t, beta_logit, states, gate, gain, rows, heads):
    width = LANES
    row_spec = column_block(rows, heads, 0)
    square = per_head((rows, rows))
    return pl.pallas_call(
        pass_kernel,
        grid=(heads // PER_STEP,),
        in_specs=[
            scalar(), row_spec, row_spec, row_spec, square, whole((rows, LANES)), row_spec,
            whole((1, width)),
        ]
        + [whole(state.shape) for state in states],
        out_specs=[row_spec, row_spec, row_spec, square],
        out_shape=[
            jax.ShapeDtypeStruct((rows, heads * width), bf16),
            jax.ShapeDtypeStruct((rows, heads * width), f32),
            jax.ShapeDtypeStruct((rows, heads * width), f32),
            jax.ShapeDtypeStruct((heads, rows, rows), f32),
        ],
        compiler_params=params(),
        cost_estimate=LIGHT,
        name="chunk_pass",
    )(place, q, k, v, t, beta_logit, gate, gain, *states)


def run_back_one(d_branch, o, gate, gain, p, t, q, k, beta_logit, rows, heads):
    width = LANES
    row_spec = column_block(rows, heads, 0)
    square = per_head((rows, rows))
    return pl.pallas_call(
        back_one_kernel,
        grid=(heads // PER_STEP,),
        in_specs=[
            row_spec, row_spec, row_spec, whole((1, width)), square, square, row_spec, row_spec,
            whole((rows, LANES)),
        ],
        out_specs=[row_spec, per_head((1, width)), row_spec, row_spec, per_head((width, width))],
        out_shape=[
            jax.ShapeDtypeStruct((rows, heads * width), bf16),
            jax.ShapeDtypeStruct((heads, 1, width), f32),
            jax.ShapeDtypeStruct((rows, heads * width), f32),
            jax.ShapeDtypeStruct((rows, heads * width), f32),
            jax.ShapeDtypeStruct((heads, width, width), bf16),
        ],
        compiler_params=params(),
        cost_estimate=LIGHT,
        name="back_one",
    )(d_branch, o, gate, gain, p, t, q, k, beta_logit)


def run_back_two(
    place, grads, states, t, p, q, k, v, beta_logit, do, dr, d, proj, taps, rows, heads
):
    width = LANES
    row_spec = column_block(rows, heads, 0)
    square = per_head((rows, rows))
    p_spec = [column_block(rows + RIM, heads, i) for i in range(3)]
    t_spec = [column_block(CONV, heads, i) for i in range(3)]
    return pl.pallas_call(
        back_two_kernel,
        grid=(heads // PER_STEP,),
        in_specs=[
            scalar(), square, square, row_spec, row_spec, row_spec, whole((rows, LANES)),
            row_spec, row_spec, row_spec,
        ]
        + p_spec
        + t_spec
        + [whole(part.shape) for part in grads]
        + [whole(part.shape) for part in states],
        out_specs=[row_spec] * 3
        + [column_block(TAIL, heads, 0)] * 3
        + [column_block(RIM, heads, 0)] * 3
        + [column_block(CONV, heads, 0)] * 3
        + [whole((rows, LANES))],
        out_shape=[jax.ShapeDtypeStruct((rows, heads * width), bf16)] * 3
        + [jax.ShapeDtypeStruct((TAIL, heads * width), f32)] * 3
        + [jax.ShapeDtypeStruct((RIM, heads * width), f32)] * 3
        + [jax.ShapeDtypeStruct((CONV, heads * width), f32)] * 3
        + [jax.ShapeDtypeStruct((rows, LANES), f32)],
        scratch_shapes=[
            pltpu.VMEM((rows + RIM, PER_STEP * width), f32),
            pltpu.VMEM((rows + 2 * RIM, PER_STEP * width), f32),
        ],
        compiler_params=params(),
        cost_estimate=LIGHT,
        name="back_two",
    )(
        place, t, p, q, k, v, beta_logit, do, dr, d, proj, proj, proj, taps, taps, taps,
        *grads, *states,
    )


def prefix_kernel(place_ref, *rest):
    prefix_out, linear_out, group_out, ordered_ref = rest[-4:]
    parts = rest[:-4]
    count = len(parts)
    for hop in range(count):
        ordered_ref[lax.rem(place_ref[0] - hop + count, count)] = parts[hop][0].astype(f32)
    for m in range(ordered_ref.shape[1]):
        joined = ordered_ref[0, m]
        prefix_out[0, m] = joined
        linear_out[0, m] = joined[:LANES]
        for i in range(1, count):
            linear = ordered_ref[i, m, :LANES]
            linear_out[i, m] = linear
            joined = mm(joined, linear)
            joined = jnp.concatenate(
                [joined[:LANES], joined[LANES:] + ordered_ref[i, m, LANES:]], axis=0
            )
            prefix_out[i, m] = joined
        group_out[m] = joined.astype(bf16)


def entry_kernel(before_ref, prefix, *rest):
    totals, out = rest[:-1], rest[-1]
    for m in range(prefix.shape[1]):
        state = jnp.zeros((LANES, LANES), f32)
        for hop in range(len(totals), 0, -1):
            total = totals[hop - 1]
            state = mm(state, total[m, :LANES]) + total[m, LANES:].astype(f32)
            state = jnp.where(hop <= before_ref[0], state, 0.0)
        out[0, m] = state.astype(bf16)
        for i in range(1, prefix.shape[0]):
            entry = mm(state, prefix[i - 1, m, :LANES]) + prefix[i - 1, m, LANES:]
            out[i, m] = entry.astype(bf16)


def suffix_kernel(place_ref, linears, prefix, *rest):
    inner_out, group_out, ordered_ref = rest[-3:]
    parts = rest[:-3]
    count = len(parts)
    for hop in range(count):
        ordered_ref[lax.rem(place_ref[0] - hop + count, count)] = parts[hop][0].astype(f32)
    for m in range(ordered_ref.shape[1]):
        grad = jnp.zeros((LANES, LANES), f32)
        for i in range(count - 1, -1, -1):
            inner_out[i, m] = grad
            grad = mm(grad, linears[i, m], NT) + ordered_ref[i, m]
        group_out[m, :LANES] = grad.astype(bf16)
        group_out[m, LANES:] = prefix[count - 1, m, :LANES].astype(bf16)


def leave_kernel(after_ref, inner, linears, *rest):
    out = rest[-1]
    reach = len(rest) - 1
    count = inner.shape[0]
    for m in range(inner.shape[1]):
        grad = jnp.zeros((LANES, LANES), f32)
        for hop in range(reach, 0, -1):
            total = rest[hop - 1]
            grad = mm(grad, total[m, LANES:], NT) + total[m, :LANES].astype(f32)
            grad = jnp.where(hop <= after_ref[0], grad, 0.0)
        for i in range(count - 1, -1, -1):
            out[i, m] = (inner[i, m] + grad).astype(bf16)
            if i:
                grad = mm(grad, linears[i, m], NT)


def run_small(kernel, number, arrays, shapes, scratch, name):
    return pl.pallas_call(
        kernel,
        in_specs=[scalar()] + [pl.BlockSpec(memory_space=pltpu.VMEM)] * len(arrays),
        out_specs=[pl.BlockSpec(memory_space=pltpu.VMEM)] * len(shapes),
        out_shape=[jax.ShapeDtypeStruct(shape, kind) for shape, kind in shapes],
        scratch_shapes=scratch,
        compiler_params=pltpu.CompilerParams(vmem_limit_bytes=56 * 1024 * 1024),
        cost_estimate=LIGHT,
        name=name,
    )(number, *arrays)


def swapped(parts, axis):
    count = lax.axis_size(axis)
    place = lax.axis_index(axis)
    result = [lax.dynamic_slice_in_dim(parts, place, 1, 0)]
    for hop in range(1, count):
        sent = lax.dynamic_slice_in_dim(parts, lax.rem(place + hop, count), 1, 0)
        result.append(lax.ppermute(sent, axis, [(i, (i + hop) % count) for i in range(count)]))
    return result


def shift_groups(array, by):
    size = lax.axis_size(SEQ)
    return lax.ppermute(
        array, SEQ, [(i, i + by) for i in range(size) if 0 <= i + by < size]
    )


def joined_chunks(pair, place):
    count = lax.axis_size(FSDP)
    heads, tall, width = pair.shape
    mine = heads // count
    parts = swapped(pair.reshape(count, mine, tall, width), FSDP)
    prefix, linears, group = run_small(
        prefix_kernel, place, parts,
        [
            ((count, mine, tall, width), f32), ((count, mine, width, width), f32),
            ((mine, tall, width), bf16),
        ],
        [pltpu.VMEM((count, mine, tall, width), f32)], "prefix",
    )
    return prefix, linears, group


def states_entering(prefix, group, before, reach, others):
    count, mine, tall, width = prefix.shape
    earlier = [shift_groups(group, hop) for hop in range(1, reach + 1)]
    earlier, others = tied(earlier, others)
    (entries,) = run_small(
        entry_kernel, before, [prefix] + list(earlier), [((count, mine, width, width), bf16)], [],
        "entry",
    )
    return swapped(entries, FSDP), others


def state_grads_leaving(
    grads, linears, prefix, place, after, reach, sent, send, wait, meanwhile
):
    count = lax.axis_size(FSDP)
    heads, width = grads.shape[0], grads.shape[1]
    mine = heads // count
    parts = swapped(grads.reshape(count, mine, width, width), FSDP)
    parts, sent = tied(parts, sent)
    got = send(sent)
    inner, group = run_small(
        suffix_kernel, place, [linears, prefix] + list(parts),
        [((count, mine, width, width), f32), ((mine, 2 * width, width), bf16)],
        [pltpu.VMEM((count, mine, width, width), f32)], "suffix",
    )
    inner, group, wait = tied(inner, group, wait)
    beyond = [shift_groups(group, -hop) for hop in range(1, reach + 1)]
    beyond, made = tied(beyond, meanwhile(wait))
    (entries,) = run_small(
        leave_kernel, after, [inner, linears] + list(beyond),
        [((count, mine, width, width), bf16)], [], "leave",
    )
    return swapped(entries, FSDP), got, made


def rms(values):
    return lax.rsqrt(jnp.mean(values * values, axis=-1, keepdims=True) + 1e-05)


def rms_back(values, scale, gain, dy):
    dyg = dy * gain
    grad = scale * dyg - values * (scale * scale * scale) * jnp.mean(
        dyg * values, axis=-1, keepdims=True
    )
    return grad, jnp.sum(dy * values * scale, axis=0)


def dot(a, b):
    return jnp.dot(a, b, preferred_element_type=f32)


def dot_t(a, b):
    return lax.dot_general(a, b, NT, preferred_element_type=f32)


def t_dot(a, b):
    return lax.dot_general(a, b, TN, preferred_element_type=f32)


def flips(bit, count):
    return [(i, i ^ bit) for i in range(count)]


def exchanged(array, bit):
    return lax.ppermute(array, BOTH, flips(bit, lax.axis_size(BOTH)))


def place_bits():
    index = lax.axis_index(BOTH)
    return {bit: lax.rem(index // bit, 2) for bit in (1, 2, 4)}


def tied(*values):
    return lax.optimization_barrier(values)


def owner_order(array, axis):
    count = lax.axis_size(BOTH)
    shape = array.shape
    blocks = array.reshape(shape[:axis] + (count // 8, 2, 2, 2, -1) + shape[axis + 1 :])
    order = tuple(range(axis)) + tuple(axis + i for i in (3, 2, 1, 0, 4))
    return blocks.transpose(order + tuple(range(axis + 5, blocks.ndim))).reshape(shape)


def owner_matrix(size):
    source = owner_order(jnp.arange(size, dtype=jnp.int32), 0)
    side = place_bits()[1]
    source = jnp.concatenate([half(source, 1 - side), half(source, side)])
    return (jnp.arange(size, dtype=jnp.int32)[:, None] == source[None, :]).astype(bf16)


def half(array, which, axis=0):
    size = array.shape[axis] // 2
    return lax.dynamic_slice_in_dim(array, which * size, size, axis)


FIRST = (2, 4)


def pick(array, axis, which):
    return lax.dynamic_index_in_dim(array, which, axis, False)


def columns(array, i):
    wide = array.shape[-1] // 2
    return array[..., i * wide : (i + 1) * wide]


def begin_terms(away, right):
    return [exchanged(t_dot(away, part).astype(bf16), 1) for part in two_of(right)]


def middle_terms(homes, rights, gots):
    bits = place_bits()
    totals, sents = [], []
    for i, (home, right, got, first) in enumerate(zip(homes, rights, gots, FIRST)):
        total = (t_dot(home, right) + got.astype(f32)).astype(bf16)
        total = total.reshape((2, 2, -1) + total.shape[1:])
        totals.append(total)
        sents.append(pick(total, i, 1 - bits[first]).reshape(-1, right.shape[1]))
    return totals, sents


def two_of(array):
    return [columns(array, 0), columns(array, 1)]


def cross(sents, bits):
    return [exchanged(sent, bit) for sent, bit in zip(sents, bits)]


def end_terms(totals, gots):
    bits = place_bits()
    mine, sents = [], []
    for i, (total, got, first) in enumerate(zip(totals, gots, FIRST)):
        kept = pick(total, i, bits[first]).reshape(got.shape)
        kept = (kept.astype(f32) + got.astype(f32)).astype(bf16)
        mine.append(half(kept, bits[6 - first]))
        sents.append(half(kept, 1 - bits[6 - first]))
    return mine, sents


def owner_blocks(mine, gots):
    length = lax.axis_size(BOTH) // 8
    parts = [(m.astype(f32) + g.astype(f32)).astype(bf16) for m, g in zip(mine, gots)]
    return jnp.concatenate([p.reshape(length, -1, p.shape[-1]) for p in parts], axis=-1)


def stacked(blocks):
    length = len(blocks)
    place = lax.axis_index(BOTH) // 8
    back = jnp.stack(blocks[::-1] + blocks[::-1])
    return lax.dynamic_slice_in_dim(back, length - 1 - place, length, 0)


def merged(blocks, got, bit):
    mine = place_bits()[bit] == 0
    return jnp.stack([jnp.where(mine, blocks, got), jnp.where(mine, got, blocks)])


def along_last(by):
    count = lax.axis_size(BOTH)
    return [(i, (i + 8 * by) % count) for i in range(count)]


def send_blocks(blocks, hops=None):
    length = blocks.shape[0]
    place = lax.axis_index(BOTH) // 8

    def block(i):
        return lax.dynamic_index_in_dim(blocks, lax.rem(i, length), 0, False)

    if hops is None:
        return [block(place)] + send_blocks(blocks, range(1, length))
    return [lax.ppermute(block(place + hop), BOTH, along_last(hop)) for hop in hops]


def last_sum(blocks):
    flat = blocks.reshape(-1, blocks.shape[-1])
    return lax.psum_scatter(flat, LAST, scatter_dimension=0, tiled=True)


def added(parts):
    total = parts[0].astype(f32)
    for part in parts[1:]:
        total = total + part.astype(f32)
    return total


def local(
    tokens, attn_gain, w_query, w_key, w_value, conv_weight, w_beta, w_gate_out, onorm_gain,
    w_out, mlp_gain, w_mlp_gate, w_mlp_up, w_down, seq_lengths, cotangent,
):
    rows, model = tokens.shape
    heads = w_beta.shape[1]
    hidden_size = w_mlp_gate.shape[1]
    devices = lax.axis_size(BOTH)
    share = model // devices
    groups = lax.axis_size(SEQ)
    reach = groups // 2 - 1
    width = model // heads
    chan = 3 * model
    wide = chan // devices
    own_gain = onorm_gain.shape[0]
    pack_one = run_pack(
        w_query, w_key, w_value, w_gate_out, w_beta, conv_weight, attn_gain, onorm_gain, mlp_gain
    )
    full_one = lax.all_gather(pack_one, BOTH, axis=0, tiled=True)
    seq_lengths, w_mlp_gate, w_mlp_up, w_out, w_down, tokens, pack_one = (
        lax.optimization_barrier(
            (seq_lengths, w_mlp_gate, w_mlp_up, w_out, w_down, tokens, pack_one)
        )
    )
    down = [w_down] + [
        lax.ppermute(w_down, BOTH, along_last(hop)) for hop in range(1, devices // 8)
    ]
    down = stacked(down)
    halves = [columns(down, i) for i in range(2)]
    gots = cross(halves, FIRST[::-1])
    halves = [merged(h, g, bit) for h, g, bit in zip(halves, gots, FIRST[::-1])]
    full_one, halves = tied(full_one, halves)
    full_two = lax.all_gather(
        jnp.concatenate([w_out, owner_order(w_mlp_gate, 1), owner_order(w_mlp_up, 1)], axis=1),
        BOTH,
        axis=0,
        tiled=True,
    )
    to_order = owner_matrix(model)

    group_rows = rows * lax.axis_size(FSDP)
    first = lax.axis_index(BOTH) * rows
    group_first = lax.axis_index(SEQ) * group_rows
    ends = jnp.cumsum(seq_lengths)
    starts = ends - seq_lengths
    begin = jnp.max(jnp.where(starts <= first, starts, 0))
    end = jnp.min(jnp.where(ends > first, ends, rows * devices))
    opens = first == begin
    before = ((group_first - begin) // group_rows).reshape(1)
    beyond = ((end - group_first) // group_rows - 1).reshape(1)
    place = lax.axis_index(FSDP).reshape(1)

    heads_wide = chan + model
    w_heads = full_one[:, :heads_wide]
    full_misc = full_one[:, heads_wide:]
    w_out_full = full_two[:, :model]
    w_both = full_two[:, model:]
    misc = full_misc.reshape(devices, share, LANES)
    gain_one = misc[:, CONV, :share].reshape(model).astype(f32)
    gain_two = misc[:, CONV + 1, :share].reshape(model).astype(f32)
    onorm = misc[:, CONV + 2, :own_gain].reshape(1, width).astype(f32)
    taps = misc[:, :CONV, :wide].swapaxes(0, 1).reshape(CONV, chan).astype(f32)
    beta_cols = jnp.where(
        lax.broadcasted_iota(jnp.int32, full_misc.shape, 1) >= LANES - heads, full_misc, 0
    )

    rim_tokens = lax.ppermute(
        tokens[rows - RIM :], BOTH, [(i, i + 1) for i in range(devices - 1)]
    )
    rim_tokens = jnp.where(opens, jnp.zeros_like(rim_tokens), rim_tokens)
    x_all = jnp.concatenate([tokens, rim_tokens], axis=0).astype(f32)
    scale_all = rms(x_all)
    normed_all = (x_all * scale_all * gain_one).astype(bf16)
    projected = dot(normed_all, w_heads[:, :chan]).astype(bf16)
    normed = normed_all[:rows]
    x = tokens.astype(f32)
    scale_one = scale_all[:rows]
    beta_logit = dot(normed, full_misc)
    normed_order = dot(normed, to_order).astype(bf16)
    gots = cross(halves, FIRST)
    q, k, v, t, pair = run_front(projected, taps, beta_logit, rows, heads)
    pair, gots = tied(pair, gots)
    prefix, linears, group = joined_chunks(pair, place)
    halves = [merged(h, g, bit) for h, g, bit in zip(halves, gots, FIRST)]
    gate_logit = dot(normed, w_heads[:, chan:])
    group, halves, gate_logit = tied(group, halves, gate_logit)
    gots = cross(halves, (1, 1))
    states, gots = states_entering(prefix, group, before, reach, gots)
    halves = [merged(h, g, 1) for h, g in zip(halves, gots)]
    halves[1] = halves[1].swapaxes(1, 2)
    full_down = jnp.concatenate([h.reshape(hidden_size, -1) for h in halves], axis=1)
    states, full_down = tied(states, full_down)
    branch, o, d, p = run_pass(
        place, q, k, v, t, beta_logit, states, gate_logit, onorm, rows, heads
    )
    hidden = x + dot(branch, w_out_full)
    scale_two = rms(hidden)
    normed_two = (hidden * scale_two * gain_two).astype(bf16)
    both_rows = dot(normed_two, w_both)
    gate_rows, up_rows = both_rows[:, :hidden_size], both_rows[:, hidden_size:]
    sig = sigmoid(gate_rows)
    act = gate_rows * sig
    inner = (act * up_rows).astype(bf16)
    side = place_bits()[1]
    down_got = begin_terms(half(inner, 1 - side, 1), cotangent)
    d_inner = dot_t(cotangent, full_down)
    d_both = jnp.concatenate(
        [d_inner * up_rows * (sig * (1.0 + gate_rows * (1.0 - sig))), d_inner * act], axis=1
    ).astype(bf16)
    two_order = dot(normed_two, to_order).astype(bf16)
    both_got = begin_terms(two_order[:, : model // 2], d_both)
    down_home = half(inner, side, 1)
    down_totals, down_sents = middle_terms([down_home] * 2, two_of(cotangent), down_got)
    d_both, down_totals, down_sents = tied(d_both, down_totals, down_sents)
    down_gots = cross(down_sents, FIRST)
    d_normed_two = dot_t(d_both, w_both)
    d_normed_two, down_gots = tied(d_normed_two, down_gots)
    down_mine, down_sents = end_terms(down_totals, down_gots)
    d_norm, grad_gain_two = rms_back(hidden, scale_two, gain_two, d_normed_two)
    d_hidden = cotangent.astype(f32) + d_norm
    d_attn = d_hidden.astype(bf16)
    d_branch = dot_t(d_attn, w_out_full)
    branch_order = dot(branch, to_order).astype(bf16)
    out_got = exchanged(t_dot(branch_order[:, : model // 2], d_attn).astype(bf16), 1)
    d_branch, down_mine, down_sents = tied(d_branch, down_mine, down_sents)
    down_gots = cross(down_sents, FIRST[::-1])
    both_totals, both_sents = middle_terms(
        [two_order[:, model // 2 :]] * 2, two_of(d_both), both_got
    )
    d_branch, down_gots, both_totals, both_sents = tied(
        d_branch, down_gots, both_totals, both_sents
    )
    up_got = exchanged(both_sents[1], FIRST[1])

    d_gate_logit, d_onorm, d_o, d_r, state_grad = run_back_one(
        d_branch, o, gate_logit, onorm, p, t, q, k, beta_logit, rows, heads
    )
    state_grad, out_got = tied(state_grad, out_got)
    away, home = normed_order[:, : model // 2], normed_order[:, model // 2 :]
    gate_got = exchanged(t_dot(away, d_gate_logit).astype(bf16), 1)

    def meanwhile(held):
        gate_got, inner, d_attn = held
        totals, sents = middle_terms(
            [branch_order[:, model // 2 :], home], [d_attn, d_gate_logit], [out_got, gate_got]
        )
        return (
            owner_blocks(down_mine, down_gots),
            totals,
            sents,
            (hidden + dot(inner, full_down)).astype(bf16),
        )

    leaving, mlp_got, (down_blocks, gate_totals, gate_sents, output) = state_grads_leaving(
        state_grad, linears, prefix, place, beyond, reach, both_sents[0],
        lambda sent: exchanged(sent, FIRST[0]), (gate_got, inner, d_attn), meanwhile,
    )
    leaving, mlp_got, up_got = tied(leaving, mlp_got, up_got)
    both_mine, both_sents = end_terms(both_totals, [mlp_got, up_got])
    leaving, both_mine, both_sents, gate_sents, down_blocks = tied(
        leaving, both_mine, both_sents, gate_sents, down_blocks
    )
    both_gots = cross(both_sents, FIRST[::-1])
    gate_gots = cross(gate_sents, FIRST)
    g_down = last_sum(down_blocks)
    outs = run_back_two(
        place, leaving, states, t, p, q, k, v, beta_logit, d_o, d_r, d, projected, taps,
        rows, heads,
    )
    outs, both_gots = tied(outs, both_gots)
    mlp_blocks = owner_blocks(both_mine, both_gots)
    tails = jnp.concatenate(outs[3:6], axis=1)
    rims = jnp.concatenate(outs[6:9], axis=1)
    d_beta = outs[12].astype(bf16)
    rims = jnp.where(opens, jnp.zeros_like(rims), rims)
    rims = lax.ppermute(rims, BOTH, [(i + 1, i) for i in range(devices - 1)])
    tails = tails + jnp.pad(rims, ((TAIL - RIM, 0), (0, 0)))
    d_proj = lax.dynamic_update_slice_in_dim(
        jnp.concatenate(outs[0:3], axis=1), tails.astype(bf16), rows - TAIL, 0
    )
    d_proj, mlp_blocks = tied(d_proj, mlp_blocks)
    g_mlp = last_sum(mlp_blocks)
    last_got = begin_terms(away, d_proj)
    d_normed = (
        dot_t(d_proj, w_heads[:, :chan])
        + dot_t(d_gate_logit, w_heads[:, chan:])
        + dot_t(d_beta, beta_cols)
    )
    d_token_norm, grad_gain_one = rms_back(x, scale_one, gain_one, d_normed)
    grad_tokens = d_hidden + d_token_norm
    last_got, grad_tokens, grad_gain_one, gate_gots, g_down = tied(
        last_got, grad_tokens, grad_gain_one, gate_gots, g_down
    )
    last_totals, last_sents = middle_terms([home] * 2, two_of(d_proj), last_got)
    last_totals, last_sents, gate_gots, grad_gain_one, d_beta = tied(
        last_totals, last_sents, gate_gots, grad_gain_one, d_beta
    )
    last_gots = cross(last_sents, FIRST)
    gate_mine, gate_sents = end_terms(gate_totals, gate_gots)
    gate_gots = cross(gate_sents, FIRST[::-1])
    grad_beta = t_dot(d_beta, normed)[LANES - heads :]
    table = jnp.concatenate(
        list(outs[9:12])
        + [
            grad_gain_one.reshape(1, model),
            grad_gain_two.reshape(1, model),
            jnp.pad(jnp.sum(d_onorm, axis=(0, 1)).reshape(1, width), ((0, 0), (0, model - width))),
            grad_beta,
        ],
        axis=0,
    )
    bit = 8
    while bit < devices:
        table = table + exchanged(table, bit)
        bit *= 2
    last_gots, gate_gots, g_mlp, table = tied(last_gots, gate_gots, g_mlp, table)
    last_mine, last_sents = end_terms(last_totals, last_gots)
    last_mine, last_sents, gate_gots, table = tied(last_mine, last_sents, gate_gots, table)
    last_gots = cross(last_sents, FIRST[::-1])
    table = table + exchanged(table, 1)
    gate_blocks = owner_blocks(gate_mine, gate_gots)
    last_gots, gate_blocks, table = tied(last_gots, gate_blocks, table)
    last_blocks = jnp.concatenate([owner_blocks(last_mine, last_gots), gate_blocks], axis=-1)
    last_blocks, table, g_mlp = tied(last_blocks, table, g_mlp)
    g_last = last_sum(last_blocks).astype(f32)
    for bit in (4, 2):
        table = table + exchanged(table, bit)
    index = lax.axis_index(BOTH)
    g_early = g_last[:, chan:]
    g_mlp, g_down = g_mlp.astype(f32), g_down.astype(f32)
    g_taps = jnp.concatenate([table[i * CONV : (i + 1) * CONV] for i in range(3)], axis=1)

    def own(rows_of, size):
        return lax.dynamic_slice_in_dim(rows_of, index * size, size, rows_of.ndim - 1)

    line = 3 * CONV

    def from_order(grad):
        blocks = grad.reshape(share, 2, 2, 2, devices // 8, -1)
        return blocks.transpose(0, 4, 3, 2, 1, 5).reshape(share, hidden_size)

    return (
        output,
        grad_tokens,
        own(table[line], share),
        g_last[:, :model],
        g_last[:, model : 2 * model],
        g_last[:, 2 * model : chan],
        own(g_taps, wide),
        own(table[line + 3 :], share).T,
        g_early[:, model:],
        own(table[line + 2], own_gain),
        g_early[:, :model],
        own(table[line + 1], share),
        from_order(g_mlp[:, :hidden_size]),
        from_order(g_mlp[:, hidden_size : 2 * hidden_size]),
        g_down,
    )


def solution(mesh):
    seq, fsdp = mesh.devices.shape
    mesh = Mesh(mesh.devices.reshape(seq // 2, 2, fsdp // 2, 2), BOTH)
    rows = P(BOTH, None)
    flat = P(BOTH)
    cols = P(None, BOTH)
    return jax.shard_map(
        local,
        mesh=mesh,
        in_specs=(
            rows, flat, rows, rows, rows, cols, rows, rows, flat, rows, flat, rows, rows, rows,
            P(), rows,
        ),
        out_specs=(
            rows, rows, flat, rows, rows, rows, cols, rows, rows, flat, rows, flat, rows, rows,
            rows,
        ),
        check_vma=False,
    )
```

```python
import jax
import jax.numpy as jnp
from jax import lax
from jax.experimental import pallas as pl
from jax.experimental.pallas import tpu as pltpu
from jax.sharding import Mesh, PartitionSpec as P

CONV = 4
RIM = 8
TAIL = 16
LANES = 128
BASE = 8
LAST = "z"
SEQ, FSDP = (LAST, "x"), ("y", "c")
BOTH = SEQ + FSDP
f32 = jnp.float32
bf16 = jnp.bfloat16
highest = lax.Precision.HIGHEST
NN = (((1,), (0,)), ((), ()))
NT = (((1,), (1,)), ((), ()))
TN = (((0,), (0,)), ((), ()))


class Parts:
    def __init__(self, value, passes=3):
        value = value.astype(f32)
        self.high = value.astype(bf16)
        self.low = (value - self.high.astype(f32)).astype(bf16) if passes == 3 else None


def mm(a, b, dims=NN, passes=3):
    a = a if isinstance(a, Parts) else Parts(a, passes)
    b = b if isinstance(b, Parts) else Parts(b, passes)
    if passes == 1:
        return lax.dot_general(a.high, b.high, dims, preferred_element_type=f32)
    left = jnp.concatenate([a.high, a.low, a.high], axis=dims[0][0][0])
    right = jnp.concatenate([b.high, b.high, b.low], axis=dims[0][1][0])
    return lax.dot_general(left, right, dims, preferred_element_type=f32)


def sigmoid(v):
    return 1.0 / (1.0 + jnp.exp(-v))


def iotas(rows):
    return (
        lax.broadcasted_iota(jnp.int32, (rows, rows), 0),
        lax.broadcasted_iota(jnp.int32, (rows, rows), 1),
    )


def unit_lower_inverses(lowers, rows, cols, passes):
    size = lowers[0].shape[0]
    same = (rows // BASE) == (cols // BASE)
    powers = [jnp.where(same, -lower, 0.0) for lower in lowers]
    inverses = [jnp.where(rows == cols, 1.0, power) for power in powers]
    covered = 2
    while covered < BASE:
        parts = [Parts(power, passes) for power in powers]
        powers = [mm(part, part, NN, passes) for part in parts]
        inverses = [a + mm(a, b, NN, passes) for a, b in zip(inverses, powers)]
        covered *= 2
    block = BASE
    while block < size:
        joined = ((rows // (2 * block)) == (cols // (2 * block))) & (
            (rows // block) != (cols // block)
        )
        parts = [Parts(inverse, passes) for inverse in inverses]
        inner = [
            mm(part, jnp.where(joined, lower, 0.0), NN, passes)
            for part, lower in zip(parts, lowers)
        ]
        inverses = [
            inverse - mm(off, part, NN, passes)
            for inverse, off, part in zip(inverses, inner, parts)
        ]
        block *= 2
    return inverses


def joined_inverses(lowers, passes):
    size = lowers[0].shape[0] // 2
    rows, cols = iotas(size)
    halves = []
    for lower in lowers:
        halves += [lower[:size, :size], lower[size:, size:]]
    halves = unit_lower_inverses(halves, rows, cols, passes)
    results = []
    for i, lower in enumerate(lowers):
        first, second = halves[2 * i], halves[2 * i + 1]
        corner = mm(mm(second, lower[size:, :size], NN, passes), first, NN, passes)
        top = jnp.concatenate([first, jnp.zeros_like(first)], axis=1)
        results.append(
            jnp.concatenate([top, jnp.concatenate([-corner, second], axis=1)], axis=0)
        )
    return results


def head_column(table, head):
    lanes = lax.broadcasted_iota(jnp.int32, table.shape, 1)
    first = LANES - pl.num_programs(0) * PER_STEP
    return jnp.sum(jnp.where(lanes == first + head, table, 0.0), axis=1, keepdims=True)


def load_extended(ref, scratch, rows):
    scratch[0:RIM, :] = ref[rows : rows + RIM, :].astype(f32)
    scratch[RIM : RIM + rows, :] = ref[0:rows, :].astype(f32)


def convolve(scratch, taps, rows):
    total = taps[CONV - 1 : CONV, :] * scratch[RIM : RIM + rows, :]
    for j in range(CONV - 1):
        first = RIM - (CONV - 1) + j
        total = total + taps[j : j + 1, :] * scratch[first : first + rows, :]
    return total


FRONT_PASSES = 3
PASS_PASSES = 3
BACK_PASSES = 1
PER_STEP = 2


def lanes_of(i):
    return slice(i * LANES, (i + 1) * LANES)


def front_kernel(
    pq, pk, pv, tq, tk, tv, beta_logit, q_out, k_out, v_out, t_out, pair_out, scratch
):
    rows = q_out.shape[0]
    active = []
    for ref, taps in ((pq, tq), (pk, tk), (pv, tv)):
        load_extended(ref, scratch, rows)
        c = convolve(scratch, taps, rows)
        active.append(c * sigmoid(c))
    logits = beta_logit[...]
    ri, ci = iotas(rows)
    lowers, keys, values, betas = [], [], [], []
    for i in range(PER_STEP):
        head = pl.program_id(0) * PER_STEP + i
        a, b, v = (part[:, lanes_of(i)] for part in active)
        q_out[:, lanes_of(i)] = a * lax.rsqrt(jnp.sum(a * a, axis=1, keepdims=True) + 1e-06)
        k = b * lax.rsqrt(jnp.sum(b * b, axis=1, keepdims=True) + 1e-06)
        k_out[:, lanes_of(i)] = k
        v_out[:, lanes_of(i)] = v
        beta = sigmoid(head_column(logits, head))
        part = Parts(k, FRONT_PASSES)
        lowers.append(jnp.where(ri > ci, beta * mm(part, part, NT, FRONT_PASSES), 0.0))
        keys.append(part)
        values.append(beta * v)
        betas.append(beta * k)
    inverses = joined_inverses(lowers, FRONT_PASSES)
    for i in range(PER_STEP):
        t_out[i] = inverses[i]
        both = mm(
            inverses[i], jnp.concatenate([betas[i], values[i]], axis=1), NN, FRONT_PASSES
        )
        rs, cs = iotas(LANES)
        made = mm(both, keys[i], TN, FRONT_PASSES)
        pair_out[i, :LANES] = (jnp.where(rs == cs, 1.0, 0.0) - made[:LANES]).astype(bf16)
        pair_out[i, LANES:] = made[LANES:].astype(bf16)


def by_hop(place_ref, refs):
    count = len(refs)
    hop = lax.rem(place_ref[0] - pl.program_id(0) + count, count)
    value = refs[0][...]
    for h in range(1, count):
        value = jnp.where(hop == h, refs[h][...], value)
    return value[0]


def pass_kernel(
    place_ref, q_ref, k_ref, v_ref, t_ref, beta_logit, gate_ref, gain_ref, *rest
):
    state_refs, (branch_out, o_out, d_out, p_out) = rest[:-4], rest[-4:]
    states = by_hop(place_ref, state_refs)
    rows = q_ref.shape[0]
    logits = beta_logit[...]
    ri, ci = iotas(rows)
    for i in range(PER_STEP):
        head = pl.program_id(0) * PER_STEP + i
        cols = lanes_of(i)
        q, k, s = (Parts(m, PASS_PASSES) for m in (q_ref[:, cols], k_ref[:, cols], states[i]))
        beta = sigmoid(head_column(logits, head))
        p = jnp.where(ri >= ci, mm(q, k, NT, PASS_PASSES), 0.0)
        p_out[i] = p
        missing = v_ref[:, cols] - mm(k, s, NT, PASS_PASSES)
        d = mm(t_ref[i], beta * missing, NN, PASS_PASSES)
        d_out[:, cols] = d
        o = mm(q, s, NT, PASS_PASSES) + mm(p, d, NN, PASS_PASSES)
        o_out[:, cols] = o
        n = o * lax.rsqrt(jnp.mean(o * o, axis=1, keepdims=True) + 1e-05)
        g = gate_ref[:, cols]
        branch_out[:, cols] = (n * gain_ref[...] * (g * sigmoid(g))).astype(bf16)


def back_one_kernel(
    db_ref, o_ref, gate_ref, gain_ref, p_ref, t_ref, q_ref, k_ref, beta_logit,
    dgate_out, donorm_out, do_out, dr_out, g_out,
):
    gain = gain_ref[...]
    logits = beta_logit[...]
    for i in range(PER_STEP):
        head = pl.program_id(0) * PER_STEP + i
        cols = lanes_of(i)
        o = o_ref[:, cols]
        g = gate_ref[:, cols]
        db = db_ref[:, cols]
        beta = sigmoid(head_column(logits, head))
        scale = lax.rsqrt(jnp.mean(o * o, axis=1, keepdims=True) + 1e-05)
        n = o * scale
        sig = sigmoid(g)
        z = g * sig
        dgate_out[:, cols] = (db * n * gain * (sig * (1.0 + g * (1.0 - sig)))).astype(bf16)
        dy = db * z
        donorm_out[i] = jnp.sum(dy * n, axis=0, keepdims=True)
        dyg = dy * gain
        do = scale * dyg - o * (scale * scale * scale) * jnp.mean(dyg * o, axis=1, keepdims=True)
        do_out[:, cols] = do
        do = Parts(do, BACK_PASSES)
        dd = mm(p_ref[i], do, TN, BACK_PASSES)
        dr = mm(t_ref[i], dd, TN, BACK_PASSES)
        dr_out[:, cols] = dr
        g_out[i] = (
            mm(do, q_ref[:, cols], TN, BACK_PASSES)
            - mm(beta * dr, k_ref[:, cols], TN, BACK_PASSES)
        ).astype(bf16)


def back_two_kernel(
    place_ref, t_ref, p_ref, q_ref, k_ref, v_ref, beta_logit, do_ref, dr_ref, d_ref,
    pq, pk, pv, tq, tk, tv, *rest,
):
    count = (len(rest) - 15) // 2
    grads_in = by_hop(place_ref, rest[:count])
    states_in = by_hop(place_ref, rest[count : 2 * count])
    dq_out, dk_out, dv_out, eq_out, ek_out, ev_out, rq_out, rk_out, rv_out = rest[-15:-6]
    cq_out, ck_out, cv_out, dbeta_out, scratch, spread = rest[-6:]
    step = pl.program_id(0)
    rows = q_ref.shape[0]
    logits = beta_logit[...]
    ri, ci = iotas(rows)
    passes = BACK_PASSES

    @pl.when(step == 0)
    def _():
        dbeta_out[...] = jnp.zeros_like(dbeta_out)

    d_units = ([], [], [])
    for i in range(PER_STEP):
        head = step * PER_STEP + i
        cols = lanes_of(i)
        ds, s, q, k, do, d = (
            Parts(m, passes)
            for m in (
                grads_in[i], states_in[i], q_ref[:, cols], k_ref[:, cols], do_ref[:, cols],
                d_ref[:, cols],
            )
        )
        beta = sigmoid(head_column(logits, head))
        dr = dr_ref[:, cols] + mm(t_ref[i], mm(k, ds, NT, passes), TN, passes)
        missing = v_ref[:, cols] - mm(k, s, NT, passes)
        dp = Parts(jnp.where(ri >= ci, mm(do, d, NT, passes), 0.0), passes)
        bdr = beta * dr
        dq = mm(do, s, NN, passes) + mm(dp, k, NN, passes)
        dk = mm(dp, q, TN, passes) + mm(d, ds, NN, passes) - mm(bdr, s, NN, passes)
        da = jnp.where(ri > ci, -mm(dr, d, NT, passes), 0.0)
        dbeta = jnp.sum(dr * missing, axis=1, keepdims=True) + jnp.sum(
            da * mm(k, k, NT, passes), axis=1, keepdims=True
        )
        dm = Parts(beta * da, passes)
        dk = dk + mm(dm, k, NN, passes) + mm(dm, k, TN, passes)
        dlogit = dbeta * beta * (1.0 - beta)
        lanes = lax.broadcasted_iota(jnp.int32, dbeta_out.shape, 1)
        column = LANES - pl.num_programs(0) * PER_STEP + head
        dbeta_out[...] = jnp.where(lanes == column, dlogit, dbeta_out[...])
        for grads, grad in zip(d_units, (dq, dk, bdr)):
            grads.append(grad)

    width = q_ref.shape[1]
    spread[0:RIM, :] = jnp.zeros((RIM, width), f32)
    spread[RIM + rows : RIM + rows + RIM, :] = jnp.zeros((RIM, width), f32)
    sets = (
        (pq, tq, d_units[0], q_ref, dq_out, eq_out, rq_out, cq_out),
        (pk, tk, d_units[1], k_ref, dk_out, ek_out, rk_out, ck_out),
        (pv, tv, d_units[2], None, dv_out, ev_out, rv_out, cv_out),
    )
    for proj, taps, grads, units, out, tail_out, rim_out, tap_out in sets:
        load_extended(proj, scratch, rows)
        c = convolve(scratch, taps, rows)
        sig = sigmoid(c)
        if units is not None:
            act = c * sig
            for i in range(PER_STEP):
                cols = lanes_of(i)
                part, unit = act[:, cols], units[:, cols]
                inv = lax.rsqrt(jnp.sum(part * part, axis=1, keepdims=True) + 1e-06)
                grads[i] = (
                    grads[i] - unit * jnp.sum(unit * grads[i], axis=1, keepdims=True)
                ) * inv
        dc = jnp.concatenate(grads, axis=1) * (sig * (1.0 + c * (1.0 - sig)))
        spread[RIM : RIM + rows, :] = dc
        total = jnp.zeros((rows, width), f32)
        rim = jnp.zeros((RIM, width), f32)
        for j in range(CONV):
            lag = CONV - 1 - j
            tap = taps[j : j + 1, :]
            total = total + tap * spread[RIM + lag : RIM + lag + rows, :]
            rim = rim + tap * spread[lag : lag + RIM, :]
            first = RIM - lag
            tap_out[j : j + 1, :] = jnp.sum(
                dc * scratch[first : first + rows, :], axis=0, keepdims=True
            )
        out[...] = total.astype(bf16)
        tail_out[...] = total[rows - TAIL :]
        rim_out[...] = rim


LIGHT = pl.CostEstimate(flops=1, bytes_accessed=1, transcendentals=0)


def params():
    return pltpu.CompilerParams(
        dimension_semantics=("arbitrary",), vmem_limit_bytes=56 * 1024 * 1024
    )


def column_block(rows, heads, part):
    steps = heads // PER_STEP
    return pl.BlockSpec((rows, PER_STEP * LANES), lambda h, part=part: (0, part * steps + h))


def whole(shape):
    return pl.BlockSpec(shape, lambda h: (0,) * len(shape))


def scalar():
    return pl.BlockSpec(memory_space=pltpu.SMEM)


def per_head(shape):
    return pl.BlockSpec((PER_STEP,) + shape, lambda h: (h, 0, 0))


def pack_kernel(
    wq, wk, wv, wg, beta_ref, conv_ref, gain_ref, onorm_ref, mlp_ref, out, scratch
):
    model = wq.shape[1]
    for i, ref in enumerate((wq, wk, wv, wg)):
        out[:, i * model : (i + 1) * model] = ref[...]
    scratch[...] = jnp.zeros_like(scratch)
    taps, wide = conv_ref.shape
    scratch[0:taps, 0:wide] = conv_ref[...].astype(f32)
    for i, ref in enumerate((gain_ref, mlp_ref, onorm_ref)):
        scratch[taps + i : taps + i + 1, 0 : ref.shape[1]] = ref[...].astype(f32)
    heads = beta_ref.shape[1]
    scratch[:, LANES - heads :] = beta_ref[...].astype(f32)
    out[:, 4 * model :] = scratch[...].astype(bf16)


def run_pack(wq, wk, wv, wg, w_beta, conv, gain, onorm, mlp_gain):
    share, model = wq.shape
    return pl.pallas_call(
        pack_kernel,
        out_shape=jax.ShapeDtypeStruct((share, 4 * model + LANES), bf16),
        scratch_shapes=[pltpu.VMEM((share, LANES), f32)],
        name="pack",
    )(
        wq, wk, wv, wg, w_beta, conv, gain.reshape(1, -1), onorm.reshape(1, -1),
        mlp_gain.reshape(1, -1),
    )


def run_front(proj, taps, beta_logit, rows, heads):
    width = LANES
    p_spec = [column_block(rows + RIM, heads, i) for i in range(3)]
    t_spec = [column_block(CONV, heads, i) for i in range(3)]
    row_spec = column_block(rows, heads, 0)
    return pl.pallas_call(
        front_kernel,
        grid=(heads // PER_STEP,),
        in_specs=p_spec + t_spec + [whole((rows, LANES))],
        out_specs=[row_spec] * 3
        + [per_head((rows, rows)), per_head((2 * width, width))],
        out_shape=[jax.ShapeDtypeStruct((rows, heads * width), f32)] * 3
        + [
            jax.ShapeDtypeStruct((heads, rows, rows), f32),
            jax.ShapeDtypeStruct((heads, 2 * width, width), bf16),
        ],
        scratch_shapes=[pltpu.VMEM((rows + RIM, PER_STEP * width), f32)],
        compiler_params=params(),
        cost_estimate=LIGHT,
        name="front",
    )(proj, proj, proj, taps, taps, taps, beta_logit)


def run_pass(place, q, k, v, t, beta_logit, states, gate, gain, rows, heads):
    width = LANES
    row_spec = column_block(rows, heads, 0)
    square = per_head((rows, rows))
    return pl.pallas_call(
        pass_kernel,
        grid=(heads // PER_STEP,),
        in_specs=[
            scalar(), row_spec, row_spec, row_spec, square, whole((rows, LANES)), row_spec,
            whole((1, width)),
        ]
        + [whole(state.shape) for state in states],
        out_specs=[row_spec, row_spec, row_spec, square],
        out_shape=[
            jax.ShapeDtypeStruct((rows, heads * width), bf16),
            jax.ShapeDtypeStruct((rows, heads * width), f32),
            jax.ShapeDtypeStruct((rows, heads * width), f32),
            jax.ShapeDtypeStruct((heads, rows, rows), f32),
        ],
        compiler_params=params(),
        cost_estimate=LIGHT,
        name="chunk_pass",
    )(place, q, k, v, t, beta_logit, gate, gain, *states)


def run_back_one(d_branch, o, gate, gain, p, t, q, k, beta_logit, rows, heads):
    width = LANES
    row_spec = column_block(rows, heads, 0)
    square = per_head((rows, rows))
    return pl.pallas_call(
        back_one_kernel,
        grid=(heads // PER_STEP,),
        in_specs=[
            row_spec, row_spec, row_spec, whole((1, width)), square, square, row_spec, row_spec,
            whole((rows, LANES)),
        ],
        out_specs=[row_spec, per_head((1, width)), row_spec, row_spec, per_head((width, width))],
        out_shape=[
            jax.ShapeDtypeStruct((rows, heads * width), bf16),
            jax.ShapeDtypeStruct((heads, 1, width), f32),
            jax.ShapeDtypeStruct((rows, heads * width), f32),
            jax.ShapeDtypeStruct((rows, heads * width), f32),
            jax.ShapeDtypeStruct((heads, width, width), bf16),
        ],
        compiler_params=params(),
        cost_estimate=LIGHT,
        name="back_one",
    )(d_branch, o, gate, gain, p, t, q, k, beta_logit)


def run_back_two(
    place, grads, states, t, p, q, k, v, beta_logit, do, dr, d, proj, taps, rows, heads
):
    width = LANES
    row_spec = column_block(rows, heads, 0)
    square = per_head((rows, rows))
    p_spec = [column_block(rows + RIM, heads, i) for i in range(3)]
    t_spec = [column_block(CONV, heads, i) for i in range(3)]
    return pl.pallas_call(
        back_two_kernel,
        grid=(heads // PER_STEP,),
        in_specs=[
            scalar(), square, square, row_spec, row_spec, row_spec, whole((rows, LANES)),
            row_spec, row_spec, row_spec,
        ]
        + p_spec
        + t_spec
        + [whole(part.shape) for part in grads]
        + [whole(part.shape) for part in states],
        out_specs=[row_spec] * 3
        + [column_block(TAIL, heads, 0)] * 3
        + [column_block(RIM, heads, 0)] * 3
        + [column_block(CONV, heads, 0)] * 3
        + [whole((rows, LANES))],
        out_shape=[jax.ShapeDtypeStruct((rows, heads * width), bf16)] * 3
        + [jax.ShapeDtypeStruct((TAIL, heads * width), f32)] * 3
        + [jax.ShapeDtypeStruct((RIM, heads * width), f32)] * 3
        + [jax.ShapeDtypeStruct((CONV, heads * width), f32)] * 3
        + [jax.ShapeDtypeStruct((rows, LANES), f32)],
        scratch_shapes=[
            pltpu.VMEM((rows + RIM, PER_STEP * width), f32),
            pltpu.VMEM((rows + 2 * RIM, PER_STEP * width), f32),
        ],
        compiler_params=params(),
        cost_estimate=LIGHT,
        name="back_two",
    )(
        place, t, p, q, k, v, beta_logit, do, dr, d, proj, proj, proj, taps, taps, taps,
        *grads, *states,
    )


def prefix_kernel(place_ref, *rest):
    prefix_out, linear_out, group_out, ordered_ref = rest[-4:]
    parts = rest[:-4]
    count = len(parts)
    for hop in range(count):
        ordered_ref[lax.rem(place_ref[0] - hop + count, count)] = parts[hop][0].astype(f32)
    for m in range(ordered_ref.shape[1]):
        joined = ordered_ref[0, m]
        prefix_out[0, m] = joined
        linear_out[0, m] = joined[:LANES]
        for i in range(1, count):
            linear = ordered_ref[i, m, :LANES]
            linear_out[i, m] = linear
            joined = mm(joined, linear)
            joined = jnp.concatenate(
                [joined[:LANES], joined[LANES:] + ordered_ref[i, m, LANES:]], axis=0
            )
            prefix_out[i, m] = joined
        group_out[m] = joined.astype(bf16)


def entry_kernel(before_ref, prefix, *rest):
    totals, out = rest[:-1], rest[-1]
    for m in range(prefix.shape[1]):
        state = jnp.zeros((LANES, LANES), f32)
        for hop in range(len(totals), 0, -1):
            total = totals[hop - 1]
            if hop == len(totals):
                state = total[m].astype(f32)
            else:
                state = mm(state, total[m, :LANES]) + total[m, LANES:].astype(f32)
            state = jnp.where(hop <= before_ref[0], state, 0.0)
        out[0, m] = state.astype(bf16)
        for i in range(1, prefix.shape[0]):
            entry = mm(state, prefix[i - 1, m, :LANES]) + prefix[i - 1, m, LANES:]
            out[i, m] = entry.astype(bf16)


def suffix_kernel(place_ref, linears, prefix, *rest):
    inner_out, group_out, ordered_ref = rest[-3:]
    parts = rest[:-3]
    count = len(parts)
    for hop in range(count):
        ordered_ref[lax.rem(place_ref[0] - hop + count, count)] = parts[hop][0].astype(f32)
    for m in range(ordered_ref.shape[1]):
        grad = jnp.zeros((LANES, LANES), f32)
        for i in range(count - 1, -1, -1):
            inner_out[i, m] = grad
            grad = mm(grad, linears[i, m], NT) + ordered_ref[i, m]
        group_out[m, :LANES] = grad.astype(bf16)
        group_out[m, LANES:] = prefix[count - 1, m, :LANES].astype(bf16)


def leave_kernel(after_ref, inner, linears, *rest):
    out = rest[-1]
    reach = len(rest) - 1
    count = inner.shape[0]
    for m in range(inner.shape[1]):
        grad = jnp.zeros((LANES, LANES), f32)
        for hop in range(reach, 0, -1):
            total = rest[hop - 1]
            if hop == reach:
                grad = total[m].astype(f32)
            else:
                grad = mm(grad, total[m, LANES:], NT) + total[m, :LANES].astype(f32)
            grad = jnp.where(hop <= after_ref[0], grad, 0.0)
        for i in range(count - 1, -1, -1):
            out[i, m] = (inner[i, m] + grad).astype(bf16)
            if i:
                grad = mm(grad, linears[i, m], NT)


def run_small(kernel, number, arrays, shapes, scratch, name):
    return pl.pallas_call(
        kernel,
        in_specs=[scalar()] + [pl.BlockSpec(memory_space=pltpu.VMEM)] * len(arrays),
        out_specs=[pl.BlockSpec(memory_space=pltpu.VMEM)] * len(shapes),
        out_shape=[jax.ShapeDtypeStruct(shape, kind) for shape, kind in shapes],
        scratch_shapes=scratch,
        compiler_params=pltpu.CompilerParams(vmem_limit_bytes=56 * 1024 * 1024),
        cost_estimate=LIGHT,
        name=name,
    )(number, *arrays)


def swapped(parts, axis):
    count = lax.axis_size(axis)
    place = lax.axis_index(axis)
    result = [lax.dynamic_slice_in_dim(parts, place, 1, 0)]
    for hop in range(1, count):
        sent = lax.dynamic_slice_in_dim(parts, lax.rem(place + hop, count), 1, 0)
        result.append(lax.ppermute(sent, axis, [(i, (i + hop) % count) for i in range(count)]))
    return result


def shift_groups(array, by):
    size = lax.axis_size(SEQ)
    return lax.ppermute(
        array, SEQ, [(i, i + by) for i in range(size) if 0 <= i + by < size]
    )


def joined_chunks(pair, place):
    count = lax.axis_size(FSDP)
    heads, tall, width = pair.shape
    mine = heads // count
    parts = swapped(pair.reshape(count, mine, tall, width), FSDP)
    prefix, linears, group = run_small(
        prefix_kernel, place, parts,
        [
            ((count, mine, tall, width), f32), ((count, mine, width, width), f32),
            ((mine, tall, width), bf16),
        ],
        [pltpu.VMEM((count, mine, tall, width), f32)], "prefix",
    )
    return prefix, linears, group


def states_entering(prefix, group, before, reach, others):
    count, mine, tall, width = prefix.shape
    earlier = [shift_groups(group, hop) for hop in range(1, reach)]
    earlier.append(shift_groups(group[:, width:], reach))
    earlier, others = tied(earlier, others)
    (entries,) = run_small(
        entry_kernel, before, [prefix] + list(earlier), [((count, mine, width, width), bf16)], [],
        "entry",
    )
    return swapped(entries, FSDP), others


def state_grads_leaving(
    grads, linears, prefix, place, after, reach, sents, wait, meanwhile
):
    count = lax.axis_size(FSDP)
    heads, width = grads.shape[0], grads.shape[1]
    mine = heads // count
    parts = swapped(grads.reshape(count, mine, width, width), FSDP)
    parts, sent = tied(parts, sents[0])
    gots = [exchanged(sent, FIRST[0]), exchanged(sents[1], FIRST[1])]
    inner, group = run_small(
        suffix_kernel, place, [linears, prefix] + list(parts),
        [((count, mine, width, width), f32), ((mine, 2 * width, width), bf16)],
        [pltpu.VMEM((count, mine, width, width), f32)], "suffix",
    )
    inner, group, wait = tied(inner, group, wait)
    beyond = [shift_groups(group, -hop) for hop in range(1, reach)]
    beyond.append(shift_groups(group[:, :width], -reach))
    beyond, made = tied(beyond, meanwhile(wait))
    (entries,) = run_small(
        leave_kernel, after, [inner, linears] + list(beyond),
        [((count, mine, width, width), bf16)], [], "leave",
    )
    return swapped(entries, FSDP), gots, made


def rms(values):
    return lax.rsqrt(jnp.mean(values * values, axis=-1, keepdims=True) + 1e-05)


def rms_back(values, scale, gain, dy):
    dyg = dy * gain
    grad = scale * dyg - values * (scale * scale * scale) * jnp.mean(
        dyg * values, axis=-1, keepdims=True
    )
    return grad, jnp.sum(dy * values * scale, axis=0)


def dot(a, b):
    return jnp.dot(a, b, preferred_element_type=f32)


def dot_t(a, b):
    return lax.dot_general(a, b, NT, preferred_element_type=f32)


def t_dot(a, b):
    return lax.dot_general(a, b, TN, preferred_element_type=f32)


def flips(bit, count):
    return [(i, i ^ bit) for i in range(count)]


def exchanged(array, bit):
    return lax.ppermute(array, BOTH, flips(bit, lax.axis_size(BOTH)))


def place_bits():
    index = lax.axis_index(BOTH)
    return {bit: lax.rem(index // bit, 2) for bit in (1, 2, 4)}


def tied(*values):
    return lax.optimization_barrier(values)


def owner_order(array, axis):
    count = lax.axis_size(BOTH)
    shape = array.shape
    blocks = array.reshape(shape[:axis] + (count // 8, 2, 2, 2, -1) + shape[axis + 1 :])
    order = tuple(range(axis)) + tuple(axis + i for i in (3, 2, 1, 0, 4))
    return blocks.transpose(order + tuple(range(axis + 5, blocks.ndim))).reshape(shape)


def owner_matrix(size):
    source = owner_order(jnp.arange(size, dtype=jnp.int32), 0)
    side = place_bits()[1]
    source = jnp.concatenate([half(source, 1 - side), half(source, side)])
    return (jnp.arange(size, dtype=jnp.int32)[:, None] == source[None, :]).astype(bf16)


def half(array, which, axis=0):
    size = array.shape[axis] // 2
    return lax.dynamic_slice_in_dim(array, which * size, size, axis)


FIRST = (2, 4)


def pick(array, axis, which):
    return lax.dynamic_index_in_dim(array, which, axis, False)


def columns(array, i):
    wide = array.shape[-1] // 2
    return array[..., i * wide : (i + 1) * wide]


def begin_terms(away, right):
    return [exchanged(t_dot(away, part).astype(bf16), 1) for part in two_of(right)]


def middle_terms(homes, rights, gots):
    bits = place_bits()
    totals, sents = [], []
    for i, (home, right, got, first) in enumerate(zip(homes, rights, gots, FIRST)):
        total = (t_dot(home, right) + got.astype(f32)).astype(bf16)
        total = total.reshape((2, 2, -1) + total.shape[1:])
        totals.append(total)
        sents.append(pick(total, i, 1 - bits[first]).reshape(-1, right.shape[1]))
    return totals, sents


def two_of(array):
    return [columns(array, 0), columns(array, 1)]


def cross(sents, bits):
    return [exchanged(sent, bit) for sent, bit in zip(sents, bits)]


def end_terms(totals, gots):
    bits = place_bits()
    mine, sents = [], []
    for i, (total, got, first) in enumerate(zip(totals, gots, FIRST)):
        kept = pick(total, i, bits[first]).reshape(got.shape)
        kept = (kept.astype(f32) + got.astype(f32)).astype(bf16)
        mine.append(half(kept, bits[6 - first]))
        sents.append(half(kept, 1 - bits[6 - first]))
    return mine, sents


def owner_blocks(mine, gots):
    length = lax.axis_size(BOTH) // 8
    parts = [(m.astype(f32) + g.astype(f32)).astype(bf16) for m, g in zip(mine, gots)]
    return jnp.concatenate([p.reshape(length, -1, p.shape[-1]) for p in parts], axis=-1)


def stacked(blocks):
    length = len(blocks)
    place = lax.axis_index(BOTH) // 8
    back = jnp.stack(blocks[::-1] + blocks[::-1])
    return lax.dynamic_slice_in_dim(back, length - 1 - place, length, 0)


def merged(blocks, got, bit):
    mine = place_bits()[bit] == 0
    return jnp.stack([jnp.where(mine, blocks, got), jnp.where(mine, got, blocks)])


def along_last(by):
    count = lax.axis_size(BOTH)
    return [(i, (i + 8 * by) % count) for i in range(count)]


def send_blocks(blocks, hops=None):
    length = blocks.shape[0]
    place = lax.axis_index(BOTH) // 8

    def block(i):
        return lax.dynamic_index_in_dim(blocks, lax.rem(i, length), 0, False)

    if hops is None:
        return [block(place)] + send_blocks(blocks, range(1, length))
    return [lax.ppermute(block(place + hop), BOTH, along_last(hop)) for hop in hops]


def last_sum(blocks):
    flat = blocks.reshape(-1, blocks.shape[-1])
    return lax.psum_scatter(flat, LAST, scatter_dimension=0, tiled=True)


def added(parts):
    total = parts[0].astype(f32)
    for part in parts[1:]:
        total = total + part.astype(f32)
    return total


def local(
    tokens, attn_gain, w_query, w_key, w_value, conv_weight, w_beta, w_gate_out, onorm_gain,
    w_out, mlp_gain, w_mlp_gate, w_mlp_up, w_down, seq_lengths, cotangent,
):
    rows, model = tokens.shape
    heads = w_beta.shape[1]
    hidden_size = w_mlp_gate.shape[1]
    devices = lax.axis_size(BOTH)
    share = model // devices
    groups = lax.axis_size(SEQ)
    reach = groups // 2 - 1
    width = model // heads
    chan = 3 * model
    wide = chan // devices
    own_gain = onorm_gain.shape[0]
    pack_one = run_pack(
        w_query, w_key, w_value, w_gate_out, w_beta, conv_weight, attn_gain, onorm_gain, mlp_gain
    )
    full_one = lax.all_gather(pack_one, BOTH, axis=0, tiled=True)
    seq_lengths, w_mlp_gate, w_mlp_up, w_out, w_down, tokens, pack_one = (
        lax.optimization_barrier(
            (seq_lengths, w_mlp_gate, w_mlp_up, w_out, w_down, tokens, pack_one)
        )
    )
    down = [w_down] + [
        lax.ppermute(w_down, BOTH, along_last(hop)) for hop in range(1, devices // 8)
    ]
    down = stacked(down)
    halves = [columns(down, i) for i in range(2)]
    gots = cross(halves, FIRST[::-1])
    halves = [merged(h, g, bit) for h, g, bit in zip(halves, gots, FIRST[::-1])]
    full_one, halves = tied(full_one, halves)
    full_two = lax.all_gather(
        jnp.concatenate([w_out, owner_order(w_mlp_gate, 1), owner_order(w_mlp_up, 1)], axis=1),
        BOTH,
        axis=0,
        tiled=True,
    )
    to_order = owner_matrix(model)

    group_rows = rows * lax.axis_size(FSDP)
    first = lax.axis_index(BOTH) * rows
    group_first = lax.axis_index(SEQ) * group_rows
    ends = jnp.cumsum(seq_lengths)
    starts = ends - seq_lengths
    begin = jnp.max(jnp.where(starts <= first, starts, 0))
    end = jnp.min(jnp.where(ends > first, ends, rows * devices))
    opens = first == begin
    before = ((group_first - begin) // group_rows).reshape(1)
    beyond = ((end - group_first) // group_rows - 1).reshape(1)
    place = lax.axis_index(FSDP).reshape(1)

    heads_wide = chan + model
    w_heads = full_one[:, :heads_wide]
    full_misc = full_one[:, heads_wide:]
    w_out_full = full_two[:, :model]
    w_both = full_two[:, model:]
    misc = full_misc.reshape(devices, share, LANES)
    gain_one = misc[:, CONV, :share].reshape(model).astype(f32)
    gain_two = misc[:, CONV + 1, :share].reshape(model).astype(f32)
    onorm = misc[:, CONV + 2, :own_gain].reshape(1, width).astype(f32)
    taps = misc[:, :CONV, :wide].swapaxes(0, 1).reshape(CONV, chan).astype(f32)
    beta_cols = jnp.where(
        lax.broadcasted_iota(jnp.int32, full_misc.shape, 1) >= LANES - heads, full_misc, 0
    )

    rim_tokens = lax.ppermute(
        tokens[rows - RIM :], BOTH, [(i, i + 1) for i in range(devices - 1)]
    )
    rim_tokens = jnp.where(opens, jnp.zeros_like(rim_tokens), rim_tokens)
    x_all = jnp.concatenate([tokens, rim_tokens], axis=0).astype(f32)
    scale_all = rms(x_all)
    normed_all = (x_all * scale_all * gain_one).astype(bf16)
    projected = dot(normed_all, w_heads[:, :chan]).astype(bf16)
    normed = normed_all[:rows]
    x = tokens.astype(f32)
    scale_one = scale_all[:rows]
    beta_logit = dot(normed, full_misc)
    normed_order = dot(normed, to_order).astype(bf16)
    gots = cross(halves, FIRST)
    q, k, v, t, pair = run_front(projected, taps, beta_logit, rows, heads)
    pair, gots = tied(pair, gots)
    prefix, linears, group = joined_chunks(pair, place)
    halves = [merged(h, g, bit) for h, g, bit in zip(halves, gots, FIRST)]
    gate_logit = dot(normed, w_heads[:, chan:])
    group, halves, gate_logit = tied(group, halves, gate_logit)
    gots = cross(halves, (1, 1))
    states, gots = states_entering(prefix, group, before, reach, gots)
    halves = [merged(h, g, 1) for h, g in zip(halves, gots)]
    halves[1] = halves[1].swapaxes(1, 2)
    full_down = jnp.concatenate([h.reshape(hidden_size, -1) for h in halves], axis=1)
    states, full_down = tied(states, full_down)
    branch, o, d, p = run_pass(
        place, q, k, v, t, beta_logit, states, gate_logit, onorm, rows, heads
    )
    hidden = x + dot(branch, w_out_full)
    scale_two = rms(hidden)
    normed_two = (hidden * scale_two * gain_two).astype(bf16)
    both_rows = dot(normed_two, w_both)
    gate_rows, up_rows = both_rows[:, :hidden_size], both_rows[:, hidden_size:]
    sig = sigmoid(gate_rows)
    act = gate_rows * sig
    inner = (act * up_rows).astype(bf16)
    side = place_bits()[1]
    down_got = begin_terms(half(inner, 1 - side, 1), cotangent)
    d_inner = dot_t(cotangent, full_down)
    d_both = jnp.concatenate(
        [d_inner * up_rows * (sig * (1.0 + gate_rows * (1.0 - sig))), d_inner * act], axis=1
    ).astype(bf16)
    two_order = dot(normed_two, to_order).astype(bf16)
    both_got = begin_terms(two_order[:, : model // 2], d_both)
    down_home = half(inner, side, 1)
    down_totals, down_sents = middle_terms([down_home] * 2, two_of(cotangent), down_got)
    d_both, down_totals, down_sents = tied(d_both, down_totals, down_sents)
    down_gots = cross(down_sents, FIRST)
    d_normed_two = dot_t(d_both, w_both)
    d_norm, grad_gain_two = rms_back(hidden, scale_two, gain_two, d_normed_two)
    d_hidden = cotangent.astype(f32) + d_norm
    d_attn = d_hidden.astype(bf16)
    d_branch = dot_t(d_attn, w_out_full)
    branch_order = dot(branch, to_order).astype(bf16)
    out_got = exchanged(t_dot(branch_order[:, : model // 2], d_attn).astype(bf16), 1)
    both_totals, both_sents = middle_terms(
        [two_order[:, model // 2 :]] * 2, two_of(d_both), both_got
    )
    d_branch, down_gots, both_totals, both_sents = tied(
        d_branch, down_gots, both_totals, both_sents
    )

    d_gate_logit, d_onorm, d_o, d_r, state_grad = run_back_one(
        d_branch, o, gate_logit, onorm, p, t, q, k, beta_logit, rows, heads
    )
    state_grad, out_got = tied(state_grad, out_got)
    away, home = normed_order[:, : model // 2], normed_order[:, model // 2 :]
    gate_got = exchanged(t_dot(away, d_gate_logit).astype(bf16), 1)

    def meanwhile(held):
        gate_got, inner, d_attn = held
        totals, sents = middle_terms(
            [branch_order[:, model // 2 :], home], [d_attn, d_gate_logit], [out_got, gate_got]
        )
        return (
            end_terms(down_totals, down_gots),
            totals,
            sents,
            (hidden + dot(inner, full_down)).astype(bf16),
        )

    leaving, firsts, (down_ends, gate_totals, gate_sents, output) = state_grads_leaving(
        state_grad, linears, prefix, place, beyond, reach, both_sents,
        (gate_got, inner, d_attn), meanwhile,
    )
    leaving, firsts = tied(leaving, firsts)
    both_mine, both_sents = end_terms(both_totals, firsts)
    leaving, both_mine, both_sents = tied(leaving, both_mine, both_sents)
    both_gots = cross(both_sents, FIRST[::-1])
    outs = run_back_two(
        place, leaving, states, t, p, q, k, v, beta_logit, d_o, d_r, d, projected, taps,
        rows, heads,
    )
    outs, both_gots, gate_sents = tied(outs, both_gots, gate_sents)
    gate_gots = cross(gate_sents, FIRST)
    mlp_blocks = owner_blocks(both_mine, both_gots)
    tails = jnp.concatenate(outs[3:6], axis=1)
    rims = jnp.concatenate(outs[6:9], axis=1)
    d_beta = outs[12].astype(bf16)
    rims = jnp.where(opens, jnp.zeros_like(rims), rims)
    rims = lax.ppermute(rims, BOTH, [(i + 1, i) for i in range(devices - 1)])
    tails = tails + jnp.pad(rims, ((TAIL - RIM, 0), (0, 0)))
    d_proj = lax.dynamic_update_slice_in_dim(
        jnp.concatenate(outs[0:3], axis=1), tails.astype(bf16), rows - TAIL, 0
    )
    d_proj, mlp_blocks, (down_mine, down_sents) = tied(d_proj, mlp_blocks, down_ends)
    down_gots = cross(down_sents, FIRST[::-1])
    g_mlp = last_sum(mlp_blocks)
    last_got = begin_terms(away, d_proj)
    d_normed = (
        dot_t(d_proj, w_heads[:, :chan])
        + dot_t(d_gate_logit, w_heads[:, chan:])
        + dot_t(d_beta, beta_cols)
    )
    d_token_norm, grad_gain_one = rms_back(x, scale_one, gain_one, d_normed)
    grad_tokens = d_hidden + d_token_norm
    grad_beta = t_dot(d_beta, normed)[LANES - heads :]
    table = jnp.concatenate(
        list(outs[9:12])
        + [
            grad_gain_one.reshape(1, model),
            grad_gain_two.reshape(1, model),
            jnp.pad(jnp.sum(d_onorm, axis=(0, 1)).reshape(1, width), ((0, 0), (0, model - width))),
            grad_beta,
        ],
        axis=0,
    )
    table = table + exchanged(table, 8)
    last_got, grad_tokens, gate_gots = tied(last_got, grad_tokens, gate_gots)
    last_totals, last_sents = middle_terms([home] * 2, two_of(d_proj), last_got)
    last_totals, last_sents, gate_gots, table, down_gots = tied(
        last_totals, last_sents, gate_gots, table, down_gots
    )
    last_gots = cross(last_sents, FIRST)
    g_down = last_sum(owner_blocks(down_mine, down_gots))
    gate_mine, gate_sents = end_terms(gate_totals, gate_gots)
    gate_gots = cross(gate_sents, FIRST[::-1])

    def from_order(grad):
        blocks = grad.reshape(share, 2, 2, 2, devices // 8, -1)
        return blocks.transpose(0, 4, 3, 2, 1, 5).reshape(share, hidden_size)

    for bit in [8 << i for i in range(1, (devices // 8).bit_length() - 1)] + [1, 4]:
        table = table + exchanged(table, bit)
    last_gots, gate_gots, g_mlp, table = tied(last_gots, gate_gots, g_mlp, table)
    last_mine, last_sents = end_terms(last_totals, last_gots)
    last_mine, last_sents, gate_gots, table, g_mlp = tied(
        last_mine, last_sents, gate_gots, table, g_mlp
    )
    last_gots = cross(last_sents, FIRST[::-1])
    g_early = last_sum(owner_blocks(gate_mine, gate_gots))
    table = table + exchanged(table, 2)
    g_mlp = g_mlp.astype(f32)
    g_gate, g_up = from_order(g_mlp[:, :hidden_size]), from_order(g_mlp[:, hidden_size:])
    last_gots, table, g_gate, g_up, g_down = tied(last_gots, table, g_gate, g_up, g_down)
    last_parts = send_blocks(owner_blocks(last_mine, last_gots))
    g_last = added(last_parts)
    g_early, g_down = g_early.astype(f32), g_down.astype(f32)
    index = lax.axis_index(BOTH)
    g_taps = jnp.concatenate([table[i * CONV : (i + 1) * CONV] for i in range(3)], axis=1)

    def own(rows_of, size):
        return lax.dynamic_slice_in_dim(rows_of, index * size, size, rows_of.ndim - 1)

    line = 3 * CONV

    return (
        output,
        grad_tokens,
        own(table[line], share),
        g_last[:, :model],
        g_last[:, model : 2 * model],
        g_last[:, 2 * model : chan],
        own(g_taps, wide),
        own(table[line + 3 :], share).T,
        g_early[:, model:],
        own(table[line + 2], own_gain),
        g_early[:, :model],
        own(table[line + 1], share),
        g_gate,
        g_up,
        g_down,
    )


def solution(mesh):
    seq, fsdp = mesh.devices.shape
    mesh = Mesh(mesh.devices.reshape(seq // 2, 2, fsdp // 2, 2), BOTH)
    rows = P(BOTH, None)
    flat = P(BOTH)
    cols = P(None, BOTH)
    return jax.shard_map(
        local,
        mesh=mesh,
        in_specs=(
            rows, flat, rows, rows, rows, cols, rows, rows, flat, rows, flat, rows, rows, rows,
            P(), rows,
        ),
        out_specs=(
            rows, rows, flat, rows, rows, rows, cols, rows, rows, flat, rows, flat, rows, rows,
            rows,
        ),
        check_vma=False,
    )
```

```python
import jax
import jax.numpy as jnp
from jax import lax
from jax.experimental import pallas as pl
from jax.experimental.pallas import tpu as pltpu
from jax.sharding import Mesh, PartitionSpec as P

CONV = 4
RIM = 8
TAIL = 16
LANES = 128
BASE = 8
LAST = "z"
SEQ, FSDP = (LAST, "x"), ("y", "c")
BOTH = SEQ + FSDP
f32 = jnp.float32
bf16 = jnp.bfloat16
highest = lax.Precision.HIGHEST
NN = (((1,), (0,)), ((), ()))
NT = (((1,), (1,)), ((), ()))
TN = (((0,), (0,)), ((), ()))


class Parts:
    def __init__(self, value, passes=3):
        value = value.astype(f32)
        self.high = value.astype(bf16)
        self.low = (value - self.high.astype(f32)).astype(bf16) if passes == 3 else None


def mm(a, b, dims=NN, passes=3):
    a = a if isinstance(a, Parts) else Parts(a, passes)
    b = b if isinstance(b, Parts) else Parts(b, passes)
    if passes == 1:
        return lax.dot_general(a.high, b.high, dims, preferred_element_type=f32)
    left = jnp.concatenate([a.high, a.low, a.high], axis=dims[0][0][0])
    right = jnp.concatenate([b.high, b.high, b.low], axis=dims[0][1][0])
    return lax.dot_general(left, right, dims, preferred_element_type=f32)


def sigmoid(v):
    return 1.0 / (1.0 + jnp.exp(-v))


def iotas(rows):
    return (
        lax.broadcasted_iota(jnp.int32, (rows, rows), 0),
        lax.broadcasted_iota(jnp.int32, (rows, rows), 1),
    )


def unit_lower_inverses(lowers, rows, cols, passes):
    size = lowers[0].shape[0]
    same = (rows // BASE) == (cols // BASE)
    powers = [jnp.where(same, -lower, 0.0) for lower in lowers]
    inverses = [jnp.where(rows == cols, 1.0, power) for power in powers]
    covered = 2
    while covered < BASE:
        parts = [Parts(power, passes) for power in powers]
        powers = [mm(part, part, NN, passes) for part in parts]
        inverses = [a + mm(a, b, NN, passes) for a, b in zip(inverses, powers)]
        covered *= 2
    block = BASE
    while block < size:
        joined = ((rows // (2 * block)) == (cols // (2 * block))) & (
            (rows // block) != (cols // block)
        )
        parts = [Parts(inverse, passes) for inverse in inverses]
        inner = [
            mm(part, jnp.where(joined, lower, 0.0), NN, passes)
            for part, lower in zip(parts, lowers)
        ]
        inverses = [
            inverse - mm(off, part, NN, passes)
            for inverse, off, part in zip(inverses, inner, parts)
        ]
        block *= 2
    return inverses


def joined_inverses(lowers, passes):
    size = lowers[0].shape[0] // 2
    rows, cols = iotas(size)
    halves = []
    for lower in lowers:
        halves += [lower[:size, :size], lower[size:, size:]]
    halves = unit_lower_inverses(halves, rows, cols, passes)
    results = []
    for i, lower in enumerate(lowers):
        first, second = halves[2 * i], halves[2 * i + 1]
        corner = mm(mm(second, lower[size:, :size], NN, passes), first, NN, passes)
        top = jnp.concatenate([first, jnp.zeros_like(first)], axis=1)
        results.append(
            jnp.concatenate([top, jnp.concatenate([-corner, second], axis=1)], axis=0)
        )
    return results


def head_column(table, head):
    lanes = lax.broadcasted_iota(jnp.int32, table.shape, 1)
    first = LANES - pl.num_programs(0) * PER_STEP
    return jnp.sum(jnp.where(lanes == first + head, table, 0.0), axis=1, keepdims=True)


def load_extended(ref, scratch, rows):
    scratch[0:RIM, :] = ref[rows : rows + RIM, :].astype(f32)
    scratch[RIM : RIM + rows, :] = ref[0:rows, :].astype(f32)


def convolve(scratch, taps, rows):
    total = taps[CONV - 1 : CONV, :] * scratch[RIM : RIM + rows, :]
    for j in range(CONV - 1):
        first = RIM - (CONV - 1) + j
        total = total + taps[j : j + 1, :] * scratch[first : first + rows, :]
    return total


FRONT_PASSES = 3
PASS_PASSES = 3
BACK_PASSES = 1
PER_STEP = 2


def lanes_of(i):
    return slice(i * LANES, (i + 1) * LANES)


def front_kernel(
    pq, pk, pv, tq, tk, tv, beta_logit, q_out, k_out, v_out, t_out, pair_out, scratch
):
    rows = q_out.shape[0]
    active = []
    for ref, taps in ((pq, tq), (pk, tk), (pv, tv)):
        load_extended(ref, scratch, rows)
        c = convolve(scratch, taps, rows)
        active.append(c * sigmoid(c))
    logits = beta_logit[...]
    ri, ci = iotas(rows)
    lowers, keys, values, betas = [], [], [], []
    for i in range(PER_STEP):
        head = pl.program_id(0) * PER_STEP + i
        a, b, v = (part[:, lanes_of(i)] for part in active)
        q_out[:, lanes_of(i)] = a * lax.rsqrt(jnp.sum(a * a, axis=1, keepdims=True) + 1e-06)
        k = b * lax.rsqrt(jnp.sum(b * b, axis=1, keepdims=True) + 1e-06)
        k_out[:, lanes_of(i)] = k
        v_out[:, lanes_of(i)] = v
        beta = sigmoid(head_column(logits, head))
        part = Parts(k, FRONT_PASSES)
        lowers.append(jnp.where(ri > ci, beta * mm(part, part, NT, FRONT_PASSES), 0.0))
        keys.append(part)
        values.append(beta * v)
        betas.append(beta * k)
    inverses = joined_inverses(lowers, FRONT_PASSES)
    for i in range(PER_STEP):
        t_out[i] = inverses[i]
        both = mm(
            inverses[i], jnp.concatenate([betas[i], values[i]], axis=1), NN, FRONT_PASSES
        )
        rs, cs = iotas(LANES)
        made = mm(both, keys[i], TN, FRONT_PASSES)
        pair_out[i, :LANES] = (jnp.where(rs == cs, 1.0, 0.0) - made[:LANES]).astype(bf16)
        pair_out[i, LANES:] = made[LANES:].astype(bf16)


def by_hop(place_ref, refs):
    count = len(refs)
    hop = lax.rem(place_ref[0] - pl.program_id(0) + count, count)
    value = refs[0][...]
    for h in range(1, count):
        value = jnp.where(hop == h, refs[h][...], value)
    return value[0]


def pass_kernel(
    place_ref, q_ref, k_ref, v_ref, t_ref, beta_logit, gate_ref, gain_ref, *rest
):
    state_refs, (branch_out, o_out, d_out, p_out) = rest[:-4], rest[-4:]
    states = by_hop(place_ref, state_refs)
    rows = q_ref.shape[0]
    logits = beta_logit[...]
    ri, ci = iotas(rows)
    for i in range(PER_STEP):
        head = pl.program_id(0) * PER_STEP + i
        cols = lanes_of(i)
        q, k, s = (Parts(m, PASS_PASSES) for m in (q_ref[:, cols], k_ref[:, cols], states[i]))
        beta = sigmoid(head_column(logits, head))
        p = jnp.where(ri >= ci, mm(q, k, NT, PASS_PASSES), 0.0)
        p_out[i] = p
        missing = v_ref[:, cols] - mm(k, s, NT, PASS_PASSES)
        d = mm(t_ref[i], beta * missing, NN, PASS_PASSES)
        d_out[:, cols] = d
        o = mm(q, s, NT, PASS_PASSES) + mm(p, d, NN, PASS_PASSES)
        o_out[:, cols] = o
        n = o * lax.rsqrt(jnp.mean(o * o, axis=1, keepdims=True) + 1e-05)
        g = gate_ref[:, cols]
        branch_out[:, cols] = (n * gain_ref[...] * (g * sigmoid(g))).astype(bf16)


def back_one_kernel(
    db_ref, o_ref, gate_ref, gain_ref, p_ref, t_ref, q_ref, k_ref, beta_logit,
    dgate_out, donorm_out, do_out, dr_out, g_out,
):
    gain = gain_ref[...]
    logits = beta_logit[...]
    for i in range(PER_STEP):
        head = pl.program_id(0) * PER_STEP + i
        cols = lanes_of(i)
        o = o_ref[:, cols]
        g = gate_ref[:, cols]
        db = db_ref[:, cols]
        beta = sigmoid(head_column(logits, head))
        scale = lax.rsqrt(jnp.mean(o * o, axis=1, keepdims=True) + 1e-05)
        n = o * scale
        sig = sigmoid(g)
        z = g * sig
        dgate_out[:, cols] = (db * n * gain * (sig * (1.0 + g * (1.0 - sig)))).astype(bf16)
        dy = db * z
        donorm_out[i] = jnp.sum(dy * n, axis=0, keepdims=True)
        dyg = dy * gain
        do = scale * dyg - o * (scale * scale * scale) * jnp.mean(dyg * o, axis=1, keepdims=True)
        do_out[:, cols] = do
        do = Parts(do, BACK_PASSES)
        dd = mm(p_ref[i], do, TN, BACK_PASSES)
        dr = mm(t_ref[i], dd, TN, BACK_PASSES)
        dr_out[:, cols] = dr
        g_out[i] = (
            mm(do, q_ref[:, cols], TN, BACK_PASSES)
            - mm(beta * dr, k_ref[:, cols], TN, BACK_PASSES)
        ).astype(bf16)


def back_two_kernel(
    place_ref, t_ref, p_ref, q_ref, k_ref, v_ref, beta_logit, do_ref, dr_ref, d_ref,
    pq, pk, pv, tq, tk, tv, *rest,
):
    count = (len(rest) - 15) // 2
    grads_in = by_hop(place_ref, rest[:count])
    states_in = by_hop(place_ref, rest[count : 2 * count])
    dq_out, dk_out, dv_out, eq_out, ek_out, ev_out, rq_out, rk_out, rv_out = rest[-15:-6]
    cq_out, ck_out, cv_out, dbeta_out, scratch, spread = rest[-6:]
    step = pl.program_id(0)
    rows = q_ref.shape[0]
    logits = beta_logit[...]
    ri, ci = iotas(rows)
    passes = BACK_PASSES

    @pl.when(step == 0)
    def _():
        dbeta_out[...] = jnp.zeros_like(dbeta_out)

    d_units = ([], [], [])
    for i in range(PER_STEP):
        head = step * PER_STEP + i
        cols = lanes_of(i)
        ds, s, q, k, do, d = (
            Parts(m, passes)
            for m in (
                grads_in[i], states_in[i], q_ref[:, cols], k_ref[:, cols], do_ref[:, cols],
                d_ref[:, cols],
            )
        )
        beta = sigmoid(head_column(logits, head))
        dr = dr_ref[:, cols] + mm(t_ref[i], mm(k, ds, NT, passes), TN, passes)
        missing = v_ref[:, cols] - mm(k, s, NT, passes)
        dp = Parts(jnp.where(ri >= ci, mm(do, d, NT, passes), 0.0), passes)
        bdr = beta * dr
        dq = mm(do, s, NN, passes) + mm(dp, k, NN, passes)
        dk = mm(dp, q, TN, passes) + mm(d, ds, NN, passes) - mm(bdr, s, NN, passes)
        da = jnp.where(ri > ci, -mm(dr, d, NT, passes), 0.0)
        dbeta = jnp.sum(dr * missing, axis=1, keepdims=True) + jnp.sum(
            da * mm(k, k, NT, passes), axis=1, keepdims=True
        )
        dm = Parts(beta * da, passes)
        dk = dk + mm(dm, k, NN, passes) + mm(dm, k, TN, passes)
        dlogit = dbeta * beta * (1.0 - beta)
        lanes = lax.broadcasted_iota(jnp.int32, dbeta_out.shape, 1)
        column = LANES - pl.num_programs(0) * PER_STEP + head
        dbeta_out[...] = jnp.where(lanes == column, dlogit, dbeta_out[...])
        for grads, grad in zip(d_units, (dq, dk, bdr)):
            grads.append(grad)

    width = q_ref.shape[1]
    spread[0:RIM, :] = jnp.zeros((RIM, width), f32)
    spread[RIM + rows : RIM + rows + RIM, :] = jnp.zeros((RIM, width), f32)
    sets = (
        (pq, tq, d_units[0], q_ref, dq_out, eq_out, rq_out, cq_out),
        (pk, tk, d_units[1], k_ref, dk_out, ek_out, rk_out, ck_out),
        (pv, tv, d_units[2], None, dv_out, ev_out, rv_out, cv_out),
    )
    for proj, taps, grads, units, out, tail_out, rim_out, tap_out in sets:
        load_extended(proj, scratch, rows)
        c = convolve(scratch, taps, rows)
        sig = sigmoid(c)
        if units is not None:
            act = c * sig
            for i in range(PER_STEP):
                cols = lanes_of(i)
                part, unit = act[:, cols], units[:, cols]
                inv = lax.rsqrt(jnp.sum(part * part, axis=1, keepdims=True) + 1e-06)
                grads[i] = (
                    grads[i] - unit * jnp.sum(unit * grads[i], axis=1, keepdims=True)
                ) * inv
        dc = jnp.concatenate(grads, axis=1) * (sig * (1.0 + c * (1.0 - sig)))
        spread[RIM : RIM + rows, :] = dc
        total = jnp.zeros((rows, width), f32)
        rim = jnp.zeros((RIM, width), f32)
        for j in range(CONV):
            lag = CONV - 1 - j
            tap = taps[j : j + 1, :]
            total = total + tap * spread[RIM + lag : RIM + lag + rows, :]
            rim = rim + tap * spread[lag : lag + RIM, :]
            first = RIM - lag
            tap_out[j : j + 1, :] = jnp.sum(
                dc * scratch[first : first + rows, :], axis=0, keepdims=True
            )
        out[...] = total.astype(bf16)
        tail_out[...] = total[rows - TAIL :]
        rim_out[...] = rim


LIGHT = pl.CostEstimate(flops=1, bytes_accessed=1, transcendentals=0)


def params():
    return pltpu.CompilerParams(
        dimension_semantics=("arbitrary",), vmem_limit_bytes=56 * 1024 * 1024
    )


def column_block(rows, heads, part):
    steps = heads // PER_STEP
    return pl.BlockSpec((rows, PER_STEP * LANES), lambda h, part=part: (0, part * steps + h))


def whole(shape):
    return pl.BlockSpec(shape, lambda h: (0,) * len(shape))


def scalar():
    return pl.BlockSpec(memory_space=pltpu.SMEM)


def per_head(shape):
    return pl.BlockSpec((PER_STEP,) + shape, lambda h: (h, 0, 0))


def pack_kernel(
    wq, wk, wv, wg, beta_ref, conv_ref, gain_ref, onorm_ref, mlp_ref, out, scratch
):
    model = wq.shape[1]
    for i, ref in enumerate((wq, wk, wv, wg)):
        out[:, i * model : (i + 1) * model] = ref[...]
    scratch[...] = jnp.zeros_like(scratch)
    taps, wide = conv_ref.shape
    scratch[0:taps, 0:wide] = conv_ref[...].astype(f32)
    for i, ref in enumerate((gain_ref, mlp_ref, onorm_ref)):
        scratch[taps + i : taps + i + 1, 0 : ref.shape[1]] = ref[...].astype(f32)
    heads = beta_ref.shape[1]
    scratch[:, LANES - heads :] = beta_ref[...].astype(f32)
    out[:, 4 * model :] = scratch[...].astype(bf16)


def run_pack(wq, wk, wv, wg, w_beta, conv, gain, onorm, mlp_gain):
    share, model = wq.shape
    return pl.pallas_call(
        pack_kernel,
        out_shape=jax.ShapeDtypeStruct((share, 4 * model + LANES), bf16),
        scratch_shapes=[pltpu.VMEM((share, LANES), f32)],
        name="pack",
    )(
        wq, wk, wv, wg, w_beta, conv, gain.reshape(1, -1), onorm.reshape(1, -1),
        mlp_gain.reshape(1, -1),
    )


def run_front(proj, taps, beta_logit, rows, heads):
    width = LANES
    p_spec = [column_block(rows + RIM, heads, i) for i in range(3)]
    t_spec = [column_block(CONV, heads, i) for i in range(3)]
    row_spec = column_block(rows, heads, 0)
    return pl.pallas_call(
        front_kernel,
        grid=(heads // PER_STEP,),
        in_specs=p_spec + t_spec + [whole((rows, LANES))],
        out_specs=[row_spec] * 3
        + [per_head((rows, rows)), per_head((2 * width, width))],
        out_shape=[jax.ShapeDtypeStruct((rows, heads * width), f32)] * 3
        + [
            jax.ShapeDtypeStruct((heads, rows, rows), f32),
            jax.ShapeDtypeStruct((heads, 2 * width, width), bf16),
        ],
        scratch_shapes=[pltpu.VMEM((rows + RIM, PER_STEP * width), f32)],
        compiler_params=params(),
        cost_estimate=LIGHT,
        name="front",
    )(proj, proj, proj, taps, taps, taps, beta_logit)


def run_pass(place, q, k, v, t, beta_logit, states, gate, gain, rows, heads):
    width = LANES
    row_spec = column_block(rows, heads, 0)
    square = per_head((rows, rows))
    return pl.pallas_call(
        pass_kernel,
        grid=(heads // PER_STEP,),
        in_specs=[
            scalar(), row_spec, row_spec, row_spec, square, whole((rows, LANES)), row_spec,
            whole((1, width)),
        ]
        + [whole(state.shape) for state in states],
        out_specs=[row_spec, row_spec, row_spec, square],
        out_shape=[
            jax.ShapeDtypeStruct((rows, heads * width), bf16),
            jax.ShapeDtypeStruct((rows, heads * width), f32),
            jax.ShapeDtypeStruct((rows, heads * width), f32),
            jax.ShapeDtypeStruct((heads, rows, rows), f32),
        ],
        compiler_params=params(),
        cost_estimate=LIGHT,
        name="chunk_pass",
    )(place, q, k, v, t, beta_logit, gate, gain, *states)


def run_back_one(d_branch, o, gate, gain, p, t, q, k, beta_logit, rows, heads):
    width = LANES
    row_spec = column_block(rows, heads, 0)
    square = per_head((rows, rows))
    return pl.pallas_call(
        back_one_kernel,
        grid=(heads // PER_STEP,),
        in_specs=[
            row_spec, row_spec, row_spec, whole((1, width)), square, square, row_spec, row_spec,
            whole((rows, LANES)),
        ],
        out_specs=[row_spec, per_head((1, width)), row_spec, row_spec, per_head((width, width))],
        out_shape=[
            jax.ShapeDtypeStruct((rows, heads * width), bf16),
            jax.ShapeDtypeStruct((heads, 1, width), f32),
            jax.ShapeDtypeStruct((rows, heads * width), f32),
            jax.ShapeDtypeStruct((rows, heads * width), f32),
            jax.ShapeDtypeStruct((heads, width, width), bf16),
        ],
        compiler_params=params(),
        cost_estimate=LIGHT,
        name="back_one",
    )(d_branch, o, gate, gain, p, t, q, k, beta_logit)


def run_back_two(
    place, grads, states, t, p, q, k, v, beta_logit, do, dr, d, proj, taps, rows, heads
):
    width = LANES
    row_spec = column_block(rows, heads, 0)
    square = per_head((rows, rows))
    p_spec = [column_block(rows + RIM, heads, i) for i in range(3)]
    t_spec = [column_block(CONV, heads, i) for i in range(3)]
    return pl.pallas_call(
        back_two_kernel,
        grid=(heads // PER_STEP,),
        in_specs=[
            scalar(), square, square, row_spec, row_spec, row_spec, whole((rows, LANES)),
            row_spec, row_spec, row_spec,
        ]
        + p_spec
        + t_spec
        + [whole(part.shape) for part in grads]
        + [whole(part.shape) for part in states],
        out_specs=[row_spec] * 3
        + [column_block(TAIL, heads, 0)] * 3
        + [column_block(RIM, heads, 0)] * 3
        + [column_block(CONV, heads, 0)] * 3
        + [whole((rows, LANES))],
        out_shape=[jax.ShapeDtypeStruct((rows, heads * width), bf16)] * 3
        + [jax.ShapeDtypeStruct((TAIL, heads * width), f32)] * 3
        + [jax.ShapeDtypeStruct((RIM, heads * width), f32)] * 3
        + [jax.ShapeDtypeStruct((CONV, heads * width), f32)] * 3
        + [jax.ShapeDtypeStruct((rows, LANES), f32)],
        scratch_shapes=[
            pltpu.VMEM((rows + RIM, PER_STEP * width), f32),
            pltpu.VMEM((rows + 2 * RIM, PER_STEP * width), f32),
        ],
        compiler_params=params(),
        cost_estimate=LIGHT,
        name="back_two",
    )(
        place, t, p, q, k, v, beta_logit, do, dr, d, proj, proj, proj, taps, taps, taps,
        *grads, *states,
    )


def prefix_kernel(place_ref, *rest):
    prefix_out, linear_out, group_out, ordered_ref = rest[-4:]
    parts = rest[:-4]
    count = len(parts)
    for hop in range(count):
        ordered_ref[lax.rem(place_ref[0] - hop + count, count)] = parts[hop][0].astype(f32)
    for m in range(ordered_ref.shape[1]):
        joined = ordered_ref[0, m]
        prefix_out[0, m] = joined
        linear_out[0, m] = joined[:LANES]
        for i in range(1, count):
            linear = ordered_ref[i, m, :LANES]
            linear_out[i, m] = linear
            joined = mm(joined, linear)
            joined = jnp.concatenate(
                [joined[:LANES], joined[LANES:] + ordered_ref[i, m, LANES:]], axis=0
            )
            prefix_out[i, m] = joined
        group_out[m] = joined.astype(bf16)


def entry_kernel(before_ref, prefix, *rest):
    totals, out = rest[:-1], rest[-1]
    for m in range(prefix.shape[1]):
        state = jnp.zeros((LANES, LANES), f32)
        for hop in range(len(totals), 0, -1):
            total = totals[hop - 1]
            if hop == len(totals):
                state = total[m].astype(f32)
            else:
                state = mm(state, total[m, :LANES]) + total[m, LANES:].astype(f32)
            state = jnp.where(hop <= before_ref[0], state, 0.0)
        out[0, m] = state.astype(bf16)
        for i in range(1, prefix.shape[0]):
            entry = mm(state, prefix[i - 1, m, :LANES]) + prefix[i - 1, m, LANES:]
            out[i, m] = entry.astype(bf16)


def suffix_kernel(place_ref, linears, prefix, *rest):
    inner_out, group_out, ordered_ref = rest[-3:]
    parts = rest[:-3]
    count = len(parts)
    for hop in range(count):
        ordered_ref[lax.rem(place_ref[0] - hop + count, count)] = parts[hop][0].astype(f32)
    for m in range(ordered_ref.shape[1]):
        grad = jnp.zeros((LANES, LANES), f32)
        for i in range(count - 1, -1, -1):
            inner_out[i, m] = grad
            grad = mm(grad, linears[i, m], NT) + ordered_ref[i, m]
        group_out[m, :LANES] = grad.astype(bf16)
        group_out[m, LANES:] = prefix[count - 1, m, :LANES].astype(bf16)


def leave_kernel(after_ref, inner, linears, *rest):
    out = rest[-1]
    reach = len(rest) - 1
    count = inner.shape[0]
    for m in range(inner.shape[1]):
        grad = jnp.zeros((LANES, LANES), f32)
        for hop in range(reach, 0, -1):
            total = rest[hop - 1]
            if hop == reach:
                grad = total[m].astype(f32)
            else:
                grad = mm(grad, total[m, LANES:], NT) + total[m, :LANES].astype(f32)
            grad = jnp.where(hop <= after_ref[0], grad, 0.0)
        for i in range(count - 1, -1, -1):
            out[i, m] = (inner[i, m] + grad).astype(bf16)
            if i:
                grad = mm(grad, linears[i, m], NT)


def run_small(kernel, number, arrays, shapes, scratch, name):
    return pl.pallas_call(
        kernel,
        in_specs=[scalar()] + [pl.BlockSpec(memory_space=pltpu.VMEM)] * len(arrays),
        out_specs=[pl.BlockSpec(memory_space=pltpu.VMEM)] * len(shapes),
        out_shape=[jax.ShapeDtypeStruct(shape, kind) for shape, kind in shapes],
        scratch_shapes=scratch,
        compiler_params=pltpu.CompilerParams(vmem_limit_bytes=56 * 1024 * 1024),
        cost_estimate=LIGHT,
        name=name,
    )(number, *arrays)


def swapped(parts, axis):
    count = lax.axis_size(axis)
    place = lax.axis_index(axis)
    result = [lax.dynamic_slice_in_dim(parts, place, 1, 0)]
    for hop in range(1, count):
        sent = lax.dynamic_slice_in_dim(parts, lax.rem(place + hop, count), 1, 0)
        result.append(lax.ppermute(sent, axis, [(i, (i + hop) % count) for i in range(count)]))
    return result


def shift_groups(array, by):
    size = lax.axis_size(SEQ)
    return lax.ppermute(
        array, SEQ, [(i, i + by) for i in range(size) if 0 <= i + by < size]
    )


def joined_chunks(pair, place):
    count = lax.axis_size(FSDP)
    heads, tall, width = pair.shape
    mine = heads // count
    parts = swapped(pair.reshape(count, mine, tall, width), FSDP)
    prefix, linears, group = run_small(
        prefix_kernel, place, parts,
        [
            ((count, mine, tall, width), f32), ((count, mine, width, width), f32),
            ((mine, tall, width), bf16),
        ],
        [pltpu.VMEM((count, mine, tall, width), f32)], "prefix",
    )
    return prefix, linears, group


def states_entering(prefix, group, before, reach, others):
    count, mine, tall, width = prefix.shape
    earlier = [shift_groups(group, hop) for hop in range(1, reach)]
    earlier.append(shift_groups(group[:, width:], reach))
    earlier, others = tied(earlier, others)
    (entries,) = run_small(
        entry_kernel, before, [prefix] + list(earlier), [((count, mine, width, width), bf16)], [],
        "entry",
    )
    return swapped(entries, FSDP), others


def state_grads_leaving(
    grads, linears, prefix, place, after, reach, sents, wait, meanwhile
):
    count = lax.axis_size(FSDP)
    heads, width = grads.shape[0], grads.shape[1]
    mine = heads // count
    parts = swapped(grads.reshape(count, mine, width, width), FSDP)
    parts, sent = tied(parts, sents[0])
    gots = [exchanged(sent, FIRST[0]), exchanged(sents[1], FIRST[1])]
    inner, group = run_small(
        suffix_kernel, place, [linears, prefix] + list(parts),
        [((count, mine, width, width), f32), ((mine, 2 * width, width), bf16)],
        [pltpu.VMEM((count, mine, width, width), f32)], "suffix",
    )
    inner, group, wait = tied(inner, group, wait)
    beyond = [shift_groups(group, -hop) for hop in range(1, reach)]
    beyond.append(shift_groups(group[:, :width], -reach))
    beyond, made = tied(beyond, meanwhile(wait))
    (entries,) = run_small(
        leave_kernel, after, [inner, linears] + list(beyond),
        [((count, mine, width, width), bf16)], [], "leave",
    )
    return swapped(entries, FSDP), gots, made


def rms(values):
    return lax.rsqrt(jnp.mean(values * values, axis=-1, keepdims=True) + 1e-05)


def rms_back(values, scale, gain, dy):
    dyg = dy * gain
    grad = scale * dyg - values * (scale * scale * scale) * jnp.mean(
        dyg * values, axis=-1, keepdims=True
    )
    return grad, jnp.sum(dy * values * scale, axis=0)


def dot(a, b):
    return jnp.dot(a, b, preferred_element_type=f32)


def dot_t(a, b):
    return lax.dot_general(a, b, NT, preferred_element_type=f32)


def t_dot(a, b):
    return lax.dot_general(a, b, TN, preferred_element_type=f32)


def flips(bit, count):
    return [(i, i ^ bit) for i in range(count)]


def exchanged(array, bit):
    return lax.ppermute(array, BOTH, flips(bit, lax.axis_size(BOTH)))


def place_bits():
    index = lax.axis_index(BOTH)
    return {bit: lax.rem(index // bit, 2) for bit in (1, 2, 4)}


def tied(*values):
    return lax.optimization_barrier(values)


def owner_order(array, axis):
    count = lax.axis_size(BOTH)
    shape = array.shape
    blocks = array.reshape(shape[:axis] + (count // 8, 2, 2, 2, -1) + shape[axis + 1 :])
    order = tuple(range(axis)) + tuple(axis + i for i in (3, 2, 1, 0, 4))
    return blocks.transpose(order + tuple(range(axis + 5, blocks.ndim))).reshape(shape)


def owner_matrix(size):
    source = owner_order(jnp.arange(size, dtype=jnp.int32), 0)
    side = place_bits()[1]
    source = jnp.concatenate([half(source, 1 - side), half(source, side)])
    return (jnp.arange(size, dtype=jnp.int32)[:, None] == source[None, :]).astype(bf16)


def half(array, which, axis=0):
    size = array.shape[axis] // 2
    return lax.dynamic_slice_in_dim(array, which * size, size, axis)


FIRST = (2, 4)


def pick(array, axis, which):
    return lax.dynamic_index_in_dim(array, which, axis, False)


def columns(array, i):
    wide = array.shape[-1] // 2
    return array[..., i * wide : (i + 1) * wide]


def begin_terms(away, right):
    return [exchanged(t_dot(away, part).astype(bf16), 1) for part in two_of(right)]


def middle_terms(homes, rights, gots):
    bits = place_bits()
    totals, sents = [], []
    for i, (home, right, got, first) in enumerate(zip(homes, rights, gots, FIRST)):
        total = (t_dot(home, right) + got.astype(f32)).astype(bf16)
        total = total.reshape((2, 2, -1) + total.shape[1:])
        totals.append(total)
        sents.append(pick(total, i, 1 - bits[first]).reshape(-1, right.shape[1]))
    return totals, sents


def two_of(array):
    return [columns(array, 0), columns(array, 1)]


def cross(sents, bits):
    return [exchanged(sent, bit) for sent, bit in zip(sents, bits)]


def end_terms(totals, gots):
    bits = place_bits()
    mine, sents = [], []
    for i, (total, got, first) in enumerate(zip(totals, gots, FIRST)):
        kept = pick(total, i, bits[first]).reshape(got.shape)
        kept = (kept.astype(f32) + got.astype(f32)).astype(bf16)
        mine.append(half(kept, bits[6 - first]))
        sents.append(half(kept, 1 - bits[6 - first]))
    return mine, sents


def owner_blocks(mine, gots):
    length = lax.axis_size(BOTH) // 8
    parts = [(m.astype(f32) + g.astype(f32)).astype(bf16) for m, g in zip(mine, gots)]
    return jnp.concatenate([p.reshape(length, -1, p.shape[-1]) for p in parts], axis=-1)


def stacked(blocks):
    length = len(blocks)
    place = lax.axis_index(BOTH) // 8
    back = jnp.stack(blocks[::-1] + blocks[::-1])
    return lax.dynamic_slice_in_dim(back, length - 1 - place, length, 0)


def merged(blocks, got, bit):
    mine = place_bits()[bit] == 0
    return jnp.stack([jnp.where(mine, blocks, got), jnp.where(mine, got, blocks)])


def along_last(by):
    count = lax.axis_size(BOTH)
    return [(i, (i + 8 * by) % count) for i in range(count)]


def send_blocks(blocks, hops=None):
    length = blocks.shape[0]
    place = lax.axis_index(BOTH) // 8

    def block(i):
        return lax.dynamic_index_in_dim(blocks, lax.rem(i, length), 0, False)

    if hops is None:
        return [block(place)] + send_blocks(blocks, range(1, length))
    return [lax.ppermute(block(place + hop), BOTH, along_last(hop)) for hop in hops]


def last_sum(blocks):
    flat = blocks.reshape(-1, blocks.shape[-1])
    return lax.psum_scatter(flat, LAST, scatter_dimension=0, tiled=True)


def added(parts):
    total = parts[0].astype(f32)
    for part in parts[1:]:
        total = total + part.astype(f32)
    return total


def local(
    tokens, attn_gain, w_query, w_key, w_value, conv_weight, w_beta, w_gate_out, onorm_gain,
    w_out, mlp_gain, w_mlp_gate, w_mlp_up, w_down, seq_lengths, cotangent,
):
    rows, model = tokens.shape
    heads = w_beta.shape[1]
    hidden_size = w_mlp_gate.shape[1]
    devices = lax.axis_size(BOTH)
    share = model // devices
    groups = lax.axis_size(SEQ)
    reach = groups // 2 - 1
    width = model // heads
    chan = 3 * model
    wide = chan // devices
    own_gain = onorm_gain.shape[0]
    pack_one = run_pack(
        w_query, w_key, w_value, w_gate_out, w_beta, conv_weight, attn_gain, onorm_gain, mlp_gain
    )
    full_one = lax.all_gather(pack_one, BOTH, axis=0, tiled=True)
    seq_lengths, w_mlp_gate, w_mlp_up, w_out, w_down, tokens, pack_one = (
        lax.optimization_barrier(
            (seq_lengths, w_mlp_gate, w_mlp_up, w_out, w_down, tokens, pack_one)
        )
    )
    down = [w_down] + [
        lax.ppermute(w_down, BOTH, along_last(hop)) for hop in range(1, devices // 8)
    ]
    down = stacked(down)
    halves = [columns(down, i) for i in range(2)]
    gots = cross(halves, FIRST[::-1])
    halves = [merged(h, g, bit) for h, g, bit in zip(halves, gots, FIRST[::-1])]
    full_one, halves = tied(full_one, halves)
    full_two = lax.all_gather(
        jnp.concatenate([w_out, owner_order(w_mlp_gate, 1), owner_order(w_mlp_up, 1)], axis=1),
        BOTH,
        axis=0,
        tiled=True,
    )
    to_order = owner_matrix(model)

    group_rows = rows * lax.axis_size(FSDP)
    first = lax.axis_index(BOTH) * rows
    group_first = lax.axis_index(SEQ) * group_rows
    ends = jnp.cumsum(seq_lengths)
    starts = ends - seq_lengths
    begin = jnp.max(jnp.where(starts <= first, starts, 0))
    end = jnp.min(jnp.where(ends > first, ends, rows * devices))
    opens = first == begin
    before = ((group_first - begin) // group_rows).reshape(1)
    beyond = ((end - group_first) // group_rows - 1).reshape(1)
    place = lax.axis_index(FSDP).reshape(1)

    heads_wide = chan + model
    w_heads = full_one[:, :heads_wide]
    full_misc = full_one[:, heads_wide:]
    w_out_full = full_two[:, :model]
    w_both = full_two[:, model:]
    misc = full_misc.reshape(devices, share, LANES)
    gain_one = misc[:, CONV, :share].reshape(model).astype(f32)
    gain_two = misc[:, CONV + 1, :share].reshape(model).astype(f32)
    onorm = misc[:, CONV + 2, :own_gain].reshape(1, width).astype(f32)
    taps = misc[:, :CONV, :wide].swapaxes(0, 1).reshape(CONV, chan).astype(f32)
    beta_cols = jnp.where(
        lax.broadcasted_iota(jnp.int32, full_misc.shape, 1) >= LANES - heads, full_misc, 0
    )

    rim_tokens = lax.ppermute(
        tokens[rows - RIM :], BOTH, [(i, i + 1) for i in range(devices - 1)]
    )
    rim_tokens = jnp.where(opens, jnp.zeros_like(rim_tokens), rim_tokens)
    x_all = jnp.concatenate([tokens, rim_tokens], axis=0).astype(f32)
    scale_all = rms(x_all)
    normed_all = (x_all * scale_all * gain_one).astype(bf16)
    projected = dot(normed_all, w_heads[:, :chan]).astype(bf16)
    normed = normed_all[:rows]
    x = tokens.astype(f32)
    scale_one = scale_all[:rows]
    beta_logit = dot(normed, full_misc)
    normed_order = dot(normed, to_order).astype(bf16)
    gots = cross(halves, FIRST)
    q, k, v, t, pair = run_front(projected, taps, beta_logit, rows, heads)
    pair, gots = tied(pair, gots)
    prefix, linears, group = joined_chunks(pair, place)
    halves = [merged(h, g, bit) for h, g, bit in zip(halves, gots, FIRST)]
    gate_logit = dot(normed, w_heads[:, chan:])
    group, halves, gate_logit = tied(group, halves, gate_logit)
    gots = cross(halves, (1, 1))
    states, gots = states_entering(prefix, group, before, reach, gots)
    halves = [merged(h, g, 1) for h, g in zip(halves, gots)]
    halves[1] = halves[1].swapaxes(1, 2)
    full_down = jnp.concatenate([h.reshape(hidden_size, -1) for h in halves], axis=1)
    states, full_down = tied(states, full_down)
    branch, o, d, p = run_pass(
        place, q, k, v, t, beta_logit, states, gate_logit, onorm, rows, heads
    )
    hidden = x + dot(branch, w_out_full)
    scale_two = rms(hidden)
    normed_two = (hidden * scale_two * gain_two).astype(bf16)
    both_rows = dot(normed_two, w_both)
    gate_rows, up_rows = both_rows[:, :hidden_size], both_rows[:, hidden_size:]
    sig = sigmoid(gate_rows)
    act = gate_rows * sig
    inner = (act * up_rows).astype(bf16)
    side = place_bits()[1]
    down_got = begin_terms(half(inner, 1 - side, 1), cotangent)
    d_inner = dot_t(cotangent, full_down)
    d_both = jnp.concatenate(
        [d_inner * up_rows * (sig * (1.0 + gate_rows * (1.0 - sig))), d_inner * act], axis=1
    ).astype(bf16)
    two_order = dot(normed_two, to_order).astype(bf16)
    both_got = begin_terms(two_order[:, : model // 2], d_both)
    down_home = half(inner, side, 1)
    down_totals, down_sents = middle_terms([down_home] * 2, two_of(cotangent), down_got)
    d_both, down_totals, down_sents = tied(d_both, down_totals, down_sents)
    down_gots = cross(down_sents, FIRST)
    d_normed_two = dot_t(d_both, w_both)
    d_norm, grad_gain_two = rms_back(hidden, scale_two, gain_two, d_normed_two)
    d_hidden = cotangent.astype(f32) + d_norm
    d_attn = d_hidden.astype(bf16)
    d_branch = dot_t(d_attn, w_out_full)
    branch_order = dot(branch, to_order).astype(bf16)
    out_got = exchanged(t_dot(branch_order[:, : model // 2], d_attn).astype(bf16), 1)
    both_totals, both_sents = middle_terms(
        [two_order[:, model // 2 :]] * 2, two_of(d_both), both_got
    )
    d_branch, down_gots, both_totals, both_sents = tied(
        d_branch, down_gots, both_totals, both_sents
    )

    d_gate_logit, d_onorm, d_o, d_r, state_grad = run_back_one(
        d_branch, o, gate_logit, onorm, p, t, q, k, beta_logit, rows, heads
    )
    state_grad, out_got = tied(state_grad, out_got)
    away, home = normed_order[:, : model // 2], normed_order[:, model // 2 :]
    gate_got = exchanged(t_dot(away, d_gate_logit).astype(bf16), 1)

    def meanwhile(held):
        gate_got, inner, d_attn = held
        totals, sents = middle_terms(
            [branch_order[:, model // 2 :], home], [d_attn, d_gate_logit], [out_got, gate_got]
        )
        return (
            end_terms(down_totals, down_gots),
            totals,
            sents,
            (hidden + dot(inner, full_down)).astype(bf16),
        )

    leaving, firsts, (down_ends, gate_totals, gate_sents, output) = state_grads_leaving(
        state_grad, linears, prefix, place, beyond, reach, both_sents,
        (gate_got, inner, d_attn), meanwhile,
    )
    leaving, firsts = tied(leaving, firsts)
    both_mine, both_sents = end_terms(both_totals, firsts)
    leaving, both_mine, both_sents = tied(leaving, both_mine, both_sents)
    both_gots = cross(both_sents, FIRST[::-1])
    outs = run_back_two(
        place, leaving, states, t, p, q, k, v, beta_logit, d_o, d_r, d, projected, taps,
        rows, heads,
    )
    outs, both_gots, gate_sents = tied(outs, both_gots, gate_sents)
    gate_gots = cross(gate_sents, FIRST)
    tails = jnp.concatenate(outs[3:6], axis=1)
    rims = jnp.concatenate(outs[6:9], axis=1)
    d_beta = outs[12].astype(bf16)
    rims = jnp.where(opens, jnp.zeros_like(rims), rims)
    rims = lax.ppermute(rims, BOTH, [(i + 1, i) for i in range(devices - 1)])
    tails = tails + jnp.pad(rims, ((TAIL - RIM, 0), (0, 0)))
    d_proj = lax.dynamic_update_slice_in_dim(
        jnp.concatenate(outs[0:3], axis=1), tails.astype(bf16), rows - TAIL, 0
    )
    d_proj, both_mine, both_gots, (down_mine, down_sents) = tied(
        d_proj, both_mine, both_gots, down_ends
    )
    mlp_blocks = owner_blocks(both_mine, both_gots)
    down_gots = cross(down_sents, FIRST[::-1])
    g_mlp = last_sum(mlp_blocks)
    last_got = begin_terms(away, d_proj)
    d_normed = (
        dot_t(d_proj, w_heads[:, :chan])
        + dot_t(d_gate_logit, w_heads[:, chan:])
        + dot_t(d_beta, beta_cols)
    )
    d_token_norm, grad_gain_one = rms_back(x, scale_one, gain_one, d_normed)
    grad_tokens = d_hidden + d_token_norm
    grad_beta = t_dot(d_beta, normed)[LANES - heads :]
    table = jnp.concatenate(
        list(outs[9:12])
        + [
            grad_gain_one.reshape(1, model),
            grad_gain_two.reshape(1, model),
            jnp.pad(jnp.sum(d_onorm, axis=(0, 1)).reshape(1, width), ((0, 0), (0, model - width))),
            grad_beta,
        ],
        axis=0,
    )
    table = table + exchanged(table, 8)
    last_got, grad_tokens, gate_gots = tied(last_got, grad_tokens, gate_gots)
    last_totals, last_sents = middle_terms([home] * 2, two_of(d_proj), last_got)
    last_totals, last_sents, gate_gots, table, down_gots = tied(
        last_totals, last_sents, gate_gots, table, down_gots
    )
    last_gots = cross(last_sents, FIRST)
    g_down = last_sum(owner_blocks(down_mine, down_gots))
    gate_mine, gate_sents = end_terms(gate_totals, gate_gots)
    gate_gots = cross(gate_sents, FIRST[::-1])

    def from_order(grad):
        blocks = grad.reshape(share, 2, 2, 2, devices // 8, -1)
        return blocks.transpose(0, 4, 3, 2, 1, 5).reshape(share, hidden_size)

    for bit in [8 << i for i in range(1, (devices // 8).bit_length() - 1)] + [1, 4]:
        table = table + exchanged(table, bit)
    last_gots, gate_gots, g_mlp, table = tied(last_gots, gate_gots, g_mlp, table)
    last_mine, last_sents = end_terms(last_totals, last_gots)
    last_mine, last_sents, gate_gots, table, g_mlp = tied(
        last_mine, last_sents, gate_gots, table, g_mlp
    )
    last_gots = cross(last_sents, FIRST[::-1])
    g_early = last_sum(owner_blocks(gate_mine, gate_gots))
    table = table + exchanged(table, 2)
    g_mlp = g_mlp.astype(f32)
    g_gate, g_up = from_order(g_mlp[:, :hidden_size]), from_order(g_mlp[:, hidden_size:])
    last_gots, table, g_gate, g_up, g_down = tied(last_gots, table, g_gate, g_up, g_down)
    last_parts = send_blocks(owner_blocks(last_mine, last_gots))
    g_last = added(last_parts)
    g_early, g_down = g_early.astype(f32), g_down.astype(f32)
    index = lax.axis_index(BOTH)
    g_taps = jnp.concatenate([table[i * CONV : (i + 1) * CONV] for i in range(3)], axis=1)

    def own(rows_of, size):
        return lax.dynamic_slice_in_dim(rows_of, index * size, size, rows_of.ndim - 1)

    line = 3 * CONV

    return (
        output,
        grad_tokens,
        own(table[line], share),
        g_last[:, :model],
        g_last[:, model : 2 * model],
        g_last[:, 2 * model : chan],
        own(g_taps, wide),
        own(table[line + 3 :], share).T,
        g_early[:, model:],
        own(table[line + 2], own_gain),
        g_early[:, :model],
        own(table[line + 1], share),
        g_gate,
        g_up,
        g_down,
    )


def solution(mesh):
    seq, fsdp = mesh.devices.shape
    mesh = Mesh(mesh.devices.reshape(seq // 2, 2, fsdp // 2, 2), BOTH)
    rows = P(BOTH, None)
    flat = P(BOTH)
    cols = P(None, BOTH)
    return jax.shard_map(
        local,
        mesh=mesh,
        in_specs=(
            rows, flat, rows, rows, rows, cols, rows, rows, flat, rows, flat, rows, rows, rows,
            P(), rows,
        ),
        out_specs=(
            rows, rows, flat, rows, rows, rows, cols, rows, rows, flat, rows, flat, rows, rows,
            rows,
        ),
        check_vma=False,
    )
```
